128 devices in a mesh: seq: 32 (over z, y_hi, x), head: 4 (over y_lo, core).
Axes of the slice: x: 4, y: 4 (y_hi: 2, y_lo: 2; y = y_hi * 2 + y_lo), z: 4, core: 2. Of those that a mesh axis runs over, the one named last changes fastest.
Arguments:
- tokens: bfloat16 [131072, 256], P('seq'), may hold values from -6 to 6
- fine_gain: float32 [256], replicated, may hold values from 0.1 to 1.9
- fine_gate: bfloat16 [256, 512], P(None, 'head'), may hold values from -0.375 to 0.375
- fine_value: bfloat16 [256, 512], P(None, 'head'), may hold values from -0.375 to 0.375
- fine_scans: bfloat16 [256, 512], replicated, may hold values from -0.375 to 0.375
- fine_steps: bfloat16 [256, 8], P(None, 'head'), may hold values from -0.375 to 0.375
- fine_kernel: float32 [4, 512], P(None, 'head'), may hold values from -3 to 3
- fine_taps: float32 [4, 512], replicated, may hold values from -3 to 3
- fine_bias: float32 [8], P('head'), may hold values from -3 to 1
- fine_decay: float32 [8], P('head'), may hold values from 7.6293945e-06 to 0.2
- fine_norm: float32 [512], P('head'), may hold values from 0.1 to 1.9
- fine_output: bfloat16 [512, 256], P('head'), may hold values from -0.25 to 0.25
- merge_weight: bfloat16 [1024, 1024], replicated, may hold values from -0.1875 to 0.1875
- coarse_gain: float32 [1024], replicated, may hold values from 0.1 to 1.9
- coarse_gate: bfloat16 [1024, 2048], P(None, 'head'), may hold values from -0.1875 to 0.1875
- coarse_value: bfloat16 [1024, 2048], P(None, 'head'), may hold values from -0.1875 to 0.1875
- coarse_scans: bfloat16 [1024, 512], replicated, may hold values from -0.1875 to 0.1875
- coarse_steps: bfloat16 [1024, 32], P(None, 'head'), may hold values from -0.1875 to 0.1875
- coarse_kernel: float32 [4, 2048], P(None, 'head'), may hold values from -3 to 3
- coarse_taps: float32 [4, 512], replicated, may hold values from -3 to 3
- coarse_bias: float32 [32], P('head'), may hold values from -3 to 1
- coarse_decay: float32 [32], P('head'), may hold values from 3.0517578e-05 to 0.2
- coarse_norm: float32 [2048], P('head'), may hold values from 0.1 to 1.9
- coarse_output: bfloat16 [2048, 1024], P('head'), may hold values from -0.125 to 0.125
Outputs:
- scene_tokens: bfloat16 [32768, 1024], P('seq', 'head')
The draws below stay inside these ranges and needn't reach their ends.
All inputs are finite; a program needn't handle non-finite values.
Results may differ from the reference program's by a relative error of at most 0.02.
Values may be sent and summed in bfloat16 or wider, within the bound.
No kernel may reach another device: no remote copies, remote signals or barrier semaphores. Data moves between devices by JAX's collectives and lax.ppermute only.
A program may use at most 128 MiB of HBM per device.

```python
import math
import jax
import jax.numpy as jnp
from jax import lax

WIDTH = 256
INNER = 512
HEADS = 8
HEAD_DIM = 64
STATE = 256
COARSE_INNER = 2048
COARSE_HEADS = 32
KERNEL = 4
BLOCK = 256
ROW_PATCHES = 64
TOKENS = 131072
COARSE_WIDTH = 1024


def level_of(rng, dims, cuts, low, top_value):
    level = 1.0
    for dim, shards_of in cuts:
        steps = jax.random.uniform(jax.random.fold_in(jax.random.fold_in(rng, 6), dim), (shards_of,), jnp.float32, low / len(cuts), top_value / len(cuts))
        level = level * jnp.repeat(jnp.exp(steps), dims[dim] // shards_of).reshape((-1,) + (1,) * (len(dims) - 1 - dim))
    return level


def scatter_about(key, dims, scale, limit, split=(), kind=jnp.bfloat16):
    entries = jax.random.normal(key, dims, jnp.float32) * scale
    if len(split) > 0:
        entries = level_of(key, dims, split, -0.22, 0.18) * entries
    return jnp.clip(entries, min=-limit, max=limit).astype(kind)


def setup_inputs(seed: int = 0) -> dict:
    streams_of = jax.random.split(jax.random.key(seed), 25)
    tokens = scatter_about(streams_of[0], (TOKENS, WIDTH), 1.0, 6.0, ((0, 32),))
    fine_gain = jnp.clip(1.0 + 0.18 * jax.random.normal(streams_of[1], (WIDTH,), jnp.float32), 0.1, 1.9)
    fine_gate = scatter_about(streams_of[2], (WIDTH, INNER), WIDTH ** -0.5, 0.375, ((1, 4),))
    fine_value = scatter_about(streams_of[3], (WIDTH, INNER), WIDTH ** -0.5, 0.375, ((1, 4),))
    fine_scans = scatter_about(streams_of[4], (WIDTH, 2 * STATE), WIDTH ** -0.5, 0.375)
    fine_steps = scatter_about(streams_of[5], (WIDTH, HEADS), WIDTH ** -0.5, 0.375, ((1, 4),))
    fine_kernel = scatter_about(streams_of[6], (KERNEL, INNER), KERNEL ** -0.5, 3.0, ((1, 4),), jnp.float32)
    fine_taps = scatter_about(streams_of[7], (KERNEL, 2 * STATE), KERNEL ** -0.5, 3.0, (), jnp.float32)
    fine_bias = jnp.clip(-3.0 + 4.0 * jax.random.uniform(streams_of[8], (HEADS,), jnp.float32) ** level_of(streams_of[8], (HEADS,), ((0, 4),), -0.2, 0.2), -3.0, 1.0)
    fine_decay = jnp.clip(jnp.exp(math.log(0.2) - 10.1740642 * jax.random.uniform(streams_of[9], (HEADS,), jnp.float32) ** level_of(streams_of[9], (HEADS,), ((0, 4),), -0.2, 0.2)), 7.62939453125e-06, 0.2)
    fine_norm = jnp.clip(1.0 + 0.18 * jax.random.normal(streams_of[10], (INNER,), jnp.float32), 0.1, 1.9)
    fine_output = scatter_about(streams_of[11], (INNER, WIDTH), INNER ** -0.5, 0.25, ((0, 4),))
    merge_weight = scatter_about(streams_of[12], (COARSE_WIDTH, COARSE_WIDTH), COARSE_WIDTH ** -0.5, 0.1875)
    coarse_gain = jnp.clip(1.0 + 0.18 * jax.random.normal(streams_of[13], (COARSE_WIDTH,), jnp.float32), 0.1, 1.9)
    coarse_gate = scatter_about(streams_of[14], (COARSE_WIDTH, COARSE_INNER), COARSE_WIDTH ** -0.5, 0.1875, ((1, 4),))
    coarse_value = scatter_about(streams_of[15], (COARSE_WIDTH, COARSE_INNER), COARSE_WIDTH ** -0.5, 0.1875, ((1, 4),))
    coarse_scans = scatter_about(streams_of[16], (COARSE_WIDTH, 2 * STATE), COARSE_WIDTH ** -0.5, 0.1875)
    coarse_steps = scatter_about(streams_of[17], (COARSE_WIDTH, COARSE_HEADS), COARSE_WIDTH ** -0.5, 0.1875, ((1, 4),))
    coarse_kernel = scatter_about(streams_of[18], (KERNEL, COARSE_INNER), KERNEL ** -0.5, 3.0, ((1, 4),), jnp.float32)
    coarse_taps = scatter_about(streams_of[19], (KERNEL, 2 * STATE), KERNEL ** -0.5, 3.0, (), jnp.float32)
    coarse_bias = jnp.clip(-3.0 + 4.0 * jax.random.uniform(streams_of[20], (COARSE_HEADS,), jnp.float32) ** level_of(streams_of[20], (COARSE_HEADS,), ((0, 4),), -0.2, 0.2), -3.0, 1.0)
    coarse_decay = jnp.clip(jnp.exp(math.log(0.2) - 8.78777 * jax.random.uniform(streams_of[21], (COARSE_HEADS,), jnp.float32) ** level_of(streams_of[21], (COARSE_HEADS,), ((0, 4),), -0.2, 0.2)), 3.0517578125e-05, 0.2)
    coarse_norm = jnp.clip(1.0 + 0.18 * jax.random.normal(streams_of[22], (COARSE_INNER,), jnp.float32), 0.1, 1.9)
    coarse_output = scatter_about(streams_of[23], (COARSE_INNER, COARSE_WIDTH), COARSE_INNER ** -0.5, 0.125, ((0, 4),))
    return dict(tokens=tokens, fine_gain=fine_gain, fine_gate=fine_gate, fine_value=fine_value, fine_scans=fine_scans, fine_steps=fine_steps, fine_kernel=fine_kernel, fine_taps=fine_taps, fine_bias=fine_bias, fine_decay=fine_decay, fine_norm=fine_norm, fine_output=fine_output, merge_weight=merge_weight, coarse_gain=coarse_gain, coarse_gate=coarse_gate, coarse_value=coarse_value, coarse_scans=coarse_scans, coarse_steps=coarse_steps, coarse_kernel=coarse_kernel, coarse_taps=coarse_taps, coarse_bias=coarse_bias, coarse_decay=coarse_decay, coarse_norm=coarse_norm, coarse_output=coarse_output)


EPSILON = 1e-05

def rms_rows(values, gain_vec):
    return values * lax.rsqrt(lax.optimization_barrier(jnp.mean(values * values, axis=-1, keepdims=True)) + EPSILON) * gain_vec

def causal_conv(inputs, kernel_rows):
    length = inputs.shape[0]
    padded = jnp.concatenate([jnp.zeros((KERNEL - 1, inputs.shape[1]), jnp.float32), inputs.astype(jnp.float32)], 0)
    summed = jnp.zeros((length, inputs.shape[1]), jnp.float32)
    for offset in range(KERNEL):
        summed = summed + padded[offset:offset + length] * kernel_rows[offset]
    return jax.nn.silu(summed)

def state_space(values, step_sizes, log_decay, input_map, output_map):
    length, heads_here, _ = values.shape
    blocks = length // BLOCK
    lower = jnp.tril(jnp.ones((BLOCK, BLOCK), dtype=bool))

    def advance(state, pieces):
        vals, dts, logs_blk, b_blk, c_blk = pieces
        cumul = jnp.cumsum(logs_blk, axis=0)
        scores = jnp.dot(c_blk, b_blk.T, preferred_element_type=jnp.float32)
        spread = cumul.T[:, :, None] - cumul.T[:, None, :]
        decays = jnp.exp(jnp.where(lower[None], spread, -jnp.inf))
        weights = (scores[None] * decays * dts.T[:, None, :]).astype(jnp.bfloat16)
        intra = jnp.einsum('hts,shp->thp', weights.astype(jnp.float32), vals.astype(jnp.float32))
        inter = jnp.einsum('tn,hpn->thp', c_blk.astype(jnp.float32), state, precision=lax.Precision.HIGHEST)
        inter = inter * jnp.exp(cumul)[:, :, None]
        tail_w = jnp.exp(cumul[-1][None, :] - cumul) * dts
        scaled = (vals.astype(jnp.float32) * tail_w[:, :, None]).astype(jnp.bfloat16)
        local = jnp.einsum('shp,sn->hpn', scaled.astype(jnp.float32), b_blk.astype(jnp.float32))
        state = jnp.exp(cumul[-1])[:, None, None] * state + local
        return (state, intra + inter)
    pieces = (values.reshape(blocks, BLOCK, heads_here, HEAD_DIM), step_sizes.reshape(blocks, BLOCK, heads_here), log_decay.reshape(blocks, BLOCK, heads_here), input_map.reshape(blocks, BLOCK, STATE), output_map.reshape(blocks, BLOCK, STATE))
    _, result = lax.scan(advance, jnp.zeros((heads_here, HEAD_DIM, STATE), jnp.float32), pieces)
    return result.reshape(length, heads_here * HEAD_DIM)

def mamba_branch(stream, gain_vec, gate_weight, value_weight, scan_weight, step_weight, kernel_value, kernel_scan, step_bias, decay_rate, norm_gain, out_weight):
    normed = rms_rows(stream.astype(jnp.float32), gain_vec).astype(jnp.bfloat16)
    gate_rows = jnp.dot(normed, gate_weight, preferred_element_type=jnp.float32).astype(jnp.bfloat16)
    value_rows = jnp.dot(normed, value_weight, preferred_element_type=jnp.float32).astype(jnp.bfloat16)
    scan_rows = jnp.dot(normed, scan_weight, preferred_element_type=jnp.float32).astype(jnp.bfloat16)
    step_raw = jnp.dot(normed, step_weight, preferred_element_type=jnp.float32)
    conv_values = causal_conv(value_rows, kernel_value).astype(jnp.bfloat16)
    conv_scans = causal_conv(scan_rows, kernel_scan).astype(jnp.bfloat16)
    step_sizes = jax.nn.softplus(step_raw + step_bias)
    log_decay = -step_sizes * decay_rate
    heads_here = step_sizes.shape[1]
    mixed_rows = state_space(conv_values.reshape(-1, heads_here, HEAD_DIM), step_sizes, log_decay, conv_scans[:, :STATE], conv_scans[:, STATE:])
    gated_rows = mixed_rows * jax.nn.silu(gate_rows.astype(jnp.float32))
    normed_out = rms_rows(gated_rows, norm_gain).astype(jnp.bfloat16)
    return jnp.dot(normed_out, out_weight, preferred_element_type=jnp.float32)

def merge_tiles(rows):
    count, width_here = rows.shape
    grid = rows.reshape(count // (2 * ROW_PATCHES), 2, ROW_PATCHES // 2, 2, width_here)
    return grid.transpose(0, 2, 1, 3, 4).reshape(count // 4, 4 * width_here)

def reference(tokens, fine_gain, fine_gate, fine_value, fine_scans, fine_steps, fine_kernel, fine_taps, fine_bias, fine_decay, fine_norm, fine_output, merge_weight, coarse_gain, coarse_gate, coarse_value, coarse_scans, coarse_steps, coarse_kernel, coarse_taps, coarse_bias, coarse_decay, coarse_norm, coarse_output):
    branch = mamba_branch(tokens, fine_gain, fine_gate, fine_value, fine_scans, fine_steps, fine_kernel, fine_taps, fine_bias, fine_decay, fine_norm, fine_output)
    hidden = (tokens.astype(jnp.float32) + branch).astype(jnp.bfloat16)
    tiles = merge_tiles(hidden)
    merged = jnp.dot(tiles, merge_weight, preferred_element_type=jnp.float32).astype(jnp.bfloat16)
    branch_two = mamba_branch(merged, coarse_gain, coarse_gate, coarse_value, coarse_scans, coarse_steps, coarse_kernel, coarse_taps, coarse_bias, coarse_decay, coarse_norm, coarse_output)
    return (merged.astype(jnp.float32) + branch_two).astype(jnp.bfloat16)
```

```python
import jax
import jax.numpy as jnp
from jax import lax
from jax.experimental import pallas as pl
from jax.experimental.pallas import tpu as pltpu
from jax.sharding import Mesh
from jax.sharding import PartitionSpec as P

SEQ = ("z", "u", "x")
HEAD = ("y", "c")
ALL = ("z", "u", "x", "y", "c")
EPSILON = 1e-05
BLK = 256
BF = jnp.bfloat16
F32 = jnp.float32
NN = (((1,), (0,)), ((), ()))
NT = (((1,), (1,)), ((), ()))
TN = (((0,), (0,)), ((), ()))


def dot(a, b, dims=NN):
    return lax.dot_general(a, b, dims, preferred_element_type=F32)


def parts(x):
    hi = x.astype(BF).astype(F32)
    rest = x - hi
    mid = rest.astype(BF).astype(F32)
    low = rest - mid
    return jnp.concatenate([hi, mid, low, jnp.zeros_like(x)], 0).astype(BF)


def decay_rows(row):
    hi = row.astype(BF).astype(F32)
    rest = row - hi
    mid = rest.astype(BF).astype(F32)
    low = rest - mid
    return jnp.concatenate([hi, mid, low, jnp.zeros((13, row.shape[1]), F32)], 0).astype(BF)


def of_rows(rows):
    rows = rows.astype(F32)
    return rows[0:1] + rows[1:2] + rows[2:3]


def iota(shape, dim):
    return lax.broadcasted_iota(jnp.int32, shape, dim)


def head_sel(width):
    return iota((8, width), 0) == iota((8, width), 1) // 64


def expander(width):
    r, lane = iota((32, width), 0), iota((32, width), 1)
    return jnp.where((r < 24) & (r % 8 == lane // 64), 1.0, 0.0).astype(BF)


def upper():
    return jnp.where(iota((BLK, BLK), 0) <= iota((BLK, BLK), 1), 1.0, 0.0).astype(BF)


def silu(v):
    h = v * 0.5
    return h + h * jnp.tanh(h)


def softplus(v):
    return jnp.maximum(v, 0.0) + jnp.log1p(jnp.exp(-jnp.abs(v)))


def rms(x, gain):
    x = x.astype(F32)
    return (x * lax.rsqrt(jnp.mean(x * x, axis=-1, keepdims=True) + EPSILON) * gain).astype(BF)


def cumulate(logs, tri):
    s = dot(parts(logs), tri)
    return s[0:8] + s[8:16] + s[16:24]


def convolve(cv, act, taps, width, length, step=64):
    for c in range(width // 128):
        cols = slice(c * 128, (c + 1) * 128)
        for r in range(length // step):
            total = cv[pl.ds(13 + r * step, step), cols] * taps[0:1, cols]
            for k in range(1, 4):
                total = total + cv[pl.ds(13 + k + r * step, step), cols] * taps[k : k + 1, cols]
            act[pl.ds(r * step, step), cols] = silu(total).astype(BF)


def rounded(x):
    return x.astype(BF).astype(F32)


def state_chunk(x, rim, gain, wv, wb, wst, kv, ks, bias, decay, taps, cv, act):
    taps[:, 0:128] = kv[...]
    taps[:, 128:384] = ks[...]
    normed = rms(x, gain[...])
    before = rms(rim, gain[...])
    cv[0:16, 0:128] = rounded(dot(before, wv[...]))
    cv[0:16, 128:384] = rounded(dot(before, wb[...]))
    cv[16:1040, 0:128] = rounded(dot(normed, wv[...]))
    cv[16:1040, 128:384] = rounded(dot(normed, wb[...]))
    convolve(cv, act, taps, 384, 1024)
    raw = dot(wst[...], normed, NT)
    dt = softplus(raw + bias[:, 0:1])
    logs = -dt * decay[:, 0:1]
    tri = upper()
    carry = jnp.zeros((8, 1), F32)
    pieces = []
    for b in range(4):
        piece = cumulate(logs[:, b * BLK : (b + 1) * BLK], tri) + carry
        carry = piece[:, BLK - 1 : BLK]
        pieces.append(piece)
    cum = jnp.concatenate(pieces, 1)
    tail = jnp.exp(carry - cum) * dt
    spread = dot(parts(tail), expander(128), TN)
    scaled = (act[:, 0:128].astype(F32) * spread).astype(BF)
    local = dot(act[:, 128:384], scaled, TN)
    total = jnp.sum(
        jnp.where(head_sel(128), jnp.broadcast_to(carry, (8, 128)), 0.0), axis=0, keepdims=True
    )
    return local, total


def later_chunks_kernel(x, rim, gain, wv, wb, wst, kv, ks, bias, decay, local, total, taps, cv, act):
    state, logs = state_chunk(
        x[...], rim[...], gain, wv, wb, wst, kv, ks, bias, decay, taps, cv, act
    )
    local[0] = state
    total[0] = jnp.broadcast_to(logs, (8, 128))


def first_chunk_kernel(
    x, rim, gain, wv, wb, wst, kv, ks, bias, decay, later, later_total,
    local, total, whole, whole_total, message, taps, cv, act,
):
    state, logs = state_chunk(
        x[...], rim[...], gain, wv, wb, wst, kv, ks, bias, decay, taps, cv, act
    )
    local[...] = state
    total[...] = jnp.broadcast_to(logs, (8, 128))
    for j in range(3):
        piece = later_total[j, 0:1, :]
        state = state * jnp.exp(piece) + later[j]
        logs = logs + piece
    whole[...] = state
    whole_total[...] = jnp.broadcast_to(logs, (8, 128))
    message[0:256, :] = state.astype(BF)
    message[256:272, :] = decay_rows(logs)


def sds(shape, dtype=F32):
    return jax.ShapeDtypeStruct(shape, dtype)


def whole_spec(shape):
    return pl.BlockSpec(shape, lambda *_: (0,) * len(shape))


PARAMS = pltpu.CompilerParams(dimension_semantics=("arbitrary",), vmem_limit_bytes=48 << 20)


def fine_states(tokens, rim, gain, wv, scans, wst, kv, ks, bias, decay):
    common = [
        whole_spec((1, 256)),
        whole_spec((256, 128)),
        whole_spec((256, 256)),
        whole_spec((8, 256)),
        whole_spec((4, 128)),
        whole_spec((4, 256)),
        whole_spec((8, 128)),
        whole_spec((8, 128)),
    ]
    scratch = [
        pltpu.VMEM((4, 384), F32),
        pltpu.VMEM((1040, 384), F32),
        pltpu.VMEM((1024, 384), BF),
    ]
    later, later_total = pl.pallas_call(
        later_chunks_kernel,
        grid=(3,),
        in_specs=[
            pl.BlockSpec((1024, 256), lambda i: (i + 1, 0)),
            pl.BlockSpec((16, 256), lambda i: ((i + 1) * 64 - 1, 0)),
        ]
        + common,
        out_specs=[
            pl.BlockSpec((1, 256, 128), lambda i: (i, 0, 0)),
            pl.BlockSpec((1, 8, 128), lambda i: (i, 0, 0)),
        ],
        out_shape=[sds((3, 256, 128)), sds((3, 8, 128))],
        scratch_shapes=scratch,
        compiler_params=PARAMS,
        name="later_chunks",
    )(tokens, tokens, gain, wv, scans, wst, kv, ks, bias, decay)
    first = pl.pallas_call(
        first_chunk_kernel,
        grid=(1,),
        in_specs=[pl.BlockSpec((1024, 256), lambda i: (0, 0)), whole_spec((16, 256))]
        + common
        + [whole_spec((3, 256, 128)), whole_spec((3, 8, 128))],
        out_specs=[
            whole_spec((256, 128)),
            whole_spec((8, 128)),
            whole_spec((256, 128)),
            whole_spec((8, 128)),
            whole_spec((272, 128)),
        ],
        out_shape=[
            sds((256, 128)),
            sds((8, 128)),
            sds((256, 128)),
            sds((8, 128)),
            sds((272, 128), BF),
        ],
        scratch_shapes=scratch,
        compiler_params=PARAMS,
        name="first_chunk",
    )(tokens, rim, gain, wv, scans, wst, kv, ks, bias, decay, later, later_total)
    return later, later_total, first


def combine(i, count, own, own_total, prior, prior_total, received):
    state = jnp.zeros_like(own)
    logs = jnp.zeros_like(own_total)
    zero = jnp.zeros((), F32)
    got = [(r[0:256, :].astype(F32), of_rows(r[256:272, :])) for r in received]
    for k in range(count - 1, 0, -1):
        s, l = got[k - 1]
        valid = i >= k
        state = jnp.where(valid, state * jnp.exp(l) + s, state)
        logs = jnp.where(valid, logs + l, logs)
    new_prior = state * jnp.exp(prior_total) + prior
    new_prior_total = logs + prior_total
    state = state * jnp.exp(own_total) + own
    logs = logs + own_total
    for m in range(1, count):
        s, l = got[count - m - 1]
        valid = i + m < count
        state = jnp.where(valid, state * jnp.exp(l) + s, state)
        logs = jnp.where(valid, logs + l, logs)
    return new_prior, new_prior_total, state, logs


def middle_kernel(count, pos, own, own_total, prior, prior_total, *refs):
    received, (np_ref, npt_ref, ns_ref, nst_ref, message) = refs[: count - 1], refs[count - 1 :]
    p, pt, s, st = combine(
        pos[0], count, own[...], own_total[0:1, :], prior[...], prior_total[0:1, :], received
    )
    np_ref[...] = p
    npt_ref[...] = jnp.broadcast_to(pt, (8, 128))
    ns_ref[...] = s
    nst_ref[...] = jnp.broadcast_to(st, (8, 128))
    message[0:256, :] = s.astype(BF)
    message[256:272, :] = decay_rows(st)


SMEM = pl.BlockSpec(memory_space=pltpu.SMEM)
VM = pl.BlockSpec(memory_space=pltpu.VMEM)


def middle_stage(count, pos, own, own_total, prior, prior_total, received, name):
    return pl.pallas_call(
        lambda *refs: middle_kernel(count, *refs),
        in_specs=[SMEM] + [VM] * (4 + len(received)),
        out_specs=[VM] * 5,
        out_shape=[
            sds((256, 128)),
            sds((8, 128)),
            sds((256, 128)),
            sds((8, 128)),
            sds((272, 128), BF),
        ],
        name=name,
    )(pos, own, own_total, prior, prior_total, *received)


def last_kernel(pos, own, own_total, prior, prior_total, r1, r2, r3, l0, t0, later, later_total,
                o0, o1, o2, o3, sub):
    p, _, _, _ = combine(
        pos[0], 4, own[...], own_total[0:1, :], prior[...], prior_total[0:1, :], (r1, r2, r3)
    )
    sub[0] = p
    p = p * jnp.exp(t0[0:1, :]) + l0[...]
    sub[1] = p
    for j in range(2):
        p = p * jnp.exp(later_total[j, 0:1, :]) + later[j]
        sub[j + 2] = p
    h = pos[1]
    for k, out in enumerate((o0, o1, o2, o3)):
        out[...] = sub[h ^ k].astype(BF)


def last_stage(pos, own, own_total, prior, prior_total, received, l0, t0, later, later_total):
    return pl.pallas_call(
        last_kernel,
        in_specs=[SMEM] + [VM] * 11,
        out_specs=[VM] * 4,
        out_shape=[sds((256, 128), BF)] * 4,
        scratch_shapes=[pltpu.VMEM((4, 256, 128), F32)],
        name="chain_last",
    )(pos, own, own_total, prior, prior_total, *received, l0, t0, later, later_total)


def scan_block(
    normed, wg, wv, ws, wst, taps, bias, decay, first, rim_normed,
    lead, tail_out, maps_out, cv, act, sc, run, run_log,
):
    @pl.when(first)
    def _():
        before = rim_normed()
        cv[0:16, 0:512] = rounded(dot(before, wv[...]))
        cv[0:16, 512:1024] = rounded(dot(before, ws[...]))
        run[...] = jnp.zeros_like(run)
        run_log[...] = jnp.zeros_like(run_log)

    cv[16:272, 0:512] = rounded(dot(normed, wv[...]))
    cv[16:272, 512:1024] = rounded(dot(normed, ws[...]))
    convolve(cv, act, taps, 1024, BLK)
    cv[0:16, :] = cv[256:272, :]
    raw = dot(wst[...], normed, NT)
    dt = softplus(raw + bias[...])
    logs = -dt * decay[...]
    cum = cumulate(logs, upper())
    last = cum[:, BLK - 1 : BLK]
    before_log = run_log[:, 0:1]
    stacked = jnp.concatenate(
        [jnp.exp(cum), jnp.exp(cum + before_log), jnp.exp(last - cum) * dt], 1
    )
    spread = dot(parts(stacked), expander(512), TN)
    run_log[...] = run_log[...] + last
    columns = dot(parts(cum), jnp.where(
        (iota((32, 128), 0) < 24) & (iota((32, 128), 0) % 8 == iota((32, 128), 1)), 1.0, 0.0
    ).astype(BF), TN)
    rows = cum - jnp.log(dt)
    in_map = act[:, 512:768]
    out_map = act[:, 768:1024]
    maps_out[...] = out_map
    sc[...] = dot(out_map, in_map, NT)
    carried = dot(out_map, run[...].astype(BF))
    low_tri = iota((128, 128), 0) >= iota((128, 128), 1)
    lane_low = iota((BLK, 128), 1) < 64
    for p in range(4):
        cols = slice(p * 128, (p + 1) * 128)
        vals = act[:, cols].astype(F32)
        v0 = jnp.where(lane_low, vals, 0.0).astype(BF)
        v1 = jnp.where(lane_low, 0.0, vals).astype(BF)
        upper_w, lower_w = [], []
        for h in (2 * p, 2 * p + 1):
            c0, c1 = columns[0:128, h : h + 1], columns[128:256, h : h + 1]
            r0, r1 = rows[h : h + 1, 0:128], rows[h : h + 1, 128:256]
            upper_w.append(
                (sc[0:128, 0:128] * jnp.exp(jnp.where(low_tri, c0 - r0, -jnp.inf))).astype(BF)
            )
            lower_w.append((sc[128:256, 0:128] * jnp.exp(c1 - r0)).astype(BF))
            lower_w.append(
                (sc[128:256, 128:256] * jnp.exp(jnp.where(low_tri, c1 - r1, -jnp.inf))).astype(BF)
            )
        top = dot(
            jnp.concatenate(upper_w, 1), jnp.concatenate([v0[0:128], v1[0:128]], 0)
        )
        bottom = dot(jnp.concatenate(lower_w, 1), jnp.concatenate([v0, v1], 0))
        gate = silu(rounded(dot(normed, wg[:, cols])))
        lead[0:128, cols] = (top + spread[0:128, cols] * carried[0:128, cols]) * gate[0:128]
        lead[128:256, cols] = (
            bottom + spread[128:256, cols] * carried[128:256, cols]
        ) * gate[128:256]
        tail_out[:, cols] = spread[256:512, cols] * gate
        scaled = (vals * spread[512:768, cols]).astype(BF)
        run[:, cols] = run[:, cols] * spread[255:256, cols] + dot(in_map, scaled, TN)


SCAN_SCRATCH = [
    pltpu.VMEM((272, 1024), F32),
    pltpu.VMEM((BLK, 1024), BF),
    pltpu.VMEM((BLK, BLK), F32),
    pltpu.VMEM((256, 512), F32),
    pltpu.VMEM((8, 128), F32),
]


def fine_main_kernel(
    h, x, rim_here, rim_there, gain, ws, ks, p0, p1, p2, p3, f0, f1, f2, f3,
    lead, tail_out, maps_out,
    wg, wv, wst, taps, bias, decay, cv, act, sc, run, run_log,
):
    first = pl.program_id(0) == 0

    @pl.when(first)
    def _():
        taps[:, 512:1024] = ks[...]
        for j, (p, f) in enumerate(((p0, f0), (p1, f1), (p2, f2), (p3, f3))):
            cols = slice(j * 128, (j + 1) * 128)
            wg[:, cols] = p[0:256, 0:128]
            wv[:, cols] = p[0:256, 128:256]
            taps[:, cols] = f[0:4, 0:128]
            wst[2 * j : 2 * j + 2, :] = f[8:10, :]
            bias[2 * j : 2 * j + 2, :] = f[10:12, 0:128]
            decay[2 * j : 2 * j + 2, :] = f[12:14, 0:128]

    def rim_normed():
        rim = jnp.where(h[0] == 0, rim_there[...].astype(F32), rim_here[...].astype(F32))
        return rms(rim, gain[...])

    scan_block(
        rms(x[...], gain[...]), wg, wv, ws, wst[...].astype(BF), taps, bias[:, 0:1], decay[:, 0:1],
        first, rim_normed, lead, tail_out, maps_out, cv, act, sc, run, run_log,
    )


def fine_main(h, tokens, rim, gain, scans, ks, packs, smalls):
    return pl.pallas_call(
        fine_main_kernel,
        grid_spec=pltpu.PrefetchScalarGridSpec(
            num_scalar_prefetch=1,
            grid=(4,),
            in_specs=[
                pl.BlockSpec((BLK, 256), lambda i, h: (h[0] * 4 + i, 0)),
                pl.BlockSpec((16, 256), lambda i, h: (jnp.maximum(h[0] * 64 - 1, 0), 0)),
                whole_spec((16, 256)),
                whole_spec((1, 256)),
                whole_spec((256, 512)),
                whole_spec((4, 512)),
            ]
            + [whole_spec((384, 256))] * 4
            + [whole_spec((16, 256))] * 4,
            out_specs=[
                pl.BlockSpec((BLK, 512), lambda i, h: (i, 0)),
                pl.BlockSpec((BLK, 512), lambda i, h: (i, 0)),
                pl.BlockSpec((BLK, 256), lambda i, h: (i, 0)),
            ],
            scratch_shapes=[
                pltpu.VMEM((256, 512), BF),
                pltpu.VMEM((256, 512), BF),
                pltpu.VMEM((8, 256), F32),
                pltpu.VMEM((4, 1024), F32),
                pltpu.VMEM((8, 128), F32),
                pltpu.VMEM((8, 128), F32),
            ]
            + SCAN_SCRATCH,
        ),
        out_shape=[sds((1024, 512)), sds((1024, 512)), sds((1024, 256), BF)],
        compiler_params=PARAMS,
        name="fine_main",
    )(h, tokens, tokens, rim, gain, scans, ks, *packs, *smalls)


def fine_close_kernel(
    h, lead, tail, maps, x, s0, s1, s2, s3, w0, w1, w2, w3, f0, f1, f2, f3, merge,
    merged, end_rows, hidden,
):
    i = pl.program_id(0)
    gated = []
    for j, s in enumerate((s0, s1, s2, s3)):
        cols = slice(j * 128, (j + 1) * 128)
        gated.append(lead[:, cols] + tail[:, cols] * dot(maps[...], s[...]))
    squares = sum(jnp.sum(g * g, axis=1, keepdims=True) for g in gated)
    factor = lax.rsqrt(squares / 512.0 + EPSILON)
    out = x[...].astype(F32)
    total = None
    for g, w, f in zip(gated, (w0, w1, w2, w3), (f0, f1, f2, f3)):
        piece = dot((g * factor * f[4:5, 0:128]).astype(BF), w[...])
        total = piece if total is None else total + piece
    start = pl.multiple_of(i * BLK, BLK)
    hidden[0, pl.ds(start, BLK), :] = rounded(out[:, 0:128] + total[:, 0:128])
    hidden[1, pl.ds(start, BLK), :] = rounded(out[:, 128:256] + total[:, 128:256])

    @pl.when(i == pl.num_programs(0) - 1)
    def _():
        total = None
        for odd in range(2):
            for half in range(2):
                rows = hidden[half, pl.ds(odd, 512, stride=2), :].reshape(8, 2, 32, 128)
                for line in range(2):
                    tile = rows[:, line].reshape(256, 128).astype(BF)
                    at = (2 * line + odd) * 256 + half * 128
                    piece = dot(tile, merge[at : at + 128, :])
                    total = piece if total is None else total + piece
        result = total.astype(BF)
        merged[...] = result
        end_rows[...] = result[240:256]


def fine_close(h, lead, tail, maps, tokens, states, packs, smalls, merge):
    return pl.pallas_call(
        fine_close_kernel,
        grid_spec=pltpu.PrefetchScalarGridSpec(
            num_scalar_prefetch=1,
            grid=(4,),
            in_specs=[
                pl.BlockSpec((BLK, 512), lambda i, h: (i, 0)),
                pl.BlockSpec((BLK, 512), lambda i, h: (i, 0)),
                pl.BlockSpec((BLK, 256), lambda i, h: (i, 0)),
                pl.BlockSpec((BLK, 256), lambda i, h: (h[0] * 4 + i, 0)),
            ]
            + [whole_spec((256, 128))] * 4
            + [pl.BlockSpec((128, 256), lambda i, h: (2, 0))] * 4
            + [whole_spec((16, 256))] * 4
            + [whole_spec((1024, 1024))],
            out_specs=[whole_spec((256, 1024)), whole_spec((16, 1024))],
            scratch_shapes=[pltpu.VMEM((2, 1024, 128), F32)],
        ),
        out_shape=[sds((256, 1024), BF), sds((16, 1024), BF)],
        compiler_params=PARAMS,
        name="fine_close",
    )(h, lead, tail, maps, tokens, *states, *packs, *smalls, merge)


def coarse_main_kernel(
    pos, q0, q1, q2, q3, ra, rb, rc, gain, wg, wv, ws, wst, kv, ks, bias, decay,
    lead, tail_out, maps_out, share, message,
    xs, sems, taps, cv, act, sc, run, run_log,
):
    i = pl.program_id(0)
    first = i == 0
    h = pos[0]

    @pl.when(first)
    def _():
        copies = [
            pltpu.make_async_copy(q, xs.at[h ^ k], sems.at[k])
            for k, q in enumerate((q0, q1, q2, q3))
        ]
        for copy in copies:
            copy.start()
        taps[:, 0:512] = kv[...]
        taps[:, 512:1024] = ks[...]
        for copy in copies:
            copy.wait()

    def rim_normed():
        rim = ra[...].astype(F32) + rb[...].astype(F32) + rc[...].astype(F32)
        return rms(rim, gain[...])

    share[...] = xs[i, :, pl.ds(pl.multiple_of(h * 256, 256), 256)]
    scan_block(
        rms(xs[i], gain[...]), wg, wv, ws, wst[...], taps, bias[:, 0:1], decay[:, 0:1],
        first, rim_normed, lead, tail_out, maps_out, cv, act, sc, run, run_log,
    )

    @pl.when(i == pl.num_programs(0) - 1)
    def _():
        total = jnp.broadcast_to(run_log[:, 0:1], (8, 512))
        row = jnp.sum(jnp.where(head_sel(512), total, 0.0), axis=0, keepdims=True)
        extra = decay_rows(row)
        for n in range(16):
            for half in range(2):
                cols = slice(half * 256, (half + 1) * 256)
                message[2 * n + half, 0:16, :] = run[n * 16 : (n + 1) * 16, cols].astype(BF)
                message[2 * n + half, 16:32, :] = extra[:, cols]


def single(shape):
    return pl.BlockSpec(shape, lambda *_: (0,) * len(shape), pipeline_mode=pl.Buffered(1))


ANY = pl.BlockSpec(memory_space=pl.ANY)


def coarse_main(pos, pieces, rims, gain, wg, wv, ws, wst, kv, ks, bias, decay):
    return pl.pallas_call(
        coarse_main_kernel,
        grid=(4,),
        in_specs=[SMEM]
        + [ANY] * 4
        + [whole_spec((16, 1024))] * 3
        + [
            whole_spec((1, 1024)),
            single((1024, 512)),
            single((1024, 512)),
            single((1024, 512)),
            whole_spec((8, 1024)),
            whole_spec((4, 512)),
            whole_spec((4, 512)),
            whole_spec((8, 128)),
            whole_spec((8, 128)),
        ],
        out_specs=[
            pl.BlockSpec((BLK, 512), lambda i: (i, 0)),
            pl.BlockSpec((BLK, 512), lambda i: (i, 0)),
            pl.BlockSpec((BLK, 256), lambda i: (i, 0)),
            pl.BlockSpec((BLK, 256), lambda i: (i, 0)),
            whole_spec((32, 32, 256)),
        ],
        out_shape=[
            sds((1024, 512)),
            sds((1024, 512)),
            sds((1024, 256), BF),
            sds((1024, 256), BF),
            sds((32, 32, 256), BF),
        ],
        scratch_shapes=[
            pltpu.VMEM((4, 256, 1024), BF),
            pltpu.SemaphoreType.DMA((4,)),
            pltpu.VMEM((4, 1024), F32),
        ]
        + SCAN_SCRATCH,
        compiler_params=PARAMS,
        name="coarse_main",
    )(pos, *pieces, *rims, gain, wg, wv, ws, wst, kv, ks, bias, decay)


def prefix_kernel(got, out):
    state = jnp.zeros((16, 256), F32)
    for d in range(32):
        out[d] = state.astype(BF)
        state = state * jnp.exp(of_rows(got[d, 16:32, :])) + got[d, 0:16, :].astype(F32)


def prefix(got):
    return pl.pallas_call(
        prefix_kernel,
        in_specs=[VM],
        out_specs=VM,
        out_shape=sds((32, 16, 256), BF),
        name="prefix",
    )(got)


def coarse_close_kernel(pos, lead, tail, maps, got, norm, wo, kk, ks, sk, ss, squares, state):
    @pl.when(pl.program_id(0) == 0)
    def _():
        for n in range(16):
            for half in range(2):
                cols = slice(half * 256, (half + 1) * 256)
                state[n * 16 : (n + 1) * 16, cols] = got[2 * n + half]

    gated = lead[...] + tail[...] * dot(maps[...], state[...])
    sq = gated * gated
    hi = sq.astype(BF)
    low = (sq - hi.astype(F32)).astype(BF)
    ones = jnp.ones((8, 512), BF)
    squares[...] = dot(ones, hi, NT) + dot(ones, low, NT)
    scaled = (gated * norm[...]).astype(BF)
    h = pos[0]
    for k, out in enumerate((kk, sk, ks, ss)):
        at = pl.multiple_of((h ^ k) * 256, 256)
        out[...] = dot(scaled, wo[:, pl.ds(at, 256)]).astype(BF)


def coarse_close(pos, lead, tail, maps, got, norm, wo):
    rows = pl.BlockSpec((BLK, 256), lambda i: (i, 0))
    return pl.pallas_call(
        coarse_close_kernel,
        grid=(4,),
        in_specs=[
            SMEM,
            pl.BlockSpec((BLK, 512), lambda i: (i, 0)),
            pl.BlockSpec((BLK, 512), lambda i: (i, 0)),
            rows,
            whole_spec((32, 16, 256)),
            whole_spec((1, 512)),
            single((512, 1024)),
        ],
        out_specs=[rows] * 4 + [pl.BlockSpec((8, BLK), lambda i: (0, i))],
        out_shape=[sds((1024, 256), BF)] * 4 + [sds((8, 1024))],
        scratch_shapes=[pltpu.VMEM((256, 512), BF)],
        compiler_params=PARAMS,
        name="coarse_close",
    )(pos, lead, tail, maps, got, norm, wo)


def final_kernel(share, kk, sk, far, sq, sq_far, out):
    factor = lax.rsqrt((sq[...] + sq_far[...]) / 2048.0 + EPSILON)
    pick = jnp.where(iota((32, 256), 0) % 8 == 0, 1.0, 0.0).astype(BF)
    spread = dot(parts(factor), pick, TN)
    total = kk[...].astype(F32) + sk[...].astype(F32) + far[...].astype(F32)
    out[...] = (share[...].astype(F32) + total * spread).astype(BF)


def final(share, kk, sk, far, sq, sq_far):
    return pl.pallas_call(
        final_kernel,
        in_specs=[VM] * 6,
        out_specs=VM,
        out_shape=sds((1024, 256), BF),
        name="final",
    )(share, kk, sk, far, sq, sq_far)


def passed(x, axes, pairs):
    return lax.ppermute(x, axes, pairs)


def swapped(x, mask):
    return passed(x, HEAD, [(j, j ^ mask) for j in range(4)])


def round_of(x, axis):
    return [passed(x, axis, [(j, (j + k) % 4) for j in range(4)]) for k in (1, 2, 3)]


def lanes(v):
    return jnp.broadcast_to(v[:, None], (v.shape[0], 128))


def shards(
    tokens, fine_gain, fine_gate, fine_value, fine_scans, fine_steps, fine_kernel, fine_taps,
    fine_bias, fine_decay, fine_norm, fine_output, merge_weight, coarse_gain, coarse_gate,
    coarse_value, coarse_scans, coarse_steps, coarse_kernel, coarse_taps, coarse_bias,
    coarse_decay, coarse_norm, coarse_output,
):
    head = lax.axis_index(HEAD).astype(jnp.int32)

    def position(axis):
        return jnp.stack([lax.axis_index(axis).astype(jnp.int32), head])

    here = head[None]
    rim = passed(tokens[4080:], SEQ, [(i, i + 1) for i in range(31)])

    pack = jnp.concatenate([jnp.concatenate([fine_gate, fine_value], 1), fine_output], 0)
    zeros = jnp.zeros((4, 128), F32)
    small = jnp.concatenate(
        [
            jnp.concatenate([fine_kernel, zeros], 1),
            jnp.concatenate([fine_norm[None], jnp.zeros((1, 128), F32)], 1),
            jnp.zeros((3, 256), F32),
            fine_steps.T.astype(F32),
            jnp.broadcast_to(fine_bias[:, None], (2, 256)),
            jnp.broadcast_to(fine_decay[:, None], (2, 256)),
            jnp.zeros((2, 256), F32),
        ],
        0,
    )
    packs = [pack] + [swapped(pack, m) for m in (1, 2, 3)]
    smalls = [small] + [swapped(small, m) for m in (1, 2, 3)]

    gain = fine_gain[None]
    wst = jnp.concatenate([fine_steps.T, jnp.zeros((6, 256), BF)], 0)
    bias = jnp.concatenate([lanes(fine_bias), jnp.zeros((6, 128), F32)], 0)
    decay = jnp.concatenate([lanes(fine_decay), jnp.zeros((6, 128), F32)], 0)
    later, later_total, (l0, t0, own, own_total, message) = fine_states(
        tokens, rim, gain, fine_value, fine_scans, wst, fine_kernel, fine_taps, bias, decay
    )
    got = round_of(message, "x")
    lead, tail, maps = fine_main(here, tokens, rim, gain, fine_scans, fine_taps, packs, smalls)
    prior, prior_total = jnp.zeros((256, 128), F32), jnp.zeros((8, 128), F32)
    prior, prior_total, own, own_total, message = middle_stage(
        4, position("x"), own, own_total, prior, prior_total, got, "chain_x"
    )
    got = [passed(message, "u", [(0, 1), (1, 0)])]
    prior, prior_total, own, own_total, message = middle_stage(
        2, position("u"), own, own_total, prior, prior_total, got, "chain_u"
    )
    got = round_of(message, "z")
    subs = last_stage(
        position("z"), own, own_total, prior, prior_total, got, l0, t0, later, later_total
    )
    states = [subs[0]] + [swapped(subs[m], m) for m in (1, 2, 3)]
    merged, end_rows = fine_close(
        here, lead, tail, maps, tokens, states, packs, smalls, merge_weight
    )

    across = swapped(merged, 2)
    beside = swapped(merged, 1)
    rim_a = passed(end_rows, ALL, [(4 * s + 3, 4 * s + 4) for s in range(31)])
    rim_b = passed(end_rows, ALL, [(4 * s + 3, 4 * s + 7) for s in range(31)])
    rim_c = swapped(rim_a + rim_b, 1)
    both = swapped(across, 1)
    lead, tail, maps, share, message = coarse_main(
        here,
        (merged, beside, across, both),
        (rim_a, rim_b, rim_c),
        coarse_gain[None],
        coarse_gate,
        coarse_value,
        coarse_scans,
        coarse_steps.T,
        coarse_kernel,
        coarse_taps,
        lanes(coarse_bias),
        lanes(coarse_decay),
    )
    got = lax.all_to_all(message, SEQ, split_axis=0, concat_axis=0, tiled=True)
    got = lax.all_to_all(prefix(got), SEQ, split_axis=0, concat_axis=0, tiled=True)
    kk, ks, sk, ss, squares = coarse_close(
        here, lead, tail, maps, got, coarse_norm[None], coarse_output
    )
    from_ss = swapped(ss, 1)
    from_sk = swapped(sk, 1)
    squares = squares + swapped(squares, 1)
    far = (ks.astype(F32) + from_ss.astype(F32)).astype(BF)
    return final(share, kk, from_sk, swapped(far, 2), squares, swapped(squares, 2))


def solution(mesh):
    finer = Mesh(mesh.devices.reshape(4, 2, 4, 2, 2), ALL)
    cols = P(None, HEAD)
    return jax.shard_map(
        shards,
        mesh=finer,
        in_specs=(
            P(SEQ, None), P(), cols, cols, P(), cols, cols, P(), P(HEAD), P(HEAD), P(HEAD),
            P(HEAD, None), P(), P(), cols, cols, P(), cols, cols, P(), P(HEAD), P(HEAD), P(HEAD),
            P(HEAD, None),
        ),
        out_specs=P(SEQ, HEAD),
        check_vma=False,
    )
```

```python
import jax
import jax.numpy as jnp
from jax import lax
from jax.experimental import pallas as pl
from jax.experimental.pallas import tpu as pltpu
from jax.sharding import Mesh
from jax.sharding import PartitionSpec as P


SEQ = ("z", "u", "x")
HEAD = ("y", "c")
ALL = ("z", "u", "x", "y", "c")
EPSILON = 1e-05
BLK = 256
BF = jnp.bfloat16
F32 = jnp.float32
NN = (((1,), (0,)), ((), ()))
NT = (((1,), (1,)), ((), ()))
TN = (((0,), (0,)), ((), ()))


def dot(a, b, dims=NN):
    return lax.dot_general(a, b, dims, preferred_element_type=F32)


def parts(x):
    hi = x.astype(BF).astype(F32)
    rest = x - hi
    mid = rest.astype(BF).astype(F32)
    low = rest - mid
    return jnp.concatenate([hi, mid, low, jnp.zeros_like(x)], 0).astype(BF)


def decay_rows(row):
    hi = row.astype(BF).astype(F32)
    rest = row - hi
    mid = rest.astype(BF).astype(F32)
    low = rest - mid
    return jnp.concatenate([hi, mid, low, jnp.zeros((13, row.shape[1]), F32)], 0).astype(BF)


def of_rows(rows):
    rows = rows.astype(F32)
    return rows[0:1] + rows[1:2] + rows[2:3]


def iota(shape, dim):
    return lax.broadcasted_iota(jnp.int32, shape, dim)


def head_sel(width):
    return iota((8, width), 0) == iota((8, width), 1) // 64


def expander(width):
    r, lane = iota((32, width), 0), iota((32, width), 1)
    return jnp.where((r < 24) & (r % 8 == lane // 64), 1.0, 0.0).astype(BF)


def upper():
    return jnp.where(iota((BLK, BLK), 0) <= iota((BLK, BLK), 1), 1.0, 0.0).astype(BF)


def silu(v):
    h = v * 0.5
    return h + h * jnp.tanh(h)


def softplus(v):
    return jnp.maximum(v, 0.0) + jnp.log1p(jnp.exp(-jnp.abs(v)))


def rms(x, gain):
    x = x.astype(F32)
    return (x * lax.rsqrt(jnp.mean(x * x, axis=-1, keepdims=True) + EPSILON) * gain).astype(BF)


def cumulate(logs, tri):
    s = dot(parts(logs), tri)
    return s[0:8] + s[8:16] + s[16:24]


def convolve(cv, act, half_taps, length):
    apart = 32

    def slab(c, carry):
        taps = half_taps[c]
        for base in range(0, length, 8 * apart):
            rows = [cv[c, pl.ds(base + 13 + i, 8, stride=apart), :] for i in range(3)]
            for i in range(apart):
                rows.append(cv[c, pl.ds(base + 16 + i, 8, stride=apart), :])
                h = rows[i] * taps[0:1]
                for k in range(1, 4):
                    h = h + rows[i + k] * taps[k : k + 1]
                act[c, pl.ds(base + i, 8, stride=apart), :] = h + h * jnp.tanh(h)
        return carry

    lax.fori_loop(0, cv.shape[0], slab, 0)


def project(rows, weights, cv, start, slab):
    product = dot(rows, weights)
    for j in range(product.shape[1] // 128):
        cv[slab + j, start : start + rows.shape[0], :] = product[:, j * 128 : (j + 1) * 128]


def rounded(x):
    return x.astype(BF).astype(F32)


def small_rows(pack):
    rows = pack[384:416, :].astype(F32)
    kv = rows[0:4, 0:128] + rows[4:8, 0:128] + rows[8:12, 0:128]
    right = rows[0:16, 128:256]
    norm, b0, b1, d0, d1 = (of_rows(right[3 * j : 3 * j + 3]) for j in range(5))
    return kv, norm, jnp.concatenate([b0, b1], 0), jnp.concatenate([d0, d1], 0), rows[16:18]


def three(row):
    hi = row.astype(BF).astype(F32)
    rest = row - hi
    mid = rest.astype(BF).astype(F32)
    return [hi, mid, rest - mid]


def pack_kernel(bias, decay, gate, value, output, steps, kv, norm, pack):
    pack[0:256, 0:128] = gate[...]
    pack[0:256, 128:256] = value[...]
    pack[256:384, :] = output[...]
    left = jnp.concatenate(three(kv[...]) + [jnp.zeros((4, 128), F32)], 0)
    rows = three(norm[...])
    for ref in (bias, decay):
        for j in range(2):
            rows = rows + three(jnp.full((1, 128), ref[j], F32))
    right = jnp.concatenate(rows + [jnp.zeros((1, 128), F32)], 0)
    below = jnp.concatenate([steps[...].astype(F32), jnp.zeros((14, 256), F32)], 0)
    pack[384:416, :] = jnp.concatenate([jnp.concatenate([left, right], 1), below], 0).astype(BF)


def packed(bias, decay, gate, value, output, steps, kv, norm):
    return pl.pallas_call(
        pack_kernel,
        in_specs=[SMEM] * 2 + [VM] * 6,
        out_specs=VM,
        out_shape=sds((416, 256), BF),
        compiler_params=few(8),
        name="pack",
    )(bias, decay, gate, value, output, steps, kv, norm)


def state_chunk(x, rim, gain, pack, wb, ks, taps, cv, act):
    kv, _, bias, decay, steps = small_rows(pack)
    pad = jnp.zeros((6, 128), F32)
    bias = jnp.concatenate([bias, pad], 0)[:, 0:1]
    decay = jnp.concatenate([decay, pad], 0)[:, 0:1]
    steps = jnp.concatenate([steps, jnp.zeros((6, 256), F32)], 0).astype(BF)
    wv = pack[0:256, 128:256]
    taps[0] = kv * 0.5
    taps[1] = ks[:, 0:128] * 0.5
    taps[2] = ks[:, 128:256] * 0.5
    normed = rms(x, gain[...])
    before = rms(rim, gain[...])
    project(before, wv, cv, 0, 0)
    project(before, wb[...], cv, 0, 1)
    project(normed, wv, cv, 16, 0)
    project(normed, wb[...], cv, 16, 1)
    convolve(cv, act, taps, 1024)
    raw = dot(steps, normed, NT)
    dt = softplus(raw + bias)
    logs = -dt * decay
    tri = upper()
    carry = jnp.zeros((8, 1), F32)
    pieces = []
    for b in range(4):
        piece = cumulate(logs[:, b * BLK : (b + 1) * BLK], tri) + carry
        carry = piece[:, BLK - 1 : BLK]
        pieces.append(piece)
    cum = jnp.concatenate(pieces, 1)
    tail = jnp.exp(carry - cum) * dt
    spread = dot(parts(tail), expander(128), TN)
    scaled = (act[0] * spread).astype(BF)
    local = dot(jnp.concatenate([act[1].astype(BF), act[2].astype(BF)], 1), scaled, TN)
    total = jnp.sum(
        jnp.where(head_sel(128), jnp.broadcast_to(carry, (8, 128)), 0.0), axis=0, keepdims=True
    )
    return local, total


def later_chunks_kernel(x, rim, gain, pack, wb, ks, local, total, taps, cv, act):
    state, logs = state_chunk(x[...], rim[...], gain, pack, wb, ks, taps, cv, act)
    local[0] = state
    total[0] = jnp.broadcast_to(logs, (8, 128))


def first_chunk_kernel(
    x, rim, gain, pack, wb, ks, later, later_total,
    local, total, whole, whole_total, message, taps, cv, act,
):
    state, logs = state_chunk(x[...], rim[...], gain, pack, wb, ks, taps, cv, act)
    local[...] = state
    total[...] = jnp.broadcast_to(logs, (8, 128))
    for j in range(3):
        piece = later_total[j, 0:1, :]
        state = state * jnp.exp(piece) + later[j]
        logs = logs + piece
    whole[...] = state
    whole_total[...] = jnp.broadcast_to(logs, (8, 128))
    message[0:256, :] = state.astype(BF)
    message[256:272, :] = decay_rows(logs)


def sds(shape, dtype=F32):
    return jax.ShapeDtypeStruct(shape, dtype)


def whole_spec(shape):
    return pl.BlockSpec(shape, lambda *_: (0,) * len(shape))


def few(mib):
    return pltpu.CompilerParams(vmem_limit_bytes=mib << 20)


SMEM = pl.BlockSpec(memory_space=pltpu.SMEM)
VM = pl.BlockSpec(memory_space=pltpu.VMEM)


def fine_states(tokens, rim, gain, pack, scans, ks):
    common = [
        whole_spec((1, 256)),
        whole_spec((416, 256)),
        whole_spec((256, 256)),
        whole_spec((4, 256)),
    ]
    scratch = [
        pltpu.VMEM((3, 4, 128), F32),
        pltpu.VMEM((3, 1040, 128), F32),
        pltpu.VMEM((3, 1024, 128), F32),
    ]
    later, later_total = pl.pallas_call(
        later_chunks_kernel,
        grid=(3,),
        in_specs=[
            pl.BlockSpec((1024, 256), lambda i: (i + 1, 0)),
            pl.BlockSpec((16, 256), lambda i: ((i + 1) * 64 - 1, 0)),
        ]
        + common,
        out_specs=[
            pl.BlockSpec((1, 256, 128), lambda i: (i, 0, 0)),
            pl.BlockSpec((1, 8, 128), lambda i: (i, 0, 0)),
        ],
        out_shape=[sds((3, 256, 128)), sds((3, 8, 128))],
        scratch_shapes=scratch,
        compiler_params=few(20),
        name="later_chunks",
    )(tokens, tokens, gain, pack, scans, ks)
    first = pl.pallas_call(
        first_chunk_kernel,
        grid=(1,),
        in_specs=[pl.BlockSpec((1024, 256), lambda i: (0, 0)), whole_spec((16, 256))]
        + common
        + [whole_spec((3, 256, 128)), whole_spec((3, 8, 128))],
        out_specs=[
            whole_spec((256, 128)),
            whole_spec((8, 128)),
            whole_spec((256, 128)),
            whole_spec((8, 128)),
            whole_spec((272, 128)),
        ],
        out_shape=[
            sds((256, 128)),
            sds((8, 128)),
            sds((256, 128)),
            sds((8, 128)),
            sds((272, 128), BF),
        ],
        scratch_shapes=scratch,
        compiler_params=few(20),
        name="first_chunk",
    )(tokens, rim, gain, pack, scans, ks, later, later_total)
    return later, later_total, first


def combine(i, count, own, own_total, prior, prior_total, received):
    state = jnp.zeros_like(own)
    logs = jnp.zeros_like(own_total)
    zero = jnp.zeros((), F32)
    got = [(r[0:256, :].astype(F32), of_rows(r[256:272, :])) for r in received]
    for k in range(count - 1, 0, -1):
        s, l = got[k - 1]
        valid = i >= k
        state = jnp.where(valid, state * jnp.exp(l) + s, state)
        logs = jnp.where(valid, logs + l, logs)
    new_prior = state * jnp.exp(prior_total) + prior
    new_prior_total = logs + prior_total
    state = state * jnp.exp(own_total) + own
    logs = logs + own_total
    for m in range(1, count):
        s, l = got[count - m - 1]
        valid = i + m < count
        state = jnp.where(valid, state * jnp.exp(l) + s, state)
        logs = jnp.where(valid, logs + l, logs)
    return new_prior, new_prior_total, state, logs


def middle_kernel(axis, count, fresh, own, own_total, *refs):
    if fresh:
        prior, prior_total = jnp.zeros((256, 128), F32), jnp.zeros((1, 128), F32)
    else:
        prior, prior_total, refs = refs[0][...], refs[1][0:1, :], refs[2:]
    received, (np_ref, npt_ref, ns_ref, nst_ref, message) = refs[: count - 1], refs[count - 1 :]
    p, pt, s, st = combine(
        lax.axis_index(axis), count, own[...], own_total[0:1, :], prior, prior_total, received
    )
    np_ref[...] = p
    npt_ref[...] = jnp.broadcast_to(pt, (8, 128))
    ns_ref[...] = s
    nst_ref[...] = jnp.broadcast_to(st, (8, 128))
    message[0:256, :] = s.astype(BF)
    message[256:272, :] = decay_rows(st)


def middle_stage(axis, count, own, own_total, prior, received):
    return pl.pallas_call(
        lambda *refs: middle_kernel(axis, count, not prior, *refs),
        in_specs=[VM] * (2 + len(prior) + len(received)),
        out_specs=[VM] * 5,
        out_shape=[
            sds((256, 128)),
            sds((8, 128)),
            sds((256, 128)),
            sds((8, 128)),
            sds((272, 128), BF),
        ],
        compiler_params=few(4),
    )(own, own_total, *prior, *received)


def last_kernel(own, own_total, prior, prior_total, r1, r2, r3, l0, t0, later, later_total,
                o0, o1, o2, o3, sub):
    p, _, _, _ = combine(
        lax.axis_index("z"), 4, own[...], own_total[0:1, :], prior[...], prior_total[0:1, :],
        (r1, r2, r3),
    )
    sub[0] = p
    p = p * jnp.exp(t0[0:1, :]) + l0[...]
    sub[1] = p
    for j in range(2):
        p = p * jnp.exp(later_total[j, 0:1, :]) + later[j]
        sub[j + 2] = p
    h = lax.axis_index(HEAD)
    for k, out in enumerate((o0, o1, o2, o3)):
        out[...] = sub[h ^ k].astype(BF)


def last_stage(own, own_total, prior, received, l0, t0, later, later_total):
    return pl.pallas_call(
        last_kernel,
        in_specs=[VM] * 11,
        out_specs=[VM] * 4,
        out_shape=[sds((256, 128), BF)] * 4,
        scratch_shapes=[pltpu.VMEM((4, 256, 128), F32)],
        compiler_params=few(6),
        name="chain_last",
    )(own, own_total, *prior, *received, l0, t0, later, later_total)


def begin(before, wv, ws, cv, run, run_log):
    project(before, wv[...], cv, 0, 0)
    project(before, ws[...], cv, 0, 4)
    run[...] = jnp.zeros_like(run)
    run_log[...] = jnp.zeros_like(run_log)


def scan_block(
    normed, wg, wv, ws, wst, taps, bias, decay,
    lead, tail_out, maps_out, cv, act, sc, run, run_log,
):
    project(normed, wv[...], cv, 16, 0)
    project(normed, ws[...], cv, 16, 4)
    convolve(cv, act, taps, BLK)
    cv[:, 0:16, :] = cv[:, 256:272, :]
    raw = dot(wst[...], normed, NT)
    dt = softplus(raw + bias[...])
    logs = -dt * decay[...]
    cum = cumulate(logs, upper())
    last = cum[:, BLK - 1 : BLK]
    before_log = run_log[:, 0:1]
    stacked = jnp.concatenate(
        [jnp.exp(cum), jnp.exp(cum + before_log), jnp.exp(last - cum) * dt], 1
    )
    spread = dot(parts(stacked), expander(512), TN)
    run_log[...] = run_log[...] + last
    columns = dot(parts(cum), jnp.where(
        (iota((32, 128), 0) < 24) & (iota((32, 128), 0) % 8 == iota((32, 128), 1)), 1.0, 0.0
    ).astype(BF), TN)
    rows = cum - jnp.log(dt)
    in_map = jnp.concatenate([act[4].astype(BF), act[5].astype(BF)], 1)
    out_map = jnp.concatenate([act[6].astype(BF), act[7].astype(BF)], 1)
    maps_out[...] = out_map
    sc[...] = dot(out_map, in_map, NT)
    carried = dot(out_map, run[...].astype(BF))
    low_tri = iota((128, 128), 0) >= iota((128, 128), 1)
    lane_low = iota((BLK, 128), 1) < 64
    for p in range(4):
        cols = slice(p * 128, (p + 1) * 128)
        vals = act[p]
        v0 = jnp.where(lane_low, vals, 0.0).astype(BF)
        v1 = jnp.where(lane_low, 0.0, vals).astype(BF)
        upper_w, lower_w = [], []
        for h in (2 * p, 2 * p + 1):
            c0, c1 = columns[0:128, h : h + 1], columns[128:256, h : h + 1]
            r0, r1 = rows[h : h + 1, 0:128], rows[h : h + 1, 128:256]
            upper_w.append(
                (sc[0:128, 0:128] * jnp.exp(jnp.where(low_tri, c0 - r0, -jnp.inf))).astype(BF)
            )
            lower_w.append((sc[128:256, 0:128] * jnp.exp(c1 - r0)).astype(BF))
            lower_w.append(
                (sc[128:256, 128:256] * jnp.exp(jnp.where(low_tri, c1 - r1, -jnp.inf))).astype(BF)
            )
        top = dot(
            jnp.concatenate(upper_w, 1), jnp.concatenate([v0[0:128], v1[0:128]], 0)
        )
        bottom = dot(jnp.concatenate(lower_w, 1), jnp.concatenate([v0, v1], 0))
        gate = silu(dot(normed, wg[:, cols]))
        lead[0:128, cols] = (top + spread[0:128, cols] * carried[0:128, cols]) * gate[0:128]
        lead[128:256, cols] = (
            bottom + spread[128:256, cols] * carried[128:256, cols]
        ) * gate[128:256]
        tail_out[:, cols] = spread[256:512, cols] * gate
        scaled = (vals * spread[512:768, cols]).astype(BF)
        run[:, cols] = run[:, cols] * spread[255:256, cols] + dot(in_map, scaled, TN)


SCAN_SCRATCH = [
    pltpu.VMEM((8, 272, 128), F32),
    pltpu.VMEM((8, BLK, 128), F32),
    pltpu.VMEM((BLK, BLK), F32),
    pltpu.VMEM((256, 512), F32),
    pltpu.VMEM((8, 128), F32),
]


def fine_main_kernel(later, h, x, gain, ws, ks, p0, p1, p2, p3, *refs):
    (
        x0, x1, x2, lead, tail_out, maps_out, run, run_log, cv_end,
        wg, wv, wst, taps, bias, decay, cv, act, sc,
    ) = refs

    @pl.when(pl.program_id(0) == 0)
    def _():
        for j in range(4):
            taps[4 + j] = ks[:, j * 128 : (j + 1) * 128] * 0.5
        for j, p in enumerate((p0, p1, p2, p3)):
            cols = slice(j * 128, (j + 1) * 128)
            two = slice(2 * j, 2 * j + 2)
            wg[:, cols] = p[0:256, 0:128]
            wv[:, cols] = p[0:256, 128:256]
            kv, _, bias[two, :], decay[two, :], wst[two, :] = small_rows(p)
            taps[j] = kv * 0.5
        if later:
            run[...] = x0[...]
            run_log[...] = x1[...]
            cv[:, 0:16, :] = x2[...]
        else:
            rim = jnp.where(h[0] == 0, x0[...].astype(F32), x1[...].astype(F32))
            begin(rms(rim, gain[...]), wv, ws, cv, run, run_log)

    scan_block(
        rms(x[...], gain[...]), wg, wv, ws, wst[...].astype(BF), taps, bias[:, 0:1], decay[:, 0:1],
        lead, tail_out, maps_out, cv, act, sc, run, run_log,
    )
    cv_end[...] = cv[:, 0:16, :]


def fine_main(h, tokens, gain, scans, ks, packs, extra, later):
    at = 2 if later else 0
    if later:
        specs = [whole_spec((256, 512)), whole_spec((8, 128)), whole_spec((8, 16, 128))]
    else:
        specs = [
            whole_spec((16, 256)),
            pl.BlockSpec((16, 256), lambda i, h: (jnp.maximum(h[0] * 64 - 1, 0), 0)),
            whole_spec((8, 128)),
        ]
    return pl.pallas_call(
        lambda *refs: fine_main_kernel(later, *refs),
        grid_spec=pltpu.PrefetchScalarGridSpec(
            num_scalar_prefetch=1,
            grid=(2,),
            in_specs=[
                pl.BlockSpec((BLK, 256), lambda i, h: (h[0] * 4 + at + i, 0)),
                whole_spec((1, 256)),
                whole_spec((256, 512)),
                whole_spec((4, 512)),
            ]
            + [whole_spec((416, 256))] * 4
            + specs,
            out_specs=[
                pl.BlockSpec((BLK, 512), lambda i, h: (i, 0)),
                pl.BlockSpec((BLK, 512), lambda i, h: (i, 0)),
                pl.BlockSpec((BLK, 256), lambda i, h: (i, 0)),
                whole_spec((256, 512)),
                whole_spec((8, 128)),
                whole_spec((8, 16, 128)),
            ],
            scratch_shapes=[
                pltpu.VMEM((256, 512), BF),
                pltpu.VMEM((256, 512), BF),
                pltpu.VMEM((8, 256), F32),
                pltpu.VMEM((8, 4, 128), F32),
                pltpu.VMEM((8, 128), F32),
                pltpu.VMEM((8, 128), F32),
            ]
            + SCAN_SCRATCH[:3],
        ),
        out_shape=[
            sds((512, 512)), sds((512, 512)), sds((512, 256), BF),
            sds((256, 512)), sds((8, 128)), sds((8, 16, 128)),
        ],
        compiler_params=few(20),
        name="fine_main_b" if later else "fine_main_a",
    )(h, tokens, gain, scans, ks, *packs, *extra)


def fine_close_kernel(
    h, lead_a, lead_b, tail_a, tail_b, maps_a, maps_b, x, s0, s1, s2, s3, p0, p1, p2, p3, merge,
    merged, end_rows, lead, tail, maps, hidden,
):
    i = pl.program_id(0)

    @pl.when(i < 2)
    def _():
        lead[...], tail[...], maps[...] = lead_a[...], tail_a[...], maps_a[...]

    @pl.when(i >= 2)
    def _():
        lead[...], tail[...], maps[...] = lead_b[...], tail_b[...], maps_b[...]

    gated = []
    for j, s in enumerate((s0, s1, s2, s3)):
        cols = slice(j * 128, (j + 1) * 128)
        gated.append(lead[:, cols] + tail[:, cols] * dot(maps[...], s[...]))
    squares = sum(jnp.sum(g * g, axis=1, keepdims=True) for g in gated)
    factor = lax.rsqrt(squares / 512.0 + EPSILON)
    out = x[...].astype(F32)
    total = None
    for g, p in zip(gated, (p0, p1, p2, p3)):
        norm = small_rows(p)[1]
        piece = dot((g * factor * norm).astype(BF), p[256:384, :])
        total = piece if total is None else total + piece
    start = pl.multiple_of(i * BLK, BLK)
    hidden[0, pl.ds(start, BLK), :] = rounded(out[:, 0:128] + total[:, 0:128])
    hidden[1, pl.ds(start, BLK), :] = rounded(out[:, 128:256] + total[:, 128:256])

    @pl.when(i == pl.num_programs(0) - 1)
    def _():
        total = None
        for odd in range(2):
            for half in range(2):
                rows = hidden[half, pl.ds(odd, 512, stride=2), :].reshape(8, 2, 32, 128)
                for line in range(2):
                    tile = rows[:, line].reshape(256, 128).astype(BF)
                    at = (2 * line + odd) * 256 + half * 128
                    piece = dot(tile, merge[at : at + 128, :])
                    total = piece if total is None else total + piece
        result = total.astype(BF)
        merged[...] = result
        end_rows[...] = result[240:256]


def fine_close(h, leads, tails, maps, tokens, states, packs, merge):
    def halves(width):
        return [
            pl.BlockSpec((BLK, width), lambda i, h: (jnp.minimum(i, 1), 0)),
            pl.BlockSpec((BLK, width), lambda i, h: (jnp.maximum(i - 2, 0), 0)),
        ]

    return pl.pallas_call(
        fine_close_kernel,
        grid_spec=pltpu.PrefetchScalarGridSpec(
            num_scalar_prefetch=1,
            grid=(4,),
            in_specs=halves(512)
            + halves(512)
            + halves(256)
            + [pl.BlockSpec((BLK, 256), lambda i, h: (h[0] * 4 + i, 0))]
            + [whole_spec((256, 128))] * 4
            + [whole_spec((416, 256))] * 4
            + [whole_spec((1024, 1024))],
            out_specs=[whole_spec((256, 1024)), whole_spec((16, 1024))],
            scratch_shapes=[
                pltpu.VMEM((BLK, 512), F32),
                pltpu.VMEM((BLK, 512), F32),
                pltpu.VMEM((BLK, 256), BF),
                pltpu.VMEM((2, 1024, 128), F32),
            ],
        ),
        out_shape=[sds((256, 1024), BF), sds((16, 1024), BF)],
        compiler_params=few(20),
        name="fine_close",
    )(h, *leads, *tails, *maps, tokens, *states, *packs, merge)


def coarse_main_kernel(
    pos, q0, q1, q2, q3, ra, rb, rc, gain, wg, wv, ws, wst, kv, ks, bias, decay,
    lead, tail_out, maps_out, share, message,
    xs, sems, taps, cv, act, sc, run, run_log,
):
    i = pl.program_id(0)
    first = i == 0
    h = pos[0]

    @pl.when(first)
    def _():
        copies = [
            pltpu.make_async_copy(q, xs.at[h ^ k], sems.at[k])
            for k, q in enumerate((q0, q1, q2, q3))
        ]
        for copy in copies:
            copy.start()
        for j in range(4):
            cols = slice(j * 128, (j + 1) * 128)
            taps[j] = kv[:, cols] * 0.5
            taps[4 + j] = ks[:, cols] * 0.5
        rim = ra[...].astype(F32) + rb[...].astype(F32) + rc[...].astype(F32)
        begin(rms(rim, gain[...]), wv, ws, cv, run, run_log)
        for copy in copies:
            copy.wait()

    share[...] = xs[i, :, pl.ds(pl.multiple_of(h * 256, 256), 256)]
    scan_block(
        rms(xs[i], gain[...]), wg, wv, ws, wst[...], taps, bias[:, 0:1], decay[:, 0:1],
        lead, tail_out, maps_out, cv, act, sc, run, run_log,
    )

    @pl.when(i == pl.num_programs(0) - 1)
    def _():
        total = jnp.broadcast_to(run_log[:, 0:1], (8, 512))
        row = jnp.sum(jnp.where(head_sel(512), total, 0.0), axis=0, keepdims=True)
        extra = decay_rows(row)
        for n in range(16):
            for half in range(2):
                cols = slice(half * 256, (half + 1) * 256)
                message[2 * n + half, 0:16, :] = run[n * 16 : (n + 1) * 16, cols].astype(BF)
                message[2 * n + half, 16:32, :] = extra[:, cols]


def single(shape):
    return pl.BlockSpec(shape, lambda *_: (0,) * len(shape), pipeline_mode=pl.Buffered(1))


ANY = pl.BlockSpec(memory_space=pl.ANY)


def coarse_main(pos, pieces, rims, gain, wg, wv, ws, wst, kv, ks, bias, decay):
    return pl.pallas_call(
        coarse_main_kernel,
        grid=(4,),
        in_specs=[SMEM]
        + [ANY] * 4
        + [whole_spec((16, 1024))] * 3
        + [
            whole_spec((1, 1024)),
            single((1024, 512)),
            single((1024, 512)),
            single((1024, 512)),
            whole_spec((8, 1024)),
            whole_spec((4, 512)),
            whole_spec((4, 512)),
            whole_spec((8, 128)),
            whole_spec((8, 128)),
        ],
        out_specs=[
            pl.BlockSpec((BLK, 512), lambda i: (i, 0)),
            pl.BlockSpec((BLK, 512), lambda i: (i, 0)),
            pl.BlockSpec((BLK, 256), lambda i: (i, 0)),
            pl.BlockSpec((BLK, 256), lambda i: (i, 0)),
            whole_spec((32, 32, 256)),
        ],
        out_shape=[
            sds((1024, 512)),
            sds((1024, 512)),
            sds((1024, 256), BF),
            sds((1024, 256), BF),
            sds((32, 32, 256), BF),
        ],
        scratch_shapes=[
            pltpu.VMEM((4, 256, 1024), BF),
            pltpu.SemaphoreType.DMA((4,)),
            pltpu.VMEM((8, 4, 128), F32),
        ]
        + SCAN_SCRATCH,
        compiler_params=few(20),
        name="coarse_main",
    )(pos, *pieces, *rims, gain, wg, wv, ws, wst, kv, ks, bias, decay)


def prefix_kernel(got, out):
    state = jnp.zeros((16, 256), F32)
    for d in range(32):
        out[d] = state.astype(BF)
        state = state * jnp.exp(of_rows(got[d, 16:32, :])) + got[d, 0:16, :].astype(F32)


def prefix(got):
    return pl.pallas_call(
        prefix_kernel,
        in_specs=[VM],
        out_specs=VM,
        out_shape=sds((32, 16, 256), BF),
        compiler_params=few(4),
        name="prefix",
    )(got)


def coarse_close_kernel(pos, lead, tail, maps, got, norm, wo, kk, ks, sk, ss, squares, state):
    @pl.when(pl.program_id(0) == 0)
    def _():
        for n in range(16):
            for half in range(2):
                cols = slice(half * 256, (half + 1) * 256)
                state[n * 16 : (n + 1) * 16, cols] = got[2 * n + half]

    gated = lead[...] + tail[...] * dot(maps[...], state[...])
    sq = gated * gated
    hi = sq.astype(BF)
    low = (sq - hi.astype(F32)).astype(BF)
    ones = jnp.ones((8, 512), BF)
    squares[...] = dot(ones, hi, NT) + dot(ones, low, NT)
    scaled = (gated * norm[...]).astype(BF)
    h = pos[0]
    for k, out in enumerate((kk, sk, ks, ss)):
        at = pl.multiple_of((h ^ k) * 256, 256)
        out[...] = dot(scaled, wo[:, pl.ds(at, 256)]).astype(BF)


def coarse_close(pos, lead, tail, maps, got, norm, wo):
    rows = pl.BlockSpec((BLK, 256), lambda i: (i, 0))
    return pl.pallas_call(
        coarse_close_kernel,
        grid=(4,),
        in_specs=[
            SMEM,
            pl.BlockSpec((BLK, 512), lambda i: (i, 0)),
            pl.BlockSpec((BLK, 512), lambda i: (i, 0)),
            rows,
            whole_spec((32, 16, 256)),
            whole_spec((1, 512)),
            single((512, 1024)),
        ],
        out_specs=[rows] * 4 + [pl.BlockSpec((8, BLK), lambda i: (0, i))],
        out_shape=[sds((1024, 256), BF)] * 4 + [sds((8, 1024))],
        scratch_shapes=[pltpu.VMEM((256, 512), BF)],
        compiler_params=few(20),
        name="coarse_close",
    )(pos, lead, tail, maps, got, norm, wo)


def final_kernel(share, kk, sk, far, sq, sq_far, out):
    factor = lax.rsqrt((sq[...] + sq_far[...]) / 2048.0 + EPSILON)
    pick = jnp.where(iota((32, 256), 0) % 8 == 0, 1.0, 0.0).astype(BF)
    spread = dot(parts(factor), pick, TN)
    total = kk[...].astype(F32) + sk[...].astype(F32) + far[...].astype(F32)
    out[...] = (share[...].astype(F32) + total * spread).astype(BF)


def final(share, kk, sk, far, sq, sq_far):
    rows = pl.BlockSpec((BLK, 256), lambda i: (i, 0))
    return pl.pallas_call(
        final_kernel,
        grid=(4,),
        in_specs=[rows] * 4 + [pl.BlockSpec((8, BLK), lambda i: (0, i))] * 2,
        out_specs=rows,
        out_shape=sds((1024, 256), BF),
        compiler_params=few(6),
        name="final",
    )(share, kk, sk, far, sq, sq_far)


def passed(x, axes, pairs):
    return lax.ppermute(x, axes, pairs)


def swapped(x, mask):
    return passed(x, HEAD, [(j, j ^ mask) for j in range(4)])


def round_of(x, axis):
    got = []
    for k in (1, 2, 3):
        got.append(passed(x, axis, [(j, (j + k) % 4) for j in range(4)]))
    return got


def lanes(v):
    return jnp.broadcast_to(v[:, None], (v.shape[0], 128))


def shards(
    tokens, fine_gain, fine_gate, fine_value, fine_scans, fine_steps, fine_kernel, fine_taps,
    fine_bias, fine_decay, fine_norm, fine_output, merge_weight, coarse_gain, coarse_gate,
    coarse_value, coarse_scans, coarse_steps, coarse_kernel, coarse_taps, coarse_bias,
    coarse_decay, coarse_norm, coarse_output,
):
    here = lax.axis_index(HEAD).astype(jnp.int32)[None]
    rim = passed(tokens[4080:], SEQ, [(i, i + 1) for i in range(31)])
    pack = packed(
        fine_bias, fine_decay, fine_gate, fine_value, fine_output, fine_steps.T, fine_kernel,
        fine_norm[None],
    )
    packs = [pack] + [swapped(pack, m) for m in (1, 2, 3)]
    gain = fine_gain[None]
    later, later_total, (l0, t0, own, own_total, message) = fine_states(
        tokens, rim, gain, pack, fine_scans, fine_taps
    )
    got = round_of(message, "x")
    first = fine_main(here, tokens, gain, fine_scans, fine_taps, packs, (rim, tokens, t0), False)
    *prior, own, own_total, message = middle_stage("x", 4, own, own_total, (), got)
    got = [passed(message, "u", [(0, 1), (1, 0)])]
    *prior, own, own_total, message = middle_stage("u", 2, own, own_total, prior, got)
    got = round_of(message, "z")
    second = fine_main(
        here, tokens, gain, fine_scans, fine_taps, packs, first[3:], True
    )
    subs = last_stage(own, own_total, prior, got, l0, t0, later, later_total)
    states = [subs[0]] + [swapped(subs[m], m) for m in (1, 2, 3)]
    merged, end_rows = fine_close(
        here, (first[0], second[0]), (first[1], second[1]), (first[2], second[2]), tokens, states,
        packs, merge_weight,
    )

    rim_a = passed(end_rows, ALL, [(4 * s + 3, 4 * s + 4) for s in range(31)])
    rim_b = passed(end_rows, ALL, [(4 * s + 3, 4 * s + 7) for s in range(31)])
    across = swapped(merged, 2)
    beside = swapped(merged, 1)
    rim_c = swapped(rim_a + rim_b, 1)
    both = swapped(across, 1)
    lead, tail, maps, share, message = coarse_main(
        here,
        (merged, beside, across, both),
        (rim_a, rim_b, rim_c),
        coarse_gain[None],
        coarse_gate,
        coarse_value,
        coarse_scans,
        coarse_steps.T,
        coarse_kernel,
        coarse_taps,
        lanes(coarse_bias),
        lanes(coarse_decay),
    )
    got = lax.all_to_all(message, SEQ, split_axis=0, concat_axis=0, tiled=True)
    got = lax.all_to_all(prefix(got), SEQ, split_axis=0, concat_axis=0, tiled=True)
    kk, ks, sk, ss, squares = coarse_close(
        here, lead, tail, maps, got, coarse_norm[None], coarse_output
    )
    from_ss = swapped(ss, 1)
    from_sk = swapped(sk, 1)
    squares = squares + swapped(squares, 1)
    far = (ks.astype(F32) + from_ss.astype(F32)).astype(BF)
    far = swapped(far, 2)
    return final(share, kk, from_sk, far, squares, swapped(squares, 2))


def solution(mesh):
    finer = Mesh(mesh.devices.reshape(4, 2, 4, 2, 2), ALL)
    cols = P(None, HEAD)
    return jax.shard_map(
        shards,
        mesh=finer,
        in_specs=(
            P(SEQ, None), P(), cols, cols, P(), cols, cols, P(), P(HEAD), P(HEAD), P(HEAD),
            P(HEAD, None), P(), P(), cols, cols, P(), cols, cols, P(), P(HEAD), P(HEAD), P(HEAD),
            P(HEAD, None),
        ),
        out_specs=P(SEQ, HEAD),
        check_vma=False,
    )
```

```python
import jax
import jax.numpy as jnp
from jax import lax
from jax.experimental import pallas as pl
from jax.experimental.pallas import tpu as pltpu
from jax.sharding import Mesh
from jax.sharding import PartitionSpec as P


SEQ = ("z", "u", "x")
HEAD = ("y", "c")
ALL = ("z", "u", "x", "y", "c")
EPSILON = 1e-05
BLK = 256
BF = jnp.bfloat16
F32 = jnp.float32
NN = (((1,), (0,)), ((), ()))
NT = (((1,), (1,)), ((), ()))
TN = (((0,), (0,)), ((), ()))


def dot(a, b, dims=NN):
    return lax.dot_general(a, b, dims, preferred_element_type=F32)


def parts(x):
    hi = x.astype(BF).astype(F32)
    rest = x - hi
    mid = rest.astype(BF).astype(F32)
    low = rest - mid
    return jnp.concatenate([hi, mid, low, jnp.zeros_like(x)], 0).astype(BF)


def decay_rows(row):
    hi = row.astype(BF).astype(F32)
    rest = row - hi
    mid = rest.astype(BF).astype(F32)
    low = rest - mid
    return jnp.concatenate([hi, mid, low, jnp.zeros((13, row.shape[1]), F32)], 0).astype(BF)


def of_rows(rows):
    rows = rows.astype(F32)
    return rows[0:1] + rows[1:2] + rows[2:3]


def iota(shape, dim):
    return lax.broadcasted_iota(jnp.int32, shape, dim)


def head_sel(width):
    return iota((8, width), 0) == iota((8, width), 1) // 64


def expander(width):
    r, lane = iota((32, width), 0), iota((32, width), 1)
    return jnp.where((r < 24) & (r % 8 == lane // 64), 1.0, 0.0).astype(BF)


def upper():
    return jnp.where(iota((BLK, BLK), 0) <= iota((BLK, BLK), 1), 1.0, 0.0).astype(BF)


def silu(v):
    h = v * 0.5
    return h + h * jnp.tanh(h)


def softplus(v):
    return jnp.maximum(v, 0.0) + jnp.log1p(jnp.exp(-jnp.abs(v)))


def rms(x, gain):
    x = x.astype(F32)
    return (x * lax.rsqrt(jnp.mean(x * x, axis=-1, keepdims=True) + EPSILON) * gain).astype(BF)


def cumulate(logs, tri):
    s = dot(parts(logs), tri)
    return s[0:8] + s[8:16] + s[16:24]


def spaced(length):
    return length // 8 + 1


def convolve(cv, act, half_taps, length):
    apart = spaced(length)

    def slab(c, carry):
        taps = half_taps[c]
        rows = [cv[c, pl.ds(13 + i, 8, stride=apart), :] for i in range(3)]
        for i in range(apart):
            rows.append(cv[c, pl.ds(16 + i, 8, stride=apart), :])
            h = rows[i] * taps[0:1]
            for k in range(1, 4):
                h = h + rows[i + k] * taps[k : k + 1]
            act[c, pl.ds(i, 8, stride=apart), :] = h + h * jnp.tanh(h)
        return carry

    lax.fori_loop(0, cv.shape[0], slab, 0)


def project(rows, weights, cv, start, slab):
    product = dot(rows, weights)
    for j in range(product.shape[1] // 128):
        cv[slab + j, start : start + rows.shape[0], :] = product[:, j * 128 : (j + 1) * 128]


def rounded(x):
    return x.astype(BF).astype(F32)


def small_rows(pack):
    rows = pack[384:416, :].astype(F32)
    kv = rows[0:4, 0:128] + rows[4:8, 0:128] + rows[8:12, 0:128]
    right = rows[0:16, 128:256]
    norm, b0, b1, d0, d1 = (of_rows(right[3 * j : 3 * j + 3]) for j in range(5))
    return kv, norm, jnp.concatenate([b0, b1], 0), jnp.concatenate([d0, d1], 0), rows[16:18]


def three(row):
    hi = row.astype(BF).astype(F32)
    rest = row - hi
    mid = rest.astype(BF).astype(F32)
    return [hi, mid, rest - mid]


def run_copies(pairs, sems):
    copies = [pltpu.make_async_copy(a, b, sems.at[j]) for j, (a, b) in enumerate(pairs)]
    for copy in copies:
        copy.start()
    return copies


def pack_kernel(
    bias, decay, gate, value, output, steps, kv, norm, tokens, pack, ends, kv_v, norm_v, steps_v, sems
):
    copies = run_copies(
        (
            (kv, kv_v),
            (norm, norm_v),
            (steps, steps_v),
            (tokens.at[4080:4096], ends),
            (gate, pack.at[0:256, 0:128]),
            (value, pack.at[0:256, 128:256]),
            (output, pack.at[256:384]),
        ),
        sems,
    )
    for copy in copies[:3]:
        copy.wait()
    left = jnp.concatenate(three(kv_v[...]) + [jnp.zeros((4, 128), F32)], 0)
    rows = three(norm_v[...])
    for ref in (bias, decay):
        for j in range(2):
            rows = rows + three(jnp.full((1, 128), ref[j], F32))
    right = jnp.concatenate(rows + [jnp.zeros((1, 128), F32)], 0)
    below = jnp.concatenate([steps_v[...].astype(F32), jnp.zeros((14, 256), F32)], 0)
    pack[384:416, :] = jnp.concatenate([jnp.concatenate([left, right], 1), below], 0).astype(BF)
    for copy in copies[3:]:
        copy.wait()


def packed(bias, decay, gate, value, output, steps, kv, norm, tokens):
    return pl.pallas_call(
        pack_kernel,
        in_specs=[SMEM] * 2 + [HBM] * 7,
        out_specs=[VM] * 2,
        out_shape=[sds((416, 256), BF), sds((16, 256), BF)],
        scratch_shapes=[
            pltpu.VMEM((4, 128), F32),
            pltpu.VMEM((1, 128), F32),
            pltpu.VMEM((2, 256), BF),
            pltpu.SemaphoreType.DMA((7,)),
        ],
        compiler_params=few(4),
        name="pack",
    )(bias, decay, gate, value, output, steps, kv, norm, tokens)


def params_kernel(bias, decay, kv, ks, gain, steps, norm, taps, both, *refs):
    outs, kv_v, ks_v, sems = refs[:3], *refs[3:]
    copies = run_copies(
        ((kv, kv_v), (ks, ks_v), (gain, outs[0]), (steps, outs[1]), (norm, outs[2])), sems
    )
    for copy in copies:
        copy.wait()
    for j in range(4):
        cols = slice(j * 128, (j + 1) * 128)
        taps[j] = kv_v[:, cols] * 0.5
        taps[4 + j] = ks_v[:, cols] * 0.5
    rows = [jnp.full((1, 128), ref[j], F32) for ref in (bias, decay) for j in range(8)]
    both[...] = jnp.concatenate(rows, 0)


def coarse_params(bias, decay, kv, ks, gain, steps, norm):
    return pl.pallas_call(
        params_kernel,
        in_specs=[SMEM] * 2 + [HBM] * 5,
        out_specs=[VM] * 5,
        out_shape=[
            sds((8, 4, 128)), sds((16, 128)), sds((1, 1024)), sds((8, 1024), BF), sds((1, 512)),
        ],
        scratch_shapes=[
            pltpu.VMEM((4, 512), F32),
            pltpu.VMEM((4, 512), F32),
            pltpu.SemaphoreType.DMA((5,)),
        ],
        compiler_params=few(4),
        name="coarse_params",
    )(bias, decay, kv, ks, gain, steps, norm)


def state_chunk(x, rim, gain, pack, scans, ks, taps, cv, act):
    kv, _, bias, decay, steps = small_rows(pack)
    pad = jnp.zeros((6, 128), F32)
    bias = jnp.concatenate([bias, pad], 0)[:, 0:1]
    decay = jnp.concatenate([decay, pad], 0)[:, 0:1]
    steps = jnp.concatenate([steps, jnp.zeros((6, 256), F32)], 0).astype(BF)
    wv, wb = pack[0:256, 128:256], scans[:, 0:256]
    taps[0] = kv * 0.5
    taps[1] = ks[:, 0:128] * 0.5
    taps[2] = ks[:, 128:256] * 0.5
    normed = rms(x, gain[...])
    before = rms(rim, gain[...])
    project(before, wv, cv, 0, 0)
    project(before, wb, cv, 0, 1)
    project(normed, wv, cv, 16, 0)
    project(normed, wb, cv, 16, 1)
    convolve(cv, act, taps, 1024)
    raw = dot(steps, normed, NT)
    dt = softplus(raw + bias)
    logs = -dt * decay
    tri = upper()
    carry = jnp.zeros((8, 1), F32)
    pieces = []
    for b in range(4):
        piece = cumulate(logs[:, b * BLK : (b + 1) * BLK], tri) + carry
        carry = piece[:, BLK - 1 : BLK]
        pieces.append(piece)
    cum = jnp.concatenate(pieces, 1)
    tail = jnp.exp(carry - cum) * dt
    spread = dot(parts(tail), expander(128), TN)
    scaled = (act[0, 0:1024] * spread).astype(BF)
    local = dot(jnp.concatenate([act[1, 0:1024].astype(BF), act[2, 0:1024].astype(BF)], 1), scaled, TN)
    total = jnp.sum(
        jnp.where(head_sel(128), jnp.broadcast_to(carry, (8, 128)), 0.0), axis=0, keepdims=True
    )
    return local, total


def later_chunks_kernel(
    tokens, gain_h, pack, scans_h, ks_h,
    local, total, x0, mine, mine_rim, gain, scans, ks, xs, taps, cv, act, sems, x_sems,
):
    i = pl.program_id(0)
    start = pl.multiple_of(lax.axis_index(HEAD) * 1024, 1024)
    early = pl.multiple_of(jnp.maximum(start - 16, 0), 16)
    mine_pairs = (
        (tokens.at[0:1024], x0),
        (tokens.at[pl.ds(start, 1024)], mine),
        (tokens.at[pl.ds(early, 16)], mine_rim),
    )

    def chunk(j):
        begin_row = pl.multiple_of((j + 1) * 1024 - 16, 16)
        return pltpu.make_async_copy(tokens.at[pl.ds(begin_row, 1040)], xs.at[j], x_sems.at[j])

    @pl.when(i == 0)
    def _():
        chunk(0).start()
        copies = run_copies(((gain_h, gain), (scans_h, scans), (ks_h, ks)), sems)
        chunk(1).start()
        chunk(2).start()
        for j, (a, b) in enumerate(mine_pairs):
            pltpu.make_async_copy(a, b, sems.at[3 + j]).start()
        for copy in copies:
            copy.wait()

    chunk(i).wait()
    state, logs = state_chunk(xs[i, 16:1040], xs[i, 0:16], gain, pack, scans, ks, taps, cv, act)
    local[i] = state
    total[i] = jnp.broadcast_to(logs, (8, 128))

    @pl.when(i == 2)
    def _():
        for j, (a, b) in enumerate(mine_pairs):
            pltpu.make_async_copy(a, b, sems.at[3 + j]).wait()


def first_chunk_kernel(
    x, rim, gain, pack, scans, ks, later, later_total,
    local, total, whole, whole_total, message, taps, cv, act,
):
    state, logs = state_chunk(x[...], rim[...], gain, pack, scans, ks, taps, cv, act)
    local[...] = state
    total[...] = jnp.broadcast_to(logs, (8, 128))
    for j in range(3):
        piece = later_total[j, 0:1, :]
        state = state * jnp.exp(piece) + later[j]
        logs = logs + piece
    whole[...] = state
    whole_total[...] = jnp.broadcast_to(logs, (8, 128))
    message[0:256, :] = state.astype(BF)
    message[256:272, :] = decay_rows(logs)


def sds(shape, dtype=F32):
    return jax.ShapeDtypeStruct(shape, dtype)


def few(mib):
    return pltpu.CompilerParams(vmem_limit_bytes=mib << 20)


SMEM = pl.BlockSpec(memory_space=pltpu.SMEM)
VM = pl.BlockSpec(memory_space=pltpu.VMEM)
HBM = pl.BlockSpec(memory_space=pltpu.HBM)


def fine_states(tokens, ends_from, gain, pack, scans, ks):
    scratch = [
        pltpu.VMEM((3, 4, 128), F32),
        pltpu.VMEM((3, 1048, 128), F32),
        pltpu.VMEM((3, 1032, 128), F32),
    ]
    later, later_total, x0, *resident = pl.pallas_call(
        later_chunks_kernel,
        grid=(3,),
        in_specs=[HBM, HBM, VM, HBM, HBM],
        out_specs=[VM] * 8,
        out_shape=[
            sds((3, 256, 128)),
            sds((3, 8, 128)),
            sds((1024, 256), BF),
            sds((1024, 256), BF),
            sds((16, 256), BF),
            sds((1, 256)),
            sds((256, 512), BF),
            sds((4, 512)),
        ],
        scratch_shapes=[pltpu.VMEM((3, 1040, 256), BF)]
        + scratch
        + [pltpu.SemaphoreType.DMA((6,)), pltpu.SemaphoreType.DMA((3,))],
        compiler_params=few(16),
        name="later_chunks",
    )(tokens, gain, pack, scans, ks)
    _, _, gain, scans, ks = resident
    first = pl.pallas_call(
        first_chunk_kernel,
        in_specs=[VM] * 8,
        out_specs=[VM] * 5,
        out_shape=[
            sds((256, 128)),
            sds((8, 128)),
            sds((256, 128)),
            sds((8, 128)),
            sds((272, 128), BF),
        ],
        scratch_shapes=scratch,
        compiler_params=few(16),
        name="first_chunk",
    )(x0, ends_from, gain, pack, scans, ks, later, later_total)
    return later, later_total, resident, first


def combine(i, count, own, own_total, prior, prior_total, received):
    state = jnp.zeros_like(own)
    logs = jnp.zeros_like(own_total)
    zero = jnp.zeros((), F32)
    got = [(r[0:256, :].astype(F32), of_rows(r[256:272, :])) for r in received]
    for k in range(count - 1, 0, -1):
        s, l = got[k - 1]
        valid = i >= k
        state = jnp.where(valid, state * jnp.exp(l) + s, state)
        logs = jnp.where(valid, logs + l, logs)
    new_prior = state * jnp.exp(prior_total) + prior
    new_prior_total = logs + prior_total
    state = state * jnp.exp(own_total) + own
    logs = logs + own_total
    for m in range(1, count):
        s, l = got[count - m - 1]
        valid = i + m < count
        state = jnp.where(valid, state * jnp.exp(l) + s, state)
        logs = jnp.where(valid, logs + l, logs)
    return new_prior, new_prior_total, state, logs


def middle_kernel(axis, count, fresh, own, own_total, *refs):
    if fresh:
        prior, prior_total = jnp.zeros((256, 128), F32), jnp.zeros((1, 128), F32)
    else:
        prior, prior_total, refs = refs[0][...], refs[1][0:1, :], refs[2:]
    received, (np_ref, npt_ref, ns_ref, nst_ref, message) = refs[: count - 1], refs[count - 1 :]
    p, pt, s, st = combine(
        lax.axis_index(axis), count, own[...], own_total[0:1, :], prior, prior_total, received
    )
    np_ref[...] = p
    npt_ref[...] = jnp.broadcast_to(pt, (8, 128))
    ns_ref[...] = s
    nst_ref[...] = jnp.broadcast_to(st, (8, 128))
    message[0:256, :] = s.astype(BF)
    message[256:272, :] = decay_rows(st)


def middle_stage(axis, count, own, own_total, prior, received):
    return pl.pallas_call(
        lambda *refs: middle_kernel(axis, count, not prior, *refs),
        in_specs=[VM] * (2 + len(prior) + len(received)),
        out_specs=[VM] * 5,
        out_shape=[
            sds((256, 128)),
            sds((8, 128)),
            sds((256, 128)),
            sds((8, 128)),
            sds((272, 128), BF),
        ],
        compiler_params=few(4),
    )(own, own_total, *prior, *received)


def last_kernel(own, own_total, prior, prior_total, r1, r2, r3, l0, t0, later, later_total,
                o0, o1, o2, o3, sub):
    p, _, _, _ = combine(
        lax.axis_index("z"), 4, own[...], own_total[0:1, :], prior[...], prior_total[0:1, :],
        (r1, r2, r3),
    )
    sub[0] = p
    p = p * jnp.exp(t0[0:1, :]) + l0[...]
    sub[1] = p
    for j in range(2):
        p = p * jnp.exp(later_total[j, 0:1, :]) + later[j]
        sub[j + 2] = p
    h = lax.axis_index(HEAD)
    for k, out in enumerate((o0, o1, o2, o3)):
        out[...] = sub[h ^ k].astype(BF)


def last_stage(own, own_total, prior, received, l0, t0, later, later_total):
    return pl.pallas_call(
        last_kernel,
        in_specs=[VM] * 11,
        out_specs=[VM] * 4,
        out_shape=[sds((256, 128), BF)] * 4,
        scratch_shapes=[pltpu.VMEM((4, 256, 128), F32)],
        compiler_params=few(6),
        name="chain_last",
    )(own, own_total, *prior, *received, l0, t0, later, later_total)


def begin(before, wv, ws, cv, run, run_log):
    project(before, wv[...], cv, 0, 0)
    project(before, ws[...], cv, 0, 4)
    run[...] = jnp.zeros_like(run)
    run_log[...] = jnp.zeros_like(run_log)


def scan_block(
    normed, wg, wv, ws, wst, taps, bias, decay,
    lead, tail_out, maps_out, cv, act, sc, run, run_log,
):
    project(normed, wv[...], cv, 16, 0)
    project(normed, ws[...], cv, 16, 4)
    convolve(cv, act, taps, BLK)
    cv[:, 0:16, :] = cv[:, 256:272, :]
    raw = dot(wst[...], normed, NT)
    dt = softplus(raw + bias[...])
    logs = -dt * decay[...]
    cum = cumulate(logs, upper())
    last = cum[:, BLK - 1 : BLK]
    before_log = run_log[:, 0:1]
    stacked = jnp.concatenate(
        [jnp.exp(cum), jnp.exp(cum + before_log), jnp.exp(last - cum) * dt], 1
    )
    spread = dot(parts(stacked), expander(512), TN)
    run_log[...] = run_log[...] + last
    columns = dot(parts(cum), jnp.where(
        (iota((32, 128), 0) < 24) & (iota((32, 128), 0) % 8 == iota((32, 128), 1)), 1.0, 0.0
    ).astype(BF), TN)
    rows = cum - jnp.log(dt)
    in_map = jnp.concatenate([act[4, 0:BLK].astype(BF), act[5, 0:BLK].astype(BF)], 1)
    out_map = jnp.concatenate([act[6, 0:BLK].astype(BF), act[7, 0:BLK].astype(BF)], 1)
    maps_out[...] = out_map
    sc[...] = dot(out_map, in_map, NT)
    carried = dot(out_map, run[...].astype(BF))
    low_tri = iota((128, 128), 0) >= iota((128, 128), 1)
    lane_low = iota((BLK, 128), 1) < 64
    for p in range(4):
        cols = slice(p * 128, (p + 1) * 128)
        vals = act[p, 0:BLK]
        v0 = jnp.where(lane_low, vals, 0.0).astype(BF)
        v1 = jnp.where(lane_low, 0.0, vals).astype(BF)
        upper_w, lower_w = [], []
        for h in (2 * p, 2 * p + 1):
            c0, c1 = columns[0:128, h : h + 1], columns[128:256, h : h + 1]
            r0, r1 = rows[h : h + 1, 0:128], rows[h : h + 1, 128:256]
            upper_w.append(
                (sc[0:128, 0:128] * jnp.exp(jnp.where(low_tri, c0 - r0, -jnp.inf))).astype(BF)
            )
            lower_w.append((sc[128:256, 0:128] * jnp.exp(c1 - r0)).astype(BF))
            lower_w.append(
                (sc[128:256, 128:256] * jnp.exp(jnp.where(low_tri, c1 - r1, -jnp.inf))).astype(BF)
            )
        top = dot(
            jnp.concatenate(upper_w, 1), jnp.concatenate([v0[0:128], v1[0:128]], 0)
        )
        bottom = dot(jnp.concatenate(lower_w, 1), jnp.concatenate([v0, v1], 0))
        gate = silu(dot(normed, wg[:, cols]))
        lead[0:128, cols] = (top + spread[0:128, cols] * carried[0:128, cols]) * gate[0:128]
        lead[128:256, cols] = (
            bottom + spread[128:256, cols] * carried[128:256, cols]
        ) * gate[128:256]
        tail_out[:, cols] = spread[256:512, cols] * gate
        scaled = (vals * spread[512:768, cols]).astype(BF)
        run[:, cols] = run[:, cols] * spread[255:256, cols] + dot(in_map, scaled, TN)


SCAN_SCRATCH = [
    pltpu.VMEM((8, 280, 128), F32),
    pltpu.VMEM((8, BLK + 8, 128), F32),
    pltpu.VMEM((BLK, BLK), F32),
    pltpu.VMEM((256, 512), F32),
    pltpu.VMEM((8, 128), F32),
]


def fine_main_kernel(later, x, gain, ws, ks, p0, p1, p2, p3, *refs):
    (
        x0, x1, x2, lead, tail_out, maps_out, run, run_log, cv_end,
        wg, wv, wst, taps, bias, decay, cv, act, sc,
    ) = refs

    @pl.when(pl.program_id(0) == 0)
    def _():
        for j in range(4):
            taps[4 + j] = ks[:, j * 128 : (j + 1) * 128] * 0.5
        for j, p in enumerate((p0, p1, p2, p3)):
            cols = slice(j * 128, (j + 1) * 128)
            two = slice(2 * j, 2 * j + 2)
            wg[:, cols] = p[0:256, 0:128]
            wv[:, cols] = p[0:256, 128:256]
            kv, _, bias[two, :], decay[two, :], wst[two, :] = small_rows(p)
            taps[j] = kv * 0.5
        if later:
            run[...] = x0[...]
            run_log[...] = x1[...]
            cv[:, 0:16, :] = x2[...]
        else:
            rim = jnp.where(lax.axis_index(HEAD) == 0, x0[...].astype(F32), x1[...].astype(F32))
            begin(rms(rim, gain[...]), wv, ws, cv, run, run_log)

    scan_block(
        rms(x[...], gain[...]), wg, wv, ws, wst[...].astype(BF), taps, bias[:, 0:1], decay[:, 0:1],
        lead, tail_out, maps_out, cv, act, sc, run, run_log,
    )
    cv_end[...] = cv[:, 0:16, :]


def fine_main(x, gain, scans, ks, packs, extra, later):
    at = 2 if later else 0
    rows = [pl.BlockSpec((BLK, n), lambda i: (i, 0)) for n in (512, 512, 256)]
    return pl.pallas_call(
        lambda *refs: fine_main_kernel(later, *refs),
        grid=(2,),
        in_specs=[pl.BlockSpec((BLK, 256), lambda i: (at + i, 0))] + [VM] * 10,
        out_specs=rows + [VM] * 3,
        out_shape=[
            sds((512, 512)), sds((512, 512)), sds((512, 256), BF),
            sds((256, 512)), sds((8, 128)), sds((8, 16, 128)),
        ],
        scratch_shapes=[
            pltpu.VMEM((256, 512), BF),
            pltpu.VMEM((256, 512), BF),
            pltpu.VMEM((8, 256), F32),
            pltpu.VMEM((8, 4, 128), F32),
            pltpu.VMEM((8, 128), F32),
            pltpu.VMEM((8, 128), F32),
        ]
        + SCAN_SCRATCH[:3],
        compiler_params=few(16),
        name="fine_main_b" if later else "fine_main_a",
    )(x, gain, scans, ks, *packs, *extra)


def fine_close_kernel(
    lead_a, lead_b, tail_a, tail_b, maps_a, maps_b, x, s0, s1, s2, s3, p0, p1, p2, p3, merge,
    merged, end_rows, lead, tail, maps, hidden,
):
    i = pl.program_id(0)

    @pl.when(i < 2)
    def _():
        lead[...], tail[...], maps[...] = lead_a[...], tail_a[...], maps_a[...]

    @pl.when(i >= 2)
    def _():
        lead[...], tail[...], maps[...] = lead_b[...], tail_b[...], maps_b[...]

    gated = []
    for j, s in enumerate((s0, s1, s2, s3)):
        cols = slice(j * 128, (j + 1) * 128)
        gated.append(lead[:, cols] + tail[:, cols] * dot(maps[...], s[...]))
    squares = sum(jnp.sum(g * g, axis=1, keepdims=True) for g in gated)
    factor = lax.rsqrt(squares / 512.0 + EPSILON)
    out = x[...].astype(F32)
    total = None
    for g, p in zip(gated, (p0, p1, p2, p3)):
        norm = small_rows(p)[1]
        piece = dot((g * factor * norm).astype(BF), p[256:384, :])
        total = piece if total is None else total + piece
    start = pl.multiple_of(i * BLK, BLK)
    hidden[0, pl.ds(start, BLK), :] = rounded(out[:, 0:128] + total[:, 0:128])
    hidden[1, pl.ds(start, BLK), :] = rounded(out[:, 128:256] + total[:, 128:256])

    @pl.when(i == pl.num_programs(0) - 1)
    def _():
        total = None
        for odd in range(2):
            for half in range(2):
                rows = hidden[half, pl.ds(odd, 512, stride=2), :].reshape(8, 2, 32, 128)
                for line in range(2):
                    tile = rows[:, line].reshape(256, 128).astype(BF)
                    at = (2 * line + odd) * 256 + half * 128
                    piece = dot(tile, merge[at : at + 128, :])
                    total = piece if total is None else total + piece
        result = total.astype(BF)
        merged[...] = result
        end_rows[...] = result[240:256]


def fine_close(leads, tails, maps, x, states, packs, merge):
    def halves(width):
        return [
            pl.BlockSpec((BLK, width), lambda i: (jnp.minimum(i, 1), 0)),
            pl.BlockSpec((BLK, width), lambda i: (jnp.maximum(i - 2, 0), 0)),
        ]

    return pl.pallas_call(
        fine_close_kernel,
        grid=(4,),
        in_specs=halves(512)
        + halves(512)
        + halves(256)
        + [pl.BlockSpec((BLK, 256), lambda i: (i, 0))]
        + [VM] * 9,
        out_specs=[VM] * 2,
        scratch_shapes=[
            pltpu.VMEM((BLK, 512), F32),
            pltpu.VMEM((BLK, 512), F32),
            pltpu.VMEM((BLK, 256), BF),
            pltpu.VMEM((2, 1024, 128), F32),
        ],
        out_shape=[sds((256, 1024), BF), sds((16, 1024), BF)],
        compiler_params=few(16),
        name="fine_close",
    )(*leads, *tails, *maps, x, *states, *packs, merge)


def coarse_main_kernel(
    near, qa, qb, ra, rb, gain, wg, wv, ws, wst, taps, both, *refs
):
    if near:
        lead, tail_out, maps_out, share, run, run_log, ends = refs[:7]
    else:
        near_ends, near_run, near_log, lead, tail_out, maps_out, share, run, run_log, message = (
            refs[:10]
        )
    xs, sems, cv, act, sc = refs[-5:]
    i = pl.program_id(0)
    y, c = lax.axis_index("y"), lax.axis_index("c")
    h = 2 * y + c

    @pl.when(i == 0)
    def _():
        copies = run_copies(((qa, xs.at[c]), (qb, xs.at[1 - c])), sems)
        rim = ra[...].astype(F32) + rb[...].astype(F32)
        if not near:
            rim = jnp.where(y == 0, near_ends[...].astype(F32), rim)
        begin(rms(rim, gain[...]), wv, ws, cv, run, run_log)
        for copy in copies:
            copy.wait()
        if near:
            ends[...] = xs[1, 240:256, :]

    share[...] = xs[i, :, pl.ds(pl.multiple_of(h * 256, 256), 256)]
    scan_block(
        rms(xs[i], gain[...]), wg, wv, ws, wst[...], taps, both[0:8, 0:1], both[8:16, 0:1],
        lead, tail_out, maps_out, cv, act, sc, run, run_log,
    )

    if not near:

        @pl.when(i == 1)
        def _():
            first_log = jnp.where(y == 0, near_log[:, 0:1], run_log[:, 0:1])
            second_log = jnp.where(y == 0, run_log[:, 0:1], near_log[:, 0:1])
            extra = decay_rows(spread_row(first_log + second_log))
            row = jnp.exp(spread_row(second_log))
            for n in range(16):
                for half in range(2):
                    cols = slice(half * 256, (half + 1) * 256)
                    mine = run[n * 16 : (n + 1) * 16, cols]
                    other = near_run[n * 16 : (n + 1) * 16, cols]
                    total = jnp.where(
                        y == 0, other * row[:, cols] + mine, mine * row[:, cols] + other
                    )
                    message[2 * n + half, 0:16, :] = total.astype(BF)
                    message[2 * n + half, 16:32, :] = extra[:, cols]


def spread_row(column):
    return jnp.sum(
        jnp.where(head_sel(512), jnp.broadcast_to(column, (8, 512)), 0.0), axis=0, keepdims=True
    )


ANY = pl.BlockSpec(memory_space=pl.ANY)


def coarse_main(near, pieces, rims, weights, params, extra):
    taps, both, gain, wst, _ = params
    rows = [pl.BlockSpec((BLK, n), lambda i: (i, 0)) for n in (512, 512, 256, 256)]
    last = sds((16, 1024), BF) if near else sds((32, 32, 256), BF)
    return pl.pallas_call(
        lambda *refs: coarse_main_kernel(near, *refs),
        grid=(2,),
        in_specs=[ANY] * 2 + [VM] * (9 + len(extra)),
        out_specs=rows + [VM] * 3,
        out_shape=[
            sds((512, 512)),
            sds((512, 512)),
            sds((512, 256), BF),
            sds((512, 256), BF),
            sds((256, 512)),
            sds((8, 128)),
            last,
        ],
        scratch_shapes=[pltpu.VMEM((2, 256, 1024), BF), pltpu.SemaphoreType.DMA((2,))]
        + SCAN_SCRATCH[:3],
        compiler_params=few(16),
        name="coarse_main_near" if near else "coarse_main_far",
    )(*pieces, *rims, gain, *weights, wst, taps, both, *extra)


def prefix_kernel(got, out):
    state = jnp.zeros((16, 256), F32)
    for d in range(32):
        out[d] = state.astype(BF)
        state = state * jnp.exp(of_rows(got[d, 16:32, :])) + got[d, 0:16, :].astype(F32)


def prefix(got):
    return pl.pallas_call(
        prefix_kernel,
        in_specs=[VM],
        out_specs=VM,
        out_shape=sds((32, 16, 256), BF),
        compiler_params=few(4),
        name="prefix",
    )(got)


def coarse_close_kernel(
    near, lead, tail, maps, got, other_run, other_log, norm, wo, kk, ks, sk, ss, square_sums,
    state, sums,
):
    i = pl.program_id(0)
    y = lax.axis_index("y")
    h = 2 * y + lax.axis_index("c")

    @pl.when(i == 0)
    def _():
        row = jnp.exp(spread_row(other_log[:, 0:1]))
        later = (y == 1) if near else (y == 0)
        for n in range(16):
            for half in range(2):
                cols = slice(half * 256, (half + 1) * 256)
                came = got[2 * n + half].astype(F32)
                other = other_run[n * 16 : (n + 1) * 16, cols]
                came = jnp.where(later, came * row[:, cols] + other, came)
                state[n * 16 : (n + 1) * 16, cols] = came.astype(BF)

    gated = lead[...] + tail[...] * dot(maps[...], state[...])
    sq = gated * gated
    hi = sq.astype(BF)
    low = (sq - hi.astype(F32)).astype(BF)
    ones = jnp.ones((8, 512), BF)
    sums[i] = dot(ones, hi, NT) + dot(ones, low, NT)
    scaled = (gated * norm[...]).astype(BF)
    rows = pl.ds(pl.multiple_of(i * BLK, BLK), BLK)
    for k, out in enumerate((kk, sk, ks, ss)):
        at = pl.multiple_of((h ^ k) * 256, 256)
        out[rows, :] = dot(scaled, wo[:, pl.ds(at, 256)]).astype(BF)

    @pl.when(i == 1)
    def _():
        square_sums[...] = jnp.concatenate([sums[0], sums[1]], 1)
        ss[512:528, :] = sum_rows(sums[0, 0:1], sums[1, 0:1])


def sum_rows(a, b):
    return jnp.concatenate(three(a) + three(b) + [jnp.zeros((10, 256), F32)], 0).astype(BF)


def rows_sum(ref):
    rows = ref[512:528, :].astype(F32)
    return jnp.concatenate([of_rows(rows[0:3]), of_rows(rows[3:6])], 1)


def coarse_close(near, lead, tail, maps, got, other, norm, wo):
    rows = [pl.BlockSpec((BLK, n), lambda i: (i, 0)) for n in (512, 512, 256)]
    return pl.pallas_call(
        lambda *refs: coarse_close_kernel(near, *refs),
        grid=(2,),
        in_specs=rows + [VM] * 5,
        out_specs=[VM] * 5,
        out_shape=[sds((512, 256), BF)] * 3 + [sds((528, 256), BF), sds((8, 512))],
        scratch_shapes=[pltpu.VMEM((256, 512), BF), pltpu.VMEM((2, 8, 256), F32)],
        compiler_params=few(12),
        name="coarse_close_near" if near else "coarse_close_far",
    )(lead, tail, maps, got, *other, norm, wo)


def relay_kernel(ks, square_sums, came, out, sums):
    out[0:512, :] = (ks[...].astype(F32) + came[0:512, :].astype(F32)).astype(BF)
    total = square_sums[0:1, :] + rows_sum(came)
    out[512:528, :] = sum_rows(total[:, 0:256], total[:, 256:512])
    sums[...] = jnp.broadcast_to(total, (8, 512))


def relay(ks, square_sums, came):
    return pl.pallas_call(
        relay_kernel,
        in_specs=[VM] * 3,
        out_specs=[VM] * 2,
        out_shape=[sds((528, 256), BF), sds((8, 512))],
        compiler_params=few(4),
    )(ks, square_sums, came)


def final_kernel(sa, ka, ca, sum_a, far_a, sb, kb, cb, sum_b, far_b, out):
    y = lax.axis_index("y")
    pick = jnp.where(iota((32, 256), 0) % 8 == 0, 1.0, 0.0).astype(BF)
    sides = (y, sa, ka, ca, sum_a, far_a), (1 - y, sb, kb, cb, sum_b, far_b)
    for half, share, kk, sk, sums, far in sides:
        total = sums[...] + rows_sum(far)
        factor = lax.rsqrt(total / 2048.0 + EPSILON)
        for b in range(2):
            rows = slice(b * BLK, (b + 1) * BLK)
            spread = dot(parts(factor[:, rows]), pick, TN)
            total = kk[rows].astype(F32) + sk[rows].astype(F32) + far[rows].astype(F32)
            at = pl.multiple_of(half * 512 + b * BLK, BLK)
            out[pl.ds(at, BLK), :] = (share[rows].astype(F32) + total * spread).astype(BF)


def final(near, far):
    return pl.pallas_call(
        final_kernel,
        in_specs=[VM] * 10,
        out_specs=VM,
        out_shape=sds((1024, 256), BF),
        compiler_params=few(8),
        name="final",
    )(*near, *far)


def passed(x, axes, pairs):
    return lax.ppermute(x, axes, pairs)


def swapped(x, mask):
    return passed(x, HEAD, [(j, j ^ mask) for j in range(4)])


def round_of(x, axis):
    got = []
    for k in (1, 2, 3):
        got.append(passed(x, axis, [(j, (j + k) % 4) for j in range(4)]))
    return got


def shards(
    tokens, fine_gain, fine_gate, fine_value, fine_scans, fine_steps, fine_kernel, fine_taps,
    fine_bias, fine_decay, fine_norm, fine_output, merge_weight, coarse_gain, coarse_gate,
    coarse_value, coarse_scans, coarse_steps, coarse_kernel, coarse_taps, coarse_bias,
    coarse_decay, coarse_norm, coarse_output,
):
    pack, ends = packed(
        fine_bias, fine_decay, fine_gate, fine_value, fine_output, fine_steps.T, fine_kernel,
        fine_norm[None], tokens,
    )
    rim = passed(ends, SEQ, [(i, i + 1) for i in range(31)])
    packs = [pack] + [swapped(pack, m) for m in (1, 2, 3)]
    later, later_total, resident, (l0, t0, own, own_total, message) = fine_states(
        tokens, rim, fine_gain[None], pack, fine_scans, fine_taps
    )
    mine, mine_rim, gain, scans, ks = resident
    got = round_of(message, "x")
    first = fine_main(mine, gain, scans, ks, packs, (rim, mine_rim, t0), False)
    *prior, own, own_total, message = middle_stage("x", 4, own, own_total, (), got)
    got = [passed(message, "u", [(0, 1), (1, 0)])]
    params = coarse_params(
        coarse_bias, coarse_decay, coarse_kernel, coarse_taps, coarse_gain[None],
        coarse_steps.T, coarse_norm[None],
    )
    *prior, own, own_total, message = middle_stage("u", 2, own, own_total, prior, got)
    got = round_of(message, "z")
    second = fine_main(mine, gain, scans, ks, packs, first[3:], True)
    subs = last_stage(own, own_total, prior, got, l0, t0, later, later_total)
    states = [subs[0]] + [swapped(subs[m], m) for m in (1, 2, 3)]
    merged, end_rows = fine_close(
        (first[0], second[0]), (first[1], second[1]), (first[2], second[2]), mine, states, packs,
        merge_weight,
    )

    def rims(pairs):
        return passed(end_rows, ALL, pairs)

    rim_a = rims([(q, q + 1) for q in range(1, 127, 2)])
    rim_b = rims([(q, q + 2) for q in range(1, 126, 2)])
    rim_c = rims([(q, q + 3) for q in range(3, 125, 4)])
    rim_d = rims([(q, q + 4) for q in range(3, 124, 4)])
    across = swapped(merged, 2)
    beside = swapped(merged, 1)
    both = swapped(across, 1)
    weights = (coarse_gate, coarse_value, coarse_scans)
    near = coarse_main(True, (merged, beside), (rim_a, rim_b), weights, params, ())
    lead, tail, maps, share, run, run_log, near_ends = near
    far = coarse_main(
        False, (across, both), (rim_c, rim_d), weights, params, (near_ends, run, run_log)
    )
    lead_f, tail_f, maps_f, share_f, run_f, run_log_f, message = far
    got = lax.all_to_all(message, SEQ, split_axis=0, concat_axis=0, tiled=True)
    got = lax.all_to_all(prefix(got), SEQ, split_axis=0, concat_axis=0, tiled=True)
    norm = params[4]
    kk, ks, sk, ss, sums = coarse_close(
        True, lead, tail, maps, got, (run_f, run_log_f), norm, coarse_output
    )
    kk_f, ks_f, sk_f, ss_f, sums_f = coarse_close(
        False, lead_f, tail_f, maps_f, got, (run, run_log), norm, coarse_output
    )
    went, sums = relay(ks, sums, swapped(ss, 1))
    went = swapped(went, 2)
    went_f, sums_f = relay(ks_f, sums_f, swapped(ss_f, 1))
    went_f = swapped(went_f, 2)
    sk = swapped(sk, 1)
    sk_f = swapped(sk_f, 1)
    return final((share, kk, sk, sums, went_f), (share_f, kk_f, sk_f, sums_f, went))


def solution(mesh):
    finer = Mesh(mesh.devices.reshape(4, 2, 4, 2, 2), ALL)
    cols = P(None, HEAD)
    return jax.shard_map(
        shards,
        mesh=finer,
        in_specs=(
            P(SEQ, None), P(), cols, cols, P(), cols, cols, P(), P(HEAD), P(HEAD), P(HEAD),
            P(HEAD, None), P(), P(), cols, cols, P(), cols, cols, P(), P(HEAD), P(HEAD), P(HEAD),
            P(HEAD, None),
        ),
        out_specs=P(SEQ, HEAD),
        check_vma=False,
    )
```

```python
import jax
import jax.numpy as jnp
from jax import lax
from jax.experimental import pallas as pl
from jax.experimental.pallas import tpu as pltpu
from jax.sharding import Mesh
from jax.sharding import PartitionSpec as P


SEQ = ("z", "u", "x")
HEAD = ("y", "c")
ALL = ("z", "u", "x", "y", "c")
EPSILON = 1e-05
BLK = 256
BF = jnp.bfloat16
F32 = jnp.float32
NN = (((1,), (0,)), ((), ()))
NT = (((1,), (1,)), ((), ()))
TN = (((0,), (0,)), ((), ()))


def dot(a, b, dims=NN):
    return lax.dot_general(a, b, dims, preferred_element_type=F32)


def parts(x):
    hi = x.astype(BF).astype(F32)
    rest = x - hi
    mid = rest.astype(BF).astype(F32)
    low = rest - mid
    return jnp.concatenate([hi, mid, low, jnp.zeros_like(x)], 0).astype(BF)


def decay_rows(row):
    hi = row.astype(BF).astype(F32)
    rest = row - hi
    mid = rest.astype(BF).astype(F32)
    low = rest - mid
    return jnp.concatenate([hi, mid, low, jnp.zeros((13, row.shape[1]), F32)], 0).astype(BF)


def of_rows(rows):
    rows = rows.astype(F32)
    return rows[0:1] + rows[1:2] + rows[2:3]


def iota(shape, dim):
    return lax.broadcasted_iota(jnp.int32, shape, dim)


def head_sel(width):
    return iota((8, width), 0) == iota((8, width), 1) // 64


def expander(width):
    r, lane = iota((32, width), 0), iota((32, width), 1)
    return jnp.where((r < 24) & (r % 8 == lane // 64), 1.0, 0.0).astype(BF)


def upper():
    return jnp.where(iota((BLK, BLK), 0) <= iota((BLK, BLK), 1), 1.0, 0.0).astype(BF)


def silu(v):
    h = v * 0.5
    return h + h * jnp.tanh(h)


def softplus(v):
    return jnp.maximum(v, 0.0) + jnp.log1p(jnp.exp(-jnp.abs(v)))


def rms(x, gain):
    x = x.astype(F32)
    return (x * lax.rsqrt(jnp.mean(x * x, axis=-1, keepdims=True) + EPSILON) * gain).astype(BF)


def cumulate(logs, tri):
    s = dot(parts(logs), tri)
    return s[0:8] + s[8:16] + s[16:24]


def spaced(length):
    return length // 8 + 1


def convolve(cv, act, half_taps, length):
    apart = spaced(length)

    def slab(c, carry):
        taps = half_taps[c]
        rows = [cv[c, pl.ds(13 + i, 8, stride=apart), :] for i in range(3)]
        for i in range(apart):
            rows.append(cv[c, pl.ds(16 + i, 8, stride=apart), :])
            h = rows[i] * taps[0:1]
            for k in range(1, 4):
                h = h + rows[i + k] * taps[k : k + 1]
            act[c, pl.ds(i, 8, stride=apart), :] = h + h * jnp.tanh(h)
        return carry

    lax.fori_loop(0, cv.shape[0], slab, 0)


def project(rows, weights, cv, start, slab):
    product = dot(rows, weights)
    for j in range(product.shape[1] // 128):
        cv[slab + j, start : start + rows.shape[0], :] = product[:, j * 128 : (j + 1) * 128]


def rounded(x):
    return x.astype(BF).astype(F32)


def small_rows(pack):
    rows = pack[384:416, :].astype(F32)
    kv = rows[0:4, 0:128] + rows[4:8, 0:128] + rows[8:12, 0:128]
    right = rows[0:16, 128:256]
    norm, b0, b1, d0, d1 = (of_rows(right[3 * j : 3 * j + 3]) for j in range(5))
    return kv, norm, jnp.concatenate([b0, b1], 0), jnp.concatenate([d0, d1], 0), rows[16:18]


def three(row):
    hi = row.astype(BF).astype(F32)
    rest = row - hi
    mid = rest.astype(BF).astype(F32)
    return [hi, mid, rest - mid]


def run_copies(pairs, sems):
    copies = [pltpu.make_async_copy(a, b, sems.at[j]) for j, (a, b) in enumerate(pairs)]
    for copy in copies:
        copy.start()
    return copies


def pack_kernel(
    bias, decay, gate, value, output, steps, kv, norm, tokens, pack, ends, kv_v, norm_v, steps_v, sems
):
    copies = run_copies(
        (
            (kv, kv_v),
            (norm, norm_v),
            (steps, steps_v),
            (tokens.at[4080:4096], ends),
            (gate, pack.at[0:256, 0:128]),
            (value, pack.at[0:256, 128:256]),
            (output, pack.at[256:384]),
        ),
        sems,
    )
    for copy in copies[:3]:
        copy.wait()
    left = jnp.concatenate(three(kv_v[...]) + [jnp.zeros((4, 128), F32)], 0)
    rows = three(norm_v[...])
    for ref in (bias, decay):
        for j in range(2):
            rows = rows + three(jnp.full((1, 128), ref[j], F32))
    right = jnp.concatenate(rows + [jnp.zeros((1, 128), F32)], 0)
    below = jnp.concatenate([steps_v[...].astype(F32), jnp.zeros((14, 256), F32)], 0)
    pack[384:416, :] = jnp.concatenate([jnp.concatenate([left, right], 1), below], 0).astype(BF)
    for copy in copies[3:]:
        copy.wait()


def packed(bias, decay, gate, value, output, steps, kv, norm, tokens):
    return pl.pallas_call(
        pack_kernel,
        in_specs=[SMEM] * 2 + [HBM] * 7,
        out_specs=[VM] * 2,
        out_shape=[sds((416, 256), BF), sds((16, 256), BF)],
        scratch_shapes=[
            pltpu.VMEM((4, 128), F32),
            pltpu.VMEM((1, 128), F32),
            pltpu.VMEM((2, 256), BF),
            pltpu.SemaphoreType.DMA((7,)),
        ],
        compiler_params=few(4),
        name="pack",
    )(bias, decay, *in_hbm(gate, value, output, steps, kv, norm, tokens))


def params_kernel(bias, decay, kv, ks, gain, steps, norm, taps, both, *refs):
    outs, kv_v, ks_v, sems = refs[:3], *refs[3:]
    copies = run_copies(
        ((kv, kv_v), (ks, ks_v), (gain, outs[0]), (steps, outs[1]), (norm, outs[2])), sems
    )
    for copy in copies:
        copy.wait()
    for j in range(4):
        cols = slice(j * 128, (j + 1) * 128)
        taps[j] = kv_v[:, cols] * 0.5
        taps[4 + j] = ks_v[:, cols] * 0.5
    rows = [jnp.full((1, 128), ref[j], F32) for ref in (bias, decay) for j in range(8)]
    both[...] = jnp.concatenate(rows, 0)


def coarse_params(bias, decay, kv, ks, gain, steps, norm):
    return pl.pallas_call(
        params_kernel,
        in_specs=[SMEM] * 2 + [HBM] * 5,
        out_specs=[VM] * 5,
        out_shape=[
            sds((8, 4, 128)), sds((16, 128)), sds((1, 1024)), sds((8, 1024), BF), sds((1, 512)),
        ],
        scratch_shapes=[
            pltpu.VMEM((4, 512), F32),
            pltpu.VMEM((4, 512), F32),
            pltpu.SemaphoreType.DMA((5,)),
        ],
        compiler_params=few(4),
        name="coarse_params",
    )(bias, decay, *in_hbm(kv, ks, gain, steps, norm))


def state_chunk(x, rim, gain, pack, scans, ks, taps, cv, act):
    kv, _, bias, decay, steps = small_rows(pack)
    pad = jnp.zeros((6, 128), F32)
    bias = jnp.concatenate([bias, pad], 0)[:, 0:1]
    decay = jnp.concatenate([decay, pad], 0)[:, 0:1]
    steps = jnp.concatenate([steps, jnp.zeros((6, 256), F32)], 0).astype(BF)
    wv, wb = pack[0:256, 128:256], scans[:, 0:256]
    taps[0] = kv * 0.5
    taps[1] = ks[:, 0:128] * 0.5
    taps[2] = ks[:, 128:256] * 0.5
    normed = rms(x, gain[...])
    before = rms(rim, gain[...])
    project(before, wv, cv, 0, 0)
    project(before, wb, cv, 0, 1)
    project(normed, wv, cv, 16, 0)
    project(normed, wb, cv, 16, 1)
    convolve(cv, act, taps, 1024)
    raw = dot(steps, normed, NT)
    dt = softplus(raw + bias)
    logs = -dt * decay
    tri = upper()
    carry = jnp.zeros((8, 1), F32)
    pieces = []
    for b in range(4):
        piece = cumulate(logs[:, b * BLK : (b + 1) * BLK], tri) + carry
        carry = piece[:, BLK - 1 : BLK]
        pieces.append(piece)
    cum = jnp.concatenate(pieces, 1)
    tail = jnp.exp(carry - cum) * dt
    spread = dot(parts(tail), expander(128), TN)
    scaled = (act[0, 0:1024] * spread).astype(BF)
    local = dot(jnp.concatenate([act[1, 0:1024].astype(BF), act[2, 0:1024].astype(BF)], 1), scaled, TN)
    total = jnp.sum(
        jnp.where(head_sel(128), jnp.broadcast_to(carry, (8, 128)), 0.0), axis=0, keepdims=True
    )
    return local, total


def later_chunks_kernel(
    tokens, gain_h, pack, scans_h, ks_h,
    local, total, x0, mine, mine_rim, gain, scans, ks, xs, taps, cv, act, sems, x_sems,
):
    i = pl.program_id(0)
    start = pl.multiple_of(lax.axis_index(HEAD) * 1024, 1024)
    early = pl.multiple_of(jnp.maximum(start - 16, 0), 16)
    mine_pairs = (
        (tokens.at[0:1024], x0),
        (tokens.at[pl.ds(start, 1024)], mine),
        (tokens.at[pl.ds(early, 16)], mine_rim),
    )

    def chunk(j):
        begin_row = pl.multiple_of((j + 1) * 1024 - 16, 16)
        return pltpu.make_async_copy(tokens.at[pl.ds(begin_row, 1040)], xs.at[j], x_sems.at[j])

    @pl.when(i == 0)
    def _():
        chunk(0).start()
        copies = run_copies(((gain_h, gain), (scans_h, scans), (ks_h, ks)), sems)
        chunk(1).start()
        chunk(2).start()
        for j, (a, b) in enumerate(mine_pairs):
            pltpu.make_async_copy(a, b, sems.at[3 + j]).start()
        for copy in copies:
            copy.wait()

    chunk(i).wait()
    state, logs = state_chunk(xs[i, 16:1040], xs[i, 0:16], gain, pack, scans, ks, taps, cv, act)
    local[i] = state
    total[i] = jnp.broadcast_to(logs, (8, 128))

    @pl.when(i == 2)
    def _():
        for j, (a, b) in enumerate(mine_pairs):
            pltpu.make_async_copy(a, b, sems.at[3 + j]).wait()


def first_chunk_kernel(
    x, rim, gain, pack, scans, ks, later, later_total,
    local, total, whole, whole_total, message, taps, cv, act,
):
    state, logs = state_chunk(x[...], rim[...], gain, pack, scans, ks, taps, cv, act)
    local[...] = state
    total[...] = jnp.broadcast_to(logs, (8, 128))
    for j in range(3):
        piece = later_total[j, 0:1, :]
        state = state * jnp.exp(piece) + later[j]
        logs = logs + piece
    whole[...] = state
    whole_total[...] = jnp.broadcast_to(logs, (8, 128))
    message[0:256, :] = state.astype(BF)
    message[256:272, :] = decay_rows(logs)


def sds(shape, dtype=F32):
    return jax.ShapeDtypeStruct(shape, dtype)


def in_hbm(*arrays):
    return [pltpu.with_memory_space_constraint(a, pltpu.HBM) for a in arrays]


def few(mib):
    return pltpu.CompilerParams(vmem_limit_bytes=mib << 20)


SMEM = pl.BlockSpec(memory_space=pltpu.SMEM)
VM = pl.BlockSpec(memory_space=pltpu.VMEM)
HBM = pl.BlockSpec(memory_space=pltpu.HBM)


def fine_states(tokens, ends_from, gain, pack, scans, ks):
    scratch = [
        pltpu.VMEM((3, 4, 128), F32),
        pltpu.VMEM((3, 1048, 128), F32),
        pltpu.VMEM((3, 1032, 128), F32),
    ]
    later, later_total, x0, *resident = pl.pallas_call(
        later_chunks_kernel,
        grid=(3,),
        in_specs=[HBM, HBM, VM, HBM, HBM],
        out_specs=[VM] * 8,
        out_shape=[
            sds((3, 256, 128)),
            sds((3, 8, 128)),
            sds((1024, 256), BF),
            sds((1024, 256), BF),
            sds((16, 256), BF),
            sds((1, 256)),
            sds((256, 512), BF),
            sds((4, 512)),
        ],
        scratch_shapes=[pltpu.VMEM((3, 1040, 256), BF)]
        + scratch
        + [pltpu.SemaphoreType.DMA((6,)), pltpu.SemaphoreType.DMA((3,))],
        compiler_params=few(16),
        name="later_chunks",
    )(*in_hbm(tokens, gain), pack, *in_hbm(scans, ks))
    _, _, gain, scans, ks = resident
    first = pl.pallas_call(
        first_chunk_kernel,
        in_specs=[VM] * 8,
        out_specs=[VM] * 5,
        out_shape=[
            sds((256, 128)),
            sds((8, 128)),
            sds((256, 128)),
            sds((8, 128)),
            sds((272, 128), BF),
        ],
        scratch_shapes=scratch,
        compiler_params=few(16),
        name="first_chunk",
    )(x0, ends_from, gain, pack, scans, ks, later, later_total)
    return later, later_total, resident, first


def combine(i, count, own, own_total, prior, prior_total, received):
    state = jnp.zeros_like(own)
    logs = jnp.zeros_like(own_total)
    zero = jnp.zeros((), F32)
    got = [(r[0:256, :].astype(F32), of_rows(r[256:272, :])) for r in received]
    for k in range(count - 1, 0, -1):
        s, l = got[k - 1]
        valid = i >= k
        state = jnp.where(valid, state * jnp.exp(l) + s, state)
        logs = jnp.where(valid, logs + l, logs)
    new_prior = state * jnp.exp(prior_total) + prior
    new_prior_total = logs + prior_total
    state = state * jnp.exp(own_total) + own
    logs = logs + own_total
    for m in range(1, count):
        s, l = got[count - m - 1]
        valid = i + m < count
        state = jnp.where(valid, state * jnp.exp(l) + s, state)
        logs = jnp.where(valid, logs + l, logs)
    return new_prior, new_prior_total, state, logs


def middle_kernel(axis, count, fresh, own, own_total, *refs):
    if fresh:
        prior, prior_total = jnp.zeros((256, 128), F32), jnp.zeros((1, 128), F32)
    else:
        prior, prior_total, refs = refs[0][...], refs[1][0:1, :], refs[2:]
    received, (np_ref, npt_ref, ns_ref, nst_ref, message) = refs[: count - 1], refs[count - 1 :]
    p, pt, s, st = combine(
        lax.axis_index(axis), count, own[...], own_total[0:1, :], prior, prior_total, received
    )
    np_ref[...] = p
    npt_ref[...] = jnp.broadcast_to(pt, (8, 128))
    ns_ref[...] = s
    nst_ref[...] = jnp.broadcast_to(st, (8, 128))
    message[0:256, :] = s.astype(BF)
    message[256:272, :] = decay_rows(st)


def middle_stage(axis, count, own, own_total, prior, received):
    return pl.pallas_call(
        lambda *refs: middle_kernel(axis, count, not prior, *refs),
        in_specs=[VM] * (2 + len(prior) + len(received)),
        out_specs=[VM] * 5,
        out_shape=[
            sds((256, 128)),
            sds((8, 128)),
            sds((256, 128)),
            sds((8, 128)),
            sds((272, 128), BF),
        ],
        compiler_params=few(4),
    )(own, own_total, *prior, *received)


def last_kernel(own, own_total, prior, prior_total, r1, r2, r3, l0, t0, later, later_total,
                o0, o1, o2, o3, sub):
    p, _, _, _ = combine(
        lax.axis_index("z"), 4, own[...], own_total[0:1, :], prior[...], prior_total[0:1, :],
        (r1, r2, r3),
    )
    sub[0] = p
    p = p * jnp.exp(t0[0:1, :]) + l0[...]
    sub[1] = p
    for j in range(2):
        p = p * jnp.exp(later_total[j, 0:1, :]) + later[j]
        sub[j + 2] = p
    h = lax.axis_index(HEAD)
    for k, out in enumerate((o0, o1, o2, o3)):
        out[...] = sub[h ^ k].astype(BF)


def last_stage(own, own_total, prior, received, l0, t0, later, later_total):
    return pl.pallas_call(
        last_kernel,
        in_specs=[VM] * 11,
        out_specs=[VM] * 4,
        out_shape=[sds((256, 128), BF)] * 4,
        scratch_shapes=[pltpu.VMEM((4, 256, 128), F32)],
        compiler_params=few(6),
        name="chain_last",
    )(own, own_total, *prior, *received, l0, t0, later, later_total)


def begin(before, wv, ws, cv, run, run_log):
    project(before, wv[...], cv, 0, 0)
    project(before, ws[...], cv, 0, 4)
    run[...] = jnp.zeros_like(run)
    run_log[...] = jnp.zeros_like(run_log)


def scan_block(
    normed, wg, wv, ws, wst, taps, bias, decay,
    lead, tail_out, maps_out, cv, act, sc, spread, scaled, run, run_log,
):
    project(normed, wv[...], cv, 16, 0)
    project(normed, ws[...], cv, 16, 4)
    tail_out[...] = silu(dot(normed, wg[...]))
    convolve(cv, act, taps, BLK)
    cv[:, 0:16, :] = cv[:, 256:272, :]
    raw = dot(wst[...], normed, NT)
    dt = softplus(raw + bias[...])
    logs = -dt * decay[...]
    cum = cumulate(logs, upper())
    last = cum[:, BLK - 1 : BLK]
    before_log = run_log[:, 0:1]
    stacked = jnp.concatenate(
        [jnp.exp(cum), jnp.exp(cum + before_log), jnp.exp(last - cum) * dt], 1
    )
    spread[...] = dot(parts(stacked), expander(512), TN)
    run_log[...] = run_log[...] + last
    columns = dot(parts(cum), jnp.where(
        (iota((32, 128), 0) < 24) & (iota((32, 128), 0) % 8 == iota((32, 128), 1)), 1.0, 0.0
    ).astype(BF), TN)
    rows = cum - jnp.log(dt)
    in_map = jnp.concatenate([act[4, 0:BLK].astype(BF), act[5, 0:BLK].astype(BF)], 1)
    out_map = jnp.concatenate([act[6, 0:BLK].astype(BF), act[7, 0:BLK].astype(BF)], 1)
    maps_out[...] = out_map
    sc[...] = dot(out_map, in_map, NT)
    lead[...] = spread[0:256, :] * dot(out_map, run[...].astype(BF))
    low_tri = iota((128, 128), 0) >= iota((128, 128), 1)
    lane_low = iota((BLK, 128), 1) < 64
    for p in range(4):
        cols = slice(p * 128, (p + 1) * 128)
        vals = act[p, 0:BLK]
        v0 = jnp.where(lane_low, vals, 0.0).astype(BF)
        v1 = jnp.where(lane_low, 0.0, vals).astype(BF)
        upper_w, lower_w = [], []
        for h in (2 * p, 2 * p + 1):
            c0, c1 = columns[0:128, h : h + 1], columns[128:256, h : h + 1]
            r0, r1 = rows[h : h + 1, 0:128], rows[h : h + 1, 128:256]
            upper_w.append(
                (sc[0:128, 0:128] * jnp.exp(jnp.where(low_tri, c0 - r0, -jnp.inf))).astype(BF)
            )
            lower_w.append((sc[128:256, 0:128] * jnp.exp(c1 - r0)).astype(BF))
            lower_w.append(
                (sc[128:256, 128:256] * jnp.exp(jnp.where(low_tri, c1 - r1, -jnp.inf))).astype(BF)
            )
        top = dot(
            jnp.concatenate(upper_w, 1), jnp.concatenate([v0[0:128], v1[0:128]], 0)
        )
        bottom = dot(jnp.concatenate(lower_w, 1), jnp.concatenate([v0, v1], 0))
        gate = tail_out[:, cols]
        lead[0:128, cols] = (top + lead[0:128, cols]) * gate[0:128]
        lead[128:256, cols] = (bottom + lead[128:256, cols]) * gate[128:256]
        tail_out[:, cols] = spread[256:512, cols] * gate
        scaled[:, cols] = (vals * spread[512:768, cols]).astype(BF)
    run[...] = run[...] * spread[255:256, :] + dot(in_map, scaled[...], TN)


SCAN_SCRATCH = [
    pltpu.VMEM((8, 280, 128), F32),
    pltpu.VMEM((8, BLK + 8, 128), F32),
    pltpu.VMEM((BLK, BLK), F32),
    pltpu.VMEM((768, 512), F32),
    pltpu.VMEM((256, 512), BF),
]


def fine_main_kernel(later, x, gain, ws, ks, p0, p1, p2, p3, *refs):
    (
        x0, x1, x2, lead, tail_out, maps_out, run, run_log, cv_end,
        wg, wv, wst, taps, bias, decay, cv, act, sc, spread, scaled,
    ) = refs

    @pl.when(pl.program_id(0) == 0)
    def _():
        for j in range(4):
            taps[4 + j] = ks[:, j * 128 : (j + 1) * 128] * 0.5
        for j, p in enumerate((p0, p1, p2, p3)):
            cols = slice(j * 128, (j + 1) * 128)
            two = slice(2 * j, 2 * j + 2)
            wg[:, cols] = p[0:256, 0:128]
            wv[:, cols] = p[0:256, 128:256]
            kv, _, bias[two, :], decay[two, :], wst[two, :] = small_rows(p)
            taps[j] = kv * 0.5
        if later:
            run[...] = x0[...]
            run_log[...] = x1[...]
            cv[:, 0:16, :] = x2[...]
        else:
            rim = jnp.where(lax.axis_index(HEAD) == 0, x0[...].astype(F32), x1[...].astype(F32))
            begin(rms(rim, gain[...]), wv, ws, cv, run, run_log)

    scan_block(
        rms(x[...], gain[...]), wg, wv, ws, wst[...].astype(BF), taps, bias[:, 0:1], decay[:, 0:1],
        lead, tail_out, maps_out, cv, act, sc, spread, scaled, run, run_log,
    )
    cv_end[...] = cv[:, 0:16, :]


def fine_main(x, gain, scans, ks, packs, extra, later):
    at = 2 if later else 0
    rows = [pl.BlockSpec((BLK, n), lambda i: (i, 0)) for n in (512, 512, 256)]
    return pl.pallas_call(
        lambda *refs: fine_main_kernel(later, *refs),
        grid=(2,),
        in_specs=[pl.BlockSpec((BLK, 256), lambda i: (at + i, 0))] + [VM] * 10,
        out_specs=rows + [VM] * 3,
        out_shape=[
            sds((512, 512)), sds((512, 512)), sds((512, 256), BF),
            sds((256, 512)), sds((8, 128)), sds((8, 16, 128)),
        ],
        scratch_shapes=[
            pltpu.VMEM((256, 512), BF),
            pltpu.VMEM((256, 512), BF),
            pltpu.VMEM((8, 256), F32),
            pltpu.VMEM((8, 4, 128), F32),
            pltpu.VMEM((8, 128), F32),
            pltpu.VMEM((8, 128), F32),
        ]
        + SCAN_SCRATCH,
        compiler_params=few(16),
        name="fine_main_b" if later else "fine_main_a",
    )(x, gain, scans, ks, *packs, *extra)


def fine_close_kernel(
    lead_a, lead_b, tail_a, tail_b, maps_a, maps_b, x, s0, s1, s2, s3, p0, p1, p2, p3, merge,
    merged, end_rows, lead, tail, maps, hidden, state, wo, norm,
):
    i = pl.program_id(0)

    @pl.when(i < 2)
    def _():
        lead[...], tail[...], maps[...] = lead_a[...], tail_a[...], maps_a[...]

    @pl.when(i >= 2)
    def _():
        lead[...], tail[...], maps[...] = lead_b[...], tail_b[...], maps_b[...]

    @pl.when(i == 0)
    def _():
        for j, (s, p) in enumerate(zip((s0, s1, s2, s3), (p0, p1, p2, p3))):
            cols = slice(j * 128, (j + 1) * 128)
            state[:, cols] = s[...]
            wo[cols, :] = p[256:384, :]
            norm[:, cols] = small_rows(p)[1]

    gated = lead[...] + tail[...] * dot(maps[...], state[...])
    factor = lax.rsqrt(jnp.sum(gated * gated, axis=1, keepdims=True) / 512.0 + EPSILON)
    out = x[...].astype(F32)
    total = dot((gated * factor * norm[...]).astype(BF), wo[...])
    start = pl.multiple_of(i * BLK, BLK)
    hidden[0, pl.ds(start, BLK), :] = rounded(out[:, 0:128] + total[:, 0:128])
    hidden[1, pl.ds(start, BLK), :] = rounded(out[:, 128:256] + total[:, 128:256])

    @pl.when(i == pl.num_programs(0) - 1)
    def _():
        total = None
        for odd in range(2):
            rows = [
                hidden[half, pl.ds(odd, 512, stride=2), :].reshape(8, 2, 32, 128)
                for half in range(2)
            ]
            for line in range(2):
                tile = [r[:, line].reshape(256, 128).astype(BF) for r in rows]
                at = (2 * line + odd) * 256
                piece = dot(jnp.concatenate(tile, 1), merge[at : at + 256, :])
                total = piece if total is None else total + piece
        result = total.astype(BF)
        merged[...] = result
        end_rows[...] = result[240:256]


def fine_close(leads, tails, maps, x, states, packs, merge):
    def halves(width):
        return [
            pl.BlockSpec((BLK, width), lambda i: (jnp.minimum(i, 1), 0)),
            pl.BlockSpec((BLK, width), lambda i: (jnp.maximum(i - 2, 0), 0)),
        ]

    return pl.pallas_call(
        fine_close_kernel,
        grid=(4,),
        in_specs=halves(512)
        + halves(512)
        + halves(256)
        + [pl.BlockSpec((BLK, 256), lambda i: (i, 0))]
        + [VM] * 9,
        out_specs=[VM] * 2,
        scratch_shapes=[
            pltpu.VMEM((BLK, 512), F32),
            pltpu.VMEM((BLK, 512), F32),
            pltpu.VMEM((BLK, 256), BF),
            pltpu.VMEM((2, 1024, 128), F32),
            pltpu.VMEM((256, 512), BF),
            pltpu.VMEM((512, 256), BF),
            pltpu.VMEM((1, 512), F32),
        ],
        out_shape=[sds((256, 1024), BF), sds((16, 1024), BF)],
        compiler_params=few(16),
        name="fine_close",
    )(*leads, *tails, *maps, x, *states, *packs, merge)


def in_order(first, a, a_log, b, b_log):
    lead_log = jnp.where(first, b_log, a_log)
    row = jnp.exp(spread_row(lead_log))
    return jnp.where(first, a, b) * row + jnp.where(first, b, a), a_log + b_log


def coarse_main_kernel(kind, pieces, gain, wg, wv, ws, wst, taps, both, *refs):
    qs, refs = refs[:pieces], refs[pieces:]
    xs, sems, cv, act, sc, spread, scaled = refs[-7:]
    y, c = lax.axis_index("y"), lax.axis_index("c")
    h = 2 * y + c
    if kind == "near":
        ra, rb, lead, tail_out, maps_out, share, run, run_log, ends = refs[:-7]
    elif kind == "far_1":
        near_ends, re, lead, tail_out, maps_out, share, run, run_log, ends = refs[:-7]
    else:
        (
            near_ends, ends_1, rd, near_run, near_log, run_1, run_log_1,
            lead, tail_out, maps_out, share, run, run_log, far_run, far_log, message,
        ) = refs[:-7]
    i = pl.program_id(0)

    @pl.when(i == 0)
    def _():
        if kind == "near":
            copies = run_copies(((qs[0], xs.at[c]), (qs[1], xs.at[1 - c])), sems)
            rim = ra[...].astype(F32) + rb[...].astype(F32)
        else:
            copies = run_copies(((qs[0], xs.at[0]),), sems)
            rim = near_ends[...].astype(F32)
            if kind == "far_1":
                rim = jnp.where(h == 0, rim, re[...].astype(F32))
            else:
                rim = jnp.where(h == 1, rim, rd[...].astype(F32))
                rim = jnp.where(c == 0, ends_1[...].astype(F32), rim)
        begin(rms(rim, gain[...]), wv, ws, cv, run, run_log)
        for copy in copies:
            copy.wait()
        if kind != "far_2":
            ends[...] = xs[pieces - 1, 240:256, :]

    share[...] = xs[i, :, pl.ds(pl.multiple_of(h * 256, 256), 256)]
    scan_block(
        rms(xs[i], gain[...]), wg, wv, ws, wst[...], taps, both[0:8, 0:1], both[8:16, 0:1],
        lead, tail_out, maps_out, cv, act, sc, spread, scaled, run, run_log,
    )

    if kind == "far_2":
        log_1, log_2, log_n = run_log_1[:, 0:1], run_log[:, 0:1], near_log[:, 0:1]
        far, log_f = in_order(c == 0, run_1[...], log_1, run[...], log_2)
        far_run[...] = far
        far_log[...] = jnp.broadcast_to(log_f, (8, 128))
        total, log = in_order(y == 0, near_run[...], log_n, far, log_f)
        extra = decay_rows(spread_row(log))[0:8]
        for n in range(16):
            for half in range(2):
                cols = slice(half * 256, (half + 1) * 256)
                message[2 * n + half, 0:16, :] = total[n * 16 : (n + 1) * 16, cols].astype(BF)
                message[2 * n + half, 16:24, :] = extra[:, cols]


def spread_row(column):
    return jnp.sum(
        jnp.where(head_sel(512), jnp.broadcast_to(column, (8, 512)), 0.0), axis=0, keepdims=True
    )


ANY = pl.BlockSpec(memory_space=pl.ANY)


def coarse_main(kind, pieces, weights, params, extra):
    taps, both, gain, wst, _ = params
    blocks = len(pieces)
    length = blocks * BLK
    rows = [pl.BlockSpec((BLK, n), lambda i: (i, 0)) for n in (512, 512, 256, 256)]
    last = [sds((16, 1024), BF)]
    if kind == "far_2":
        last = [sds((256, 512)), sds((8, 128)), sds((32, 24, 256), BF)]
    return pl.pallas_call(
        lambda *refs: coarse_main_kernel(kind, blocks, *refs),
        grid=(blocks,),
        in_specs=[VM] * 7 + [ANY] * blocks + [VM] * len(extra),
        out_specs=rows + [VM] * (2 + len(last)),
        out_shape=[
            sds((length, 512)),
            sds((length, 512)),
            sds((length, 256), BF),
            sds((length, 256), BF),
            sds((256, 512)),
            sds((8, 128)),
        ]
        + last,
        scratch_shapes=[pltpu.VMEM((blocks, 256, 1024), BF), pltpu.SemaphoreType.DMA((blocks,))]
        + SCAN_SCRATCH,
        compiler_params=few(16),
    )(gain, *weights, wst, taps, both, *pieces, *extra)


def prefix_kernel(got, out):
    state = jnp.zeros((16, 256), F32)
    for d in range(32):
        out[d] = state.astype(BF)
        state = state * jnp.exp(of_rows(got[d, 16:24, :])) + got[d, 0:16, :].astype(F32)


def prefix(got):
    return pl.pallas_call(
        prefix_kernel,
        in_specs=[VM],
        out_specs=VM,
        out_shape=sds((32, 16, 256), BF),
        compiler_params=few(4),
        name="prefix",
    )(got)


def coarse_close_kernel(near, *refs):
    if near:
        lead, tail, maps, got, far_run, far_log, norm, wo, *refs = refs
    else:
        leads, tails, mapss = refs[0:2], refs[2:4], refs[4:6]
        got, near_run, near_log, run_1, log_1, run_2, log_2, norm, wo, *refs = refs[6:]
    gn, ks, ss, square_sums, states, sums = refs
    y, c = lax.axis_index("y"), lax.axis_index("c")
    h = 2 * y + c
    came = jnp.concatenate(
        [jnp.concatenate([got[2 * n], got[2 * n + 1]], 1) for n in range(16)], 0
    ).astype(F32)

    def after(state, cond, run, log):
        row = jnp.exp(spread_row(log[:, 0:1]))
        return jnp.where(cond, state * row + run[...], state)

    if near:
        states[0] = after(came, y == 1, far_run, far_log).astype(BF)
    else:
        came = after(came, y == 0, near_run, near_log)
        states[0] = after(came, c == 1, run_2, log_2).astype(BF)
        states[1] = after(came, c == 0, run_1, log_1).astype(BF)
    ones = jnp.ones((8, 512), BF)
    for i in range(2):
        if near:
            rows = slice(i * BLK, (i + 1) * BLK)
            gated = lead[rows] + tail[rows] * dot(maps[rows], states[0])
            place = i
        else:
            gated = leads[i][...] + tails[i][...] * dot(mapss[i][...], states[i])
            place = jnp.bitwise_xor(c, i)
        sq = gated * gated
        hi = sq.astype(BF)
        low = (sq - hi.astype(F32)).astype(BF)
        sums[place] = dot(ones, hi, NT) + dot(ones, low, NT)
        scaled = (gated * norm[...]).astype(BF)
        at = pl.ds(pl.multiple_of(place * BLK, BLK), BLK)
        gn[at, :] = scaled
        for k, out in ((2, ks), (3, ss)):
            col = pl.multiple_of((h ^ k) * 256, 256)
            out[at, :] = dot(scaled, wo[:, pl.ds(col, 256)]).astype(BF)
    square_sums[...] = jnp.concatenate([sums[0], sums[1]], 1)
    ss[512:528, :] = sum_rows(sums[0, 0:1], sums[1, 0:1])


def coarse_close(near, *args):
    return pl.pallas_call(
        lambda *refs: coarse_close_kernel(near, *refs),
        in_specs=[VM] * len(args),
        out_specs=[VM] * 4,
        out_shape=[
            sds((512, 512), BF), sds((512, 256), BF), sds((528, 256), BF), sds((8, 512)),
        ],
        scratch_shapes=[pltpu.VMEM((2, 256, 512), BF), pltpu.VMEM((2, 8, 256), F32)],
        compiler_params=few(12),
        name="coarse_close_near" if near else "coarse_close_far",
    )(*args)


def close_rest_kernel(near, far, wo, kk, sk):
    h = lax.axis_index(HEAD)
    for k, out in enumerate((kk, sk)):
        col = pl.multiple_of((h ^ k) * 256, 256)
        for j, ref in enumerate((near, far)):
            out[j * 512 : (j + 1) * 512, :] = dot(ref[...], wo[:, pl.ds(col, 256)]).astype(BF)


def close_rest(near, far, wo):
    return pl.pallas_call(
        close_rest_kernel,
        in_specs=[VM] * 3,
        out_specs=[VM] * 2,
        out_shape=[sds((1024, 256), BF)] * 2,
        compiler_params=few(8),
        name="close_rest",
    )(near, far, wo)


def sum_rows(a, b):
    return jnp.concatenate(three(a) + three(b) + [jnp.zeros((10, 256), F32)], 0).astype(BF)


def rows_sum(ref):
    rows = ref[512:528, :].astype(F32)
    return jnp.concatenate([of_rows(rows[0:3]), of_rows(rows[3:6])], 1)


def relay_kernel(ks, square_sums, came, out, sums):
    out[0:512, :] = (ks[...].astype(F32) + came[0:512, :].astype(F32)).astype(BF)
    total = square_sums[0:1, :] + rows_sum(came)
    out[512:528, :] = sum_rows(total[:, 0:256], total[:, 256:512])
    sums[...] = jnp.broadcast_to(total, (8, 512))


def relay(ks, square_sums, came):
    return pl.pallas_call(
        relay_kernel,
        in_specs=[VM] * 3,
        out_specs=[VM] * 2,
        out_shape=[sds((528, 256), BF), sds((8, 512))],
        compiler_params=few(4),
    )(ks, square_sums, came)


def final_kernel(share, share_1, share_2, kk, sk, sum_a, far_a, sum_b, far_b, out):
    y, c = lax.axis_index("y"), lax.axis_index("c")
    pick = jnp.where(iota((32, 256), 0) % 8 == 0, 1.0, 0.0).astype(BF)
    for side, (half, sums, far) in enumerate(((y, sum_a, far_a), (1 - y, sum_b, far_b))):
        total = sums[...] + rows_sum(far)
        factor = lax.rsqrt(total / 2048.0 + EPSILON)
        for b in range(2):
            rows = slice(b * BLK, (b + 1) * BLK)
            here = slice(side * 512 + b * BLK, side * 512 + (b + 1) * BLK)
            spread = dot(parts(factor[:, rows]), pick, TN)
            total = kk[here].astype(F32) + sk[here].astype(F32) + far[rows].astype(F32)
            if side == 0:
                own = share[rows].astype(F32)
            else:
                own = jnp.where(c == b, share_1[...].astype(F32), share_2[...].astype(F32))
            at = pl.multiple_of(half * 512 + b * BLK, BLK)
            out[pl.ds(at, BLK), :] = (own + total * spread).astype(BF)


def final(*args):
    return pl.pallas_call(
        final_kernel,
        in_specs=[VM] * 9,
        out_specs=VM,
        out_shape=sds((1024, 256), BF),
        compiler_params=few(8),
        name="final",
    )(*args)


def passed(x, axes, pairs):
    return lax.ppermute(x, axes, pairs)


def swapped(x, mask):
    return passed(x, HEAD, [(j, j ^ mask) for j in range(4)])


def round_of(x, axis):
    got = []
    for k in (1, 2, 3):
        got.append(passed(x, axis, [(j, (j + k) % 4) for j in range(4)]))
    return got


def shards(
    tokens, fine_gain, fine_gate, fine_value, fine_scans, fine_steps, fine_kernel, fine_taps,
    fine_bias, fine_decay, fine_norm, fine_output, merge_weight, coarse_gain, coarse_gate,
    coarse_value, coarse_scans, coarse_steps, coarse_kernel, coarse_taps, coarse_bias,
    coarse_decay, coarse_norm, coarse_output,
):
    pack, ends = packed(
        fine_bias, fine_decay, fine_gate, fine_value, fine_output, fine_steps.T, fine_kernel,
        fine_norm[None], tokens,
    )
    rim = passed(ends, SEQ, [(i, i + 1) for i in range(31)])
    packs = [pack] + [swapped(pack, m) for m in (1, 2, 3)]
    later, later_total, resident, (l0, t0, own, own_total, message) = fine_states(
        tokens, rim, fine_gain[None], pack, fine_scans, fine_taps
    )
    mine, mine_rim, gain, scans, ks = resident
    got = round_of(message, "x")
    first = fine_main(mine, gain, scans, ks, packs, (rim, mine_rim, t0), False)
    *prior, own, own_total, message = middle_stage("x", 4, own, own_total, (), got)
    got = [passed(message, "u", [(0, 1), (1, 0)])]
    params = coarse_params(
        coarse_bias, coarse_decay, coarse_kernel, coarse_taps, coarse_gain[None],
        coarse_steps.T, coarse_norm[None],
    )
    *prior, own, own_total, message = middle_stage("u", 2, own, own_total, prior, got)
    got = round_of(message, "z")
    second = fine_main(mine, gain, scans, ks, packs, first[3:], True)
    subs = last_stage(own, own_total, prior, got, l0, t0, later, later_total)
    states = [subs[0]] + [swapped(subs[m], m) for m in (1, 2, 3)]
    merged, end_rows = fine_close(
        (first[0], second[0]), (first[1], second[1]), (first[2], second[2]), mine, states, packs,
        merge_weight,
    )

    def rims(pairs):
        return passed(end_rows, ALL, pairs)

    rim_a = rims([(q, q + 1) for q in range(1, 127, 2)])
    rim_b = rims([(q, q + 2) for q in range(1, 126, 2)])
    rim_d = rims([(q, q + 4) for q in range(3, 124, 4)])
    rim_e = rims(
        [(q, q - 1) for q in range(2, 128, 4)]
        + [(q, q + 3) for q in range(0, 128, 4)]
        + [(q, q + 3) for q in range(3, 124, 4)],
    )
    across = swapped(merged, 2)
    beside = swapped(merged, 1)
    both = swapped(across, 1)
    weights = (coarse_gate, coarse_value, coarse_scans)
    lead, tail, maps, share, run, run_log, near_ends = coarse_main(
        "near", (merged, beside), weights, params, (rim_a, rim_b)
    )
    lead_1, tail_1, maps_1, share_1, run_1, run_log_1, ends_1 = coarse_main(
        "far_1", (across,), weights, params, (near_ends, rim_e)
    )
    lead_2, tail_2, maps_2, share_2, run_2, run_log_2, run_f, run_log_f, message = coarse_main(
        "far_2", (both,), weights, params,
        (near_ends, ends_1, rim_d, run, run_log, run_1, run_log_1),
    )
    got = lax.all_to_all(message, SEQ, split_axis=0, concat_axis=0, tiled=True)
    got = lax.all_to_all(prefix(got), SEQ, split_axis=0, concat_axis=0, tiled=True)
    norm = params[4]
    gn, ks, ss, sums = coarse_close(
        True, lead, tail, maps, got, run_f, run_log_f, norm, coarse_output
    )
    gn_f, ks_f, ss_f, sums_f = coarse_close(
        False, lead_1, lead_2, tail_1, tail_2, maps_1, maps_2, got, run, run_log,
        run_1, run_log_1, run_2, run_log_2, norm, coarse_output,
    )
    went, sums = relay(ks, sums, swapped(ss, 1))
    went = swapped(went, 2)
    went_f, sums_f = relay(ks_f, sums_f, swapped(ss_f, 1))
    went_f = swapped(went_f, 2)
    kk, sk = close_rest(gn, gn_f, coarse_output)
    sk = swapped(sk, 1)
    return final(share, share_1, share_2, kk, sk, sums, went_f, sums_f, went)


def solution(mesh):
    finer = Mesh(mesh.devices.reshape(4, 2, 4, 2, 2), ALL)
    cols = P(None, HEAD)
    return jax.shard_map(
        shards,
        mesh=finer,
        in_specs=(
            P(SEQ, None), P(), cols, cols, P(), cols, cols, P(), P(HEAD), P(HEAD), P(HEAD),
            P(HEAD, None), P(), P(), cols, cols, P(), cols, cols, P(), P(HEAD), P(HEAD), P(HEAD),
            P(HEAD, None),
        ),
        out_specs=P(SEQ, HEAD),
        check_vma=False,
    )
```

```python
import jax
import jax.numpy as jnp
from jax import lax
from jax.experimental import pallas as pl
from jax.experimental.pallas import tpu as pltpu
from jax.sharding import Mesh
from jax.sharding import PartitionSpec as P


SEQ = ("z", "u", "x")
HEAD = ("y", "c")
ALL = ("z", "u", "x", "y", "c")
EPSILON = 1e-05
BLK = 256
BF = jnp.bfloat16
F32 = jnp.float32
NN = (((1,), (0,)), ((), ()))
NT = (((1,), (1,)), ((), ()))
TN = (((0,), (0,)), ((), ()))


def dot(a, b, dims=NN):
    return lax.dot_general(a, b, dims, preferred_element_type=F32)


def parts(x):
    hi = x.astype(BF).astype(F32)
    rest = x - hi
    mid = rest.astype(BF).astype(F32)
    low = rest - mid
    return jnp.concatenate([hi, mid, low, jnp.zeros_like(x)], 0).astype(BF)


def decay_rows(row):
    hi = row.astype(BF).astype(F32)
    rest = row - hi
    mid = rest.astype(BF).astype(F32)
    low = rest - mid
    return jnp.concatenate([hi, mid, low, jnp.zeros((13, row.shape[1]), F32)], 0).astype(BF)


def of_rows(rows):
    rows = rows.astype(F32)
    return rows[0:1] + rows[1:2] + rows[2:3]


def iota(shape, dim):
    return lax.broadcasted_iota(jnp.int32, shape, dim)


def head_sel(width):
    return iota((8, width), 0) == iota((8, width), 1) // 64


def expander(width):
    r, lane = iota((32, width), 0), iota((32, width), 1)
    return jnp.where((r < 24) & (r % 8 == lane // 64), 1.0, 0.0).astype(BF)


def upper():
    return jnp.where(iota((BLK, BLK), 0) <= iota((BLK, BLK), 1), 1.0, 0.0).astype(BF)


def silu(v):
    h = v * 0.5
    return h + h * jnp.tanh(h)


def softplus(v):
    return jnp.maximum(v, 0.0) + jnp.log1p(jnp.exp(-jnp.abs(v)))


def rms(x, gain):
    x = x.astype(F32)
    return (x * lax.rsqrt(jnp.mean(x * x, axis=-1, keepdims=True) + EPSILON) * gain).astype(BF)


def cumulate(logs, tri):
    s = dot(parts(logs), tri)
    return s[0:8] + s[8:16] + s[16:24]


def spaced(length):
    return length // 8 + 1


def convolve(cv, act, half_taps, length):
    apart = spaced(length)

    def slab(c):
        taps = half_taps[c]
        rows = [cv[c, pl.ds(13 + i, 8, stride=apart), :] for i in range(3)]
        for i in range(apart):
            rows.append(cv[c, pl.ds(16 + i, 8, stride=apart), :])
            h = rows[i] * taps[0:1]
            for k in range(1, 4):
                h = h + rows[i + k] * taps[k : k + 1]
            act[c, pl.ds(i, 8, stride=apart), :] = h + h * jnp.tanh(h)

    for c in range(cv.shape[0]):
        slab(c)


def project(rows, weights, cv, start, slab):
    product = dot(rows, weights)
    for j in range(product.shape[1] // 128):
        cv[slab + j, start : start + rows.shape[0], :] = product[:, j * 128 : (j + 1) * 128]


def rounded(x):
    return x.astype(BF).astype(F32)


def small_rows(pack):
    rows = pack[384:416, :].astype(F32)
    kv = rows[0:4, 0:128] + rows[4:8, 0:128] + rows[8:12, 0:128]
    right = rows[0:16, 128:256]
    norm, b0, b1, d0, d1 = (of_rows(right[3 * j : 3 * j + 3]) for j in range(5))
    return kv, norm, jnp.concatenate([b0, b1], 0), jnp.concatenate([d0, d1], 0), rows[16:18]


def three(row):
    hi = row.astype(BF).astype(F32)
    rest = row - hi
    mid = rest.astype(BF).astype(F32)
    return [hi, mid, rest - mid]


def run_copies(pairs, sems):
    copies = [pltpu.make_async_copy(a, b, sems.at[j]) for j, (a, b) in enumerate(pairs)]
    for copy in copies:
        copy.start()
    return copies


def pack_kernel(
    bias, decay, gate, value, output, steps, kv, norm, tokens,
    pack, ends, kv_v, norm_v, steps_v, bias_v, decay_v, sems,
):
    copies = run_copies(
        (
            (kv, kv_v),
            (norm, norm_v),
            (steps, steps_v),
            (bias, bias_v),
            (decay, decay_v),
            (tokens.at[4080:4096], ends),
            (gate, pack.at[0:256, 0:128]),
            (value, pack.at[0:256, 128:256]),
            (output, pack.at[256:384]),
        ),
        sems,
    )
    for copy in copies[:5]:
        copy.wait()
    left = jnp.concatenate(three(kv_v[...]) + [jnp.zeros((4, 128), F32)], 0)
    rows = three(norm_v[...])
    for ref in (bias_v, decay_v):
        for j in range(2):
            rows = rows + three(jnp.broadcast_to(ref[:, j : j + 1], (1, 128)))
    right = jnp.concatenate(rows + [jnp.zeros((1, 128), F32)], 0)
    below = jnp.concatenate([steps_v[...].astype(F32), jnp.zeros((14, 256), F32)], 0)
    pack[384:416, :] = jnp.concatenate([jnp.concatenate([left, right], 1), below], 0).astype(BF)
    for copy in copies[5:]:
        copy.wait()


def packed(bias, decay, gate, value, output, steps, kv, norm, tokens):
    return pl.pallas_call(
        pack_kernel,
        in_specs=[HBM] * 9,
        out_specs=[VM] * 2,
        out_shape=[sds((416, 256), BF), sds((16, 256), BF)],
        scratch_shapes=[
            pltpu.VMEM((4, 128), F32),
            pltpu.VMEM((1, 128), F32),
            pltpu.VMEM((2, 256), BF),
            pltpu.VMEM((1, 2), F32),
            pltpu.VMEM((1, 2), F32),
            pltpu.SemaphoreType.DMA((9,)),
        ],
        compiler_params=few(4),
        name="pack",
    )(*in_hbm(bias, decay, gate, value, output, steps, kv, norm, tokens))


def params_kernel(bias, decay, kv, ks, gain, steps, norm, taps, both, *refs):
    outs, kv_v, ks_v, bias_v, decay_v, sems = refs[:3], *refs[3:]
    copies = run_copies(
        (
            (kv, kv_v), (ks, ks_v), (bias, bias_v), (decay, decay_v),
            (gain, outs[0]), (steps, outs[1]), (norm, outs[2]),
        ),
        sems,
    )
    for copy in copies:
        copy.wait()
    for j in range(4):
        cols = slice(j * 128, (j + 1) * 128)
        taps[j] = kv_v[:, cols] * 0.5
        taps[4 + j] = ks_v[:, cols] * 0.5
    rows = [
        jnp.broadcast_to(ref[:, j : j + 1], (1, 128)) for ref in (bias_v, decay_v) for j in range(8)
    ]
    both[...] = jnp.concatenate(rows, 0)


def coarse_params(bias, decay, kv, ks, gain, steps, norm):
    return pl.pallas_call(
        params_kernel,
        in_specs=[HBM] * 7,
        out_specs=[VM] * 5,
        out_shape=[
            sds((8, 4, 128)), sds((16, 128)), sds((1, 1024)), sds((8, 1024), BF), sds((1, 512)),
        ],
        scratch_shapes=[
            pltpu.VMEM((4, 512), F32),
            pltpu.VMEM((4, 512), F32),
            pltpu.VMEM((1, 8), F32),
            pltpu.VMEM((1, 8), F32),
            pltpu.SemaphoreType.DMA((7,)),
        ],
        compiler_params=few(4),
        name="coarse_params",
    )(*in_hbm(bias, decay, kv, ks, gain, steps, norm))


def state_chunk(x, rim, gain, pack, scans, ks, taps, cv, act):
    kv, _, bias, decay, steps = small_rows(pack)
    pad = jnp.zeros((6, 128), F32)
    bias = jnp.concatenate([bias, pad], 0)[:, 0:1]
    decay = jnp.concatenate([decay, pad], 0)[:, 0:1]
    steps = jnp.concatenate([steps, jnp.zeros((6, 256), F32)], 0).astype(BF)
    wv, wb = pack[0:256, 128:256], scans[:, 0:256]
    taps[0] = kv * 0.5
    taps[1] = ks[:, 0:128] * 0.5
    taps[2] = ks[:, 128:256] * 0.5
    normed = rms(x, gain[...])
    before = rms(rim, gain[...])
    project(before, wv, cv, 0, 0)
    project(before, wb, cv, 0, 1)
    project(normed, wv, cv, 16, 0)
    project(normed, wb, cv, 16, 1)
    convolve(cv, act, taps, 1024)
    raw = dot(steps, normed, NT)
    dt = softplus(raw + bias)
    logs = -dt * decay
    tri = upper()
    carry = jnp.zeros((8, 1), F32)
    pieces = []
    for b in range(4):
        piece = cumulate(logs[:, b * BLK : (b + 1) * BLK], tri) + carry
        carry = piece[:, BLK - 1 : BLK]
        pieces.append(piece)
    cum = jnp.concatenate(pieces, 1)
    tail = jnp.exp(carry - cum) * dt
    spread = dot(parts(tail), expander(128), TN)
    scaled = (act[0, 0:1024] * spread).astype(BF)
    local = dot(jnp.concatenate([act[1, 0:1024].astype(BF), act[2, 0:1024].astype(BF)], 1), scaled, TN)
    total = jnp.sum(
        jnp.where(head_sel(128), jnp.broadcast_to(carry, (8, 128)), 0.0), axis=0, keepdims=True
    )
    return local, total


def later_chunks_kernel(
    tokens, gain_h, pack, scans_h, ks_h,
    local, total, x0, mine, mine_rim, gain, scans, ks, xs, taps, cv, act, sems, x_sems,
):
    i = pl.program_id(0)
    start = pl.multiple_of(lax.axis_index(HEAD) * 1024, 1024)
    early = pl.multiple_of(jnp.maximum(start - 16, 0), 16)
    mine_pairs = (
        (tokens.at[0:1024], x0),
        (tokens.at[pl.ds(start, 1024)], mine),
        (tokens.at[pl.ds(early, 16)], mine_rim),
    )

    def chunk(j):
        begin_row = pl.multiple_of((j + 1) * 1024 - 16, 16)
        return pltpu.make_async_copy(tokens.at[pl.ds(begin_row, 1040)], xs.at[j], x_sems.at[j])

    @pl.when(i == 0)
    def _():
        chunk(0).start()
        copies = run_copies(((gain_h, gain), (scans_h, scans), (ks_h, ks)), sems)
        chunk(1).start()
        chunk(2).start()
        for j, (a, b) in enumerate(mine_pairs):
            pltpu.make_async_copy(a, b, sems.at[3 + j]).start()
        for copy in copies:
            copy.wait()

    chunk(i).wait()
    state, logs = state_chunk(xs[i, 16:1040], xs[i, 0:16], gain, pack, scans, ks, taps, cv, act)
    local[i] = state
    total[i] = jnp.broadcast_to(logs, (8, 128))

    @pl.when(i == 2)
    def _():
        for j, (a, b) in enumerate(mine_pairs):
            pltpu.make_async_copy(a, b, sems.at[3 + j]).wait()


def first_chunk_kernel(
    x, rim, gain, pack, scans, ks, later, later_total,
    local, total, whole, whole_total, message, taps, cv, act,
):
    state, logs = state_chunk(x[...], rim[...], gain, pack, scans, ks, taps, cv, act)
    local[...] = state
    total[...] = jnp.broadcast_to(logs, (8, 128))
    for j in range(3):
        piece = later_total[j, 0:1, :]
        state = state * jnp.exp(piece) + later[j]
        logs = logs + piece
    whole[...] = state
    whole_total[...] = jnp.broadcast_to(logs, (8, 128))
    message[0:256, :] = state.astype(BF)
    message[256:272, :] = decay_rows(logs)


def sds(shape, dtype=F32):
    return jax.ShapeDtypeStruct(shape, dtype)


def in_hbm(*arrays):
    return [pltpu.with_memory_space_constraint(a, pltpu.HBM) for a in arrays]


def few(mib):
    return pltpu.CompilerParams(vmem_limit_bytes=mib << 20)


VM = pl.BlockSpec(memory_space=pltpu.VMEM)
HBM = pl.BlockSpec(memory_space=pltpu.HBM)


def fine_states(tokens, ends_from, gain, pack, scans, ks):
    scratch = [
        pltpu.VMEM((3, 4, 128), F32),
        pltpu.VMEM((3, 1048, 128), F32),
        pltpu.VMEM((3, 1032, 128), F32),
    ]
    later, later_total, x0, *resident = pl.pallas_call(
        later_chunks_kernel,
        grid=(3,),
        in_specs=[HBM, HBM, VM, HBM, HBM],
        out_specs=[VM] * 8,
        out_shape=[
            sds((3, 256, 128)),
            sds((3, 8, 128)),
            sds((1024, 256), BF),
            sds((1024, 256), BF),
            sds((16, 256), BF),
            sds((1, 256)),
            sds((256, 512), BF),
            sds((4, 512)),
        ],
        scratch_shapes=[pltpu.VMEM((3, 1040, 256), BF)]
        + scratch
        + [pltpu.SemaphoreType.DMA((6,)), pltpu.SemaphoreType.DMA((3,))],
        compiler_params=few(16),
        name="later_chunks",
    )(*in_hbm(tokens, gain), pack, *in_hbm(scans, ks))
    _, _, gain, scans, ks = resident
    first = pl.pallas_call(
        first_chunk_kernel,
        in_specs=[VM] * 8,
        out_specs=[VM] * 5,
        out_shape=[
            sds((256, 128)),
            sds((8, 128)),
            sds((256, 128)),
            sds((8, 128)),
            sds((272, 128), BF),
        ],
        scratch_shapes=scratch,
        compiler_params=few(16),
        name="first_chunk",
    )(x0, ends_from, gain, pack, scans, ks, later, later_total)
    return later, later_total, resident, first


def combine(i, count, own, own_total, prior, prior_total, received):
    state = jnp.zeros_like(own)
    logs = jnp.zeros_like(own_total)
    zero = jnp.zeros((), F32)
    got = [(r[0:256, :].astype(F32), of_rows(r[256:272, :])) for r in received]
    for k in range(count - 1, 0, -1):
        s, l = got[k - 1]
        valid = i >= k
        state = jnp.where(valid, state * jnp.exp(l) + s, state)
        logs = jnp.where(valid, logs + l, logs)
    new_prior = state * jnp.exp(prior_total) + prior
    new_prior_total = logs + prior_total
    state = state * jnp.exp(own_total) + own
    logs = logs + own_total
    for m in range(1, count):
        s, l = got[count - m - 1]
        valid = i + m < count
        state = jnp.where(valid, state * jnp.exp(l) + s, state)
        logs = jnp.where(valid, logs + l, logs)
    return new_prior, new_prior_total, state, logs


def middle_kernel(axis, count, fresh, own, own_total, *refs):
    if fresh:
        prior, prior_total = jnp.zeros((256, 128), F32), jnp.zeros((1, 128), F32)
    else:
        prior, prior_total, refs = refs[0][...], refs[1][0:1, :], refs[2:]
    received, (np_ref, npt_ref, ns_ref, nst_ref, message) = refs[: count - 1], refs[count - 1 :]
    p, pt, s, st = combine(
        lax.axis_index(axis), count, own[...], own_total[0:1, :], prior, prior_total, received
    )
    np_ref[...] = p
    npt_ref[...] = jnp.broadcast_to(pt, (8, 128))
    ns_ref[...] = s
    nst_ref[...] = jnp.broadcast_to(st, (8, 128))
    message[0:256, :] = s.astype(BF)
    message[256:272, :] = decay_rows(st)


def middle_stage(axis, count, own, own_total, prior, received):
    return pl.pallas_call(
        lambda *refs: middle_kernel(axis, count, not prior, *refs),
        in_specs=[VM] * (2 + len(prior) + len(received)),
        out_specs=[VM] * 5,
        out_shape=[
            sds((256, 128)),
            sds((8, 128)),
            sds((256, 128)),
            sds((8, 128)),
            sds((272, 128), BF),
        ],
        compiler_params=few(4),
    )(own, own_total, *prior, *received)


def last_kernel(own, own_total, prior, prior_total, r1, r2, r3, l0, t0, later, later_total,
                o0, o1, o2, o3, sub):
    p, _, _, _ = combine(
        lax.axis_index("z"), 4, own[...], own_total[0:1, :], prior[...], prior_total[0:1, :],
        (r1, r2, r3),
    )
    sub[0] = p
    p = p * jnp.exp(t0[0:1, :]) + l0[...]
    sub[1] = p
    for j in range(2):
        p = p * jnp.exp(later_total[j, 0:1, :]) + later[j]
        sub[j + 2] = p
    h = lax.axis_index(HEAD)
    for k, out in enumerate((o0, o1, o2, o3)):
        out[...] = sub[h ^ k].astype(BF)


def last_stage(own, own_total, prior, received, l0, t0, later, later_total):
    return pl.pallas_call(
        last_kernel,
        in_specs=[VM] * 11,
        out_specs=[VM] * 4,
        out_shape=[sds((256, 128), BF)] * 4,
        scratch_shapes=[pltpu.VMEM((4, 256, 128), F32)],
        compiler_params=few(6),
        name="chain_last",
    )(own, own_total, *prior, *received, l0, t0, later, later_total)


def begin(before, wv, ws, cv, run, run_log):
    project(before, wv[...], cv, 0, 0)
    project(before, ws[...], cv, 0, 4)
    run[...] = jnp.zeros_like(run)
    run_log[...] = jnp.zeros_like(run_log)


def scan_block(
    normed, wg, wv, ws, wst, taps, bias, decay,
    lead, tail_out, maps_out, cv, act, sc, spread, scaled, run, run_log,
):
    project(normed, wv[...], cv, 16, 0)
    project(normed, ws[...], cv, 16, 4)
    tail_out[...] = silu(dot(normed, wg[...]))
    convolve(cv, act, taps, BLK)
    cv[:, 0:16, :] = cv[:, 256:272, :]
    raw = dot(wst[...], normed, NT)
    dt = softplus(raw + bias[...])
    logs = -dt * decay[...]
    cum = cumulate(logs, upper())
    last = cum[:, BLK - 1 : BLK]
    before_log = run_log[:, 0:1]
    stacked = jnp.concatenate(
        [jnp.exp(cum), jnp.exp(cum + before_log), jnp.exp(last - cum) * dt], 1
    )
    spread[...] = dot(parts(stacked), expander(512), TN)
    run_log[...] = run_log[...] + last
    columns = dot(parts(cum), jnp.where(
        (iota((32, 128), 0) < 24) & (iota((32, 128), 0) % 8 == iota((32, 128), 1)), 1.0, 0.0
    ).astype(BF), TN)
    rows = cum - jnp.log(dt)
    in_map = jnp.concatenate([act[4, 0:BLK].astype(BF), act[5, 0:BLK].astype(BF)], 1)
    out_map = jnp.concatenate([act[6, 0:BLK].astype(BF), act[7, 0:BLK].astype(BF)], 1)
    maps_out[...] = out_map
    sc[...] = dot(out_map, in_map, NT)
    lead[...] = spread[0:256, :] * dot(out_map, run[...].astype(BF))
    low_tri = iota((128, 128), 0) >= iota((128, 128), 1)
    lane_low = iota((BLK, 128), 1) < 64
    for p in range(4):
        cols = slice(p * 128, (p + 1) * 128)
        vals = act[p, 0:BLK]
        v0 = jnp.where(lane_low, vals, 0.0).astype(BF)
        v1 = jnp.where(lane_low, 0.0, vals).astype(BF)
        upper_w, lower_w = [], []
        for h in (2 * p, 2 * p + 1):
            c0, c1 = columns[0:128, h : h + 1], columns[128:256, h : h + 1]
            r0, r1 = rows[h : h + 1, 0:128], rows[h : h + 1, 128:256]
            upper_w.append(
                (sc[0:128, 0:128] * jnp.exp(jnp.where(low_tri, c0 - r0, -jnp.inf))).astype(BF)
            )
            lower_w.append((sc[128:256, 0:128] * jnp.exp(c1 - r0)).astype(BF))
            lower_w.append(
                (sc[128:256, 128:256] * jnp.exp(jnp.where(low_tri, c1 - r1, -jnp.inf))).astype(BF)
            )
        top = dot(
            jnp.concatenate(upper_w, 1), jnp.concatenate([v0[0:128], v1[0:128]], 0)
        )
        bottom = dot(jnp.concatenate(lower_w, 1), jnp.concatenate([v0, v1], 0))
        gate = tail_out[:, cols]
        lead[0:128, cols] = (top + lead[0:128, cols]) * gate[0:128]
        lead[128:256, cols] = (bottom + lead[128:256, cols]) * gate[128:256]
        tail_out[:, cols] = spread[256:512, cols] * gate
        scaled[:, cols] = (vals * spread[512:768, cols]).astype(BF)
    run[...] = run[...] * spread[255:256, :] + dot(in_map, scaled[...], TN)


SCAN_SCRATCH = [
    pltpu.VMEM((8, 280, 128), F32),
    pltpu.VMEM((8, BLK + 8, 128), F32),
    pltpu.VMEM((BLK, BLK), F32),
    pltpu.VMEM((768, 512), F32),
    pltpu.VMEM((256, 512), BF),
]


def fine_main_kernel(later, x, gain, ws, ks, p0, p1, p2, p3, *refs):
    (
        x0, x1, x2, lead, tail_out, maps_out, run, run_log, cv_end,
        wg, wv, wst, taps, bias, decay, cv, act, sc, spread, scaled,
    ) = refs

    @pl.when(pl.program_id(0) == 0)
    def _():
        for j in range(4):
            taps[4 + j] = ks[:, j * 128 : (j + 1) * 128] * 0.5
        for j, p in enumerate((p0, p1, p2, p3)):
            cols = slice(j * 128, (j + 1) * 128)
            two = slice(2 * j, 2 * j + 2)
            wg[:, cols] = p[0:256, 0:128]
            wv[:, cols] = p[0:256, 128:256]
            kv, _, bias[two, :], decay[two, :], wst[two, :] = small_rows(p)
            taps[j] = kv * 0.5
        if later:
            run[...] = x0[...]
            run_log[...] = x1[...]
            cv[:, 0:16, :] = x2[...]
        else:
            rim = jnp.where(lax.axis_index(HEAD) == 0, x0[...].astype(F32), x1[...].astype(F32))
            begin(rms(rim, gain[...]), wv, ws, cv, run, run_log)

    scan_block(
        rms(x[...], gain[...]), wg, wv, ws, wst[...].astype(BF), taps, bias[:, 0:1], decay[:, 0:1],
        lead, tail_out, maps_out, cv, act, sc, spread, scaled, run, run_log,
    )
    cv_end[...] = cv[:, 0:16, :]


def fine_main(x, gain, scans, ks, packs, extra, later):
    at = 2 if later else 0
    rows = [pl.BlockSpec((BLK, n), lambda i: (i, 0)) for n in (512, 512, 256)]
    return pl.pallas_call(
        lambda *refs: fine_main_kernel(later, *refs),
        grid=(2,),
        in_specs=[pl.BlockSpec((BLK, 256), lambda i: (at + i, 0))] + [VM] * 10,
        out_specs=rows + [VM] * 3,
        out_shape=[
            sds((512, 512)), sds((512, 512)), sds((512, 256), BF),
            sds((256, 512)), sds((8, 128)), sds((8, 16, 128)),
        ],
        scratch_shapes=[
            pltpu.VMEM((256, 512), BF),
            pltpu.VMEM((256, 512), BF),
            pltpu.VMEM((8, 256), F32),
            pltpu.VMEM((8, 4, 128), F32),
            pltpu.VMEM((8, 128), F32),
            pltpu.VMEM((8, 128), F32),
        ]
        + SCAN_SCRATCH,
        compiler_params=few(16),
        name="fine_main_b" if later else "fine_main_a",
    )(x, gain, scans, ks, *packs, *extra)


def fine_close_kernel(
    lead_a, lead_b, tail_a, tail_b, maps_a, maps_b, x, s0, s1, s2, s3, p0, p1, p2, p3, merge,
    merged, end_rows, lead, tail, maps, hidden, state, wo, norm,
):
    i = pl.program_id(0)

    @pl.when(i < 2)
    def _():
        lead[...], tail[...], maps[...] = lead_a[...], tail_a[...], maps_a[...]

    @pl.when(i >= 2)
    def _():
        lead[...], tail[...], maps[...] = lead_b[...], tail_b[...], maps_b[...]

    @pl.when(i == 0)
    def _():
        for j, (s, p) in enumerate(zip((s0, s1, s2, s3), (p0, p1, p2, p3))):
            cols = slice(j * 128, (j + 1) * 128)
            state[:, cols] = s[...]
            wo[cols, :] = p[256:384, :]
            norm[:, cols] = small_rows(p)[1]

    gated = lead[...] + tail[...] * dot(maps[...], state[...])
    factor = lax.rsqrt(jnp.sum(gated * gated, axis=1, keepdims=True) / 512.0 + EPSILON)
    out = x[...].astype(F32)
    total = dot((gated * factor * norm[...]).astype(BF), wo[...])
    start = pl.multiple_of(i * BLK, BLK)
    hidden[0, pl.ds(start, BLK), :] = rounded(out[:, 0:128] + total[:, 0:128])
    hidden[1, pl.ds(start, BLK), :] = rounded(out[:, 128:256] + total[:, 128:256])

    @pl.when(i == pl.num_programs(0) - 1)
    def _():
        total = None
        for odd in range(2):
            rows = [
                hidden[half, pl.ds(odd, 512, stride=2), :].reshape(8, 2, 32, 128)
                for half in range(2)
            ]
            for line in range(2):
                tile = [r[:, line].reshape(256, 128).astype(BF) for r in rows]
                at = (2 * line + odd) * 256
                piece = dot(jnp.concatenate(tile, 1), merge[at : at + 256, :])
                total = piece if total is None else total + piece
        result = total.astype(BF)
        merged[...] = result
        end_rows[...] = result[240:256]


def fine_close(leads, tails, maps, x, states, packs, merge):
    def halves(width):
        return [
            pl.BlockSpec((BLK, width), lambda i: (jnp.minimum(i, 1), 0)),
            pl.BlockSpec((BLK, width), lambda i: (jnp.maximum(i - 2, 0), 0)),
        ]

    return pl.pallas_call(
        fine_close_kernel,
        grid=(4,),
        in_specs=halves(512)
        + halves(512)
        + halves(256)
        + [pl.BlockSpec((BLK, 256), lambda i: (i, 0))]
        + [VM] * 9,
        out_specs=[VM] * 2,
        scratch_shapes=[
            pltpu.VMEM((BLK, 512), F32),
            pltpu.VMEM((BLK, 512), F32),
            pltpu.VMEM((BLK, 256), BF),
            pltpu.VMEM((2, 1024, 128), F32),
            pltpu.VMEM((256, 512), BF),
            pltpu.VMEM((512, 256), BF),
            pltpu.VMEM((1, 512), F32),
        ],
        out_shape=[sds((256, 1024), BF), sds((16, 1024), BF)],
        compiler_params=few(16),
        name="fine_close",
    )(*leads, *tails, *maps, x, *states, *packs, merge)


def in_order(first, a, a_log, b, b_log):
    lead_log = jnp.where(first, b_log, a_log)
    row = jnp.exp(spread_row(lead_log))
    return jnp.where(first, a, b) * row + jnp.where(first, b, a), a_log + b_log


def coarse_main_kernel(kind, pieces, gain, wg, wv, ws, wst, taps, both, *refs):
    qs, refs = refs[:pieces], refs[pieces:]
    xs, sems, cv, act, sc, spread, scaled = refs[-7:]
    y, c = lax.axis_index("y"), lax.axis_index("c")
    h = 2 * y + c
    if kind == "near":
        ra, rb, lead, tail_out, maps_out, share, run, run_log, ends = refs[:-7]
    elif kind == "far_1":
        near_ends, re, lead, tail_out, maps_out, share, run, run_log, ends = refs[:-7]
    else:
        (
            near_ends, ends_1, rd, near_run, near_log, run_1, run_log_1,
            lead, tail_out, maps_out, share, run, run_log, far_run, far_log, message,
        ) = refs[:-7]
    i = pl.program_id(0)

    @pl.when(i == 0)
    def _():
        if kind == "near":
            copies = run_copies(((qs[0], xs.at[c]), (qs[1], xs.at[1 - c])), sems)
            rim = jnp.where(c == 0, ra[...].astype(F32), rb[...].astype(F32))
        else:
            copies = run_copies(((qs[0], xs.at[0]),), sems)
            rim = near_ends[...].astype(F32)
            if kind == "far_1":
                rim = jnp.where(h == 0, rim, re[...].astype(F32))
            else:
                rim = jnp.where(h == 1, rim, rd[...].astype(F32))
                rim = jnp.where(c == 0, ends_1[...].astype(F32), rim)
        begin(rms(rim, gain[...]), wv, ws, cv, run, run_log)
        for copy in copies:
            copy.wait()
        if kind != "far_2":
            ends[...] = xs[pieces - 1, 240:256, :]

    share[...] = xs[i, :, pl.ds(pl.multiple_of(h * 256, 256), 256)]
    scan_block(
        rms(xs[i], gain[...]), wg, wv, ws, wst[...], taps, both[0:8, 0:1], both[8:16, 0:1],
        lead, tail_out, maps_out, cv, act, sc, spread, scaled, run, run_log,
    )

    if kind == "far_2":
        log_1, log_2, log_n = run_log_1[:, 0:1], run_log[:, 0:1], near_log[:, 0:1]
        far, log_f = in_order(c == 0, run_1[...], log_1, run[...], log_2)
        far_run[...] = far
        far_log[...] = jnp.broadcast_to(log_f, (8, 128))
        total, log = in_order(y == 0, near_run[...], log_n, far, log_f)
        extra = decay_rows(spread_row(log))[0:8]
        for n in range(16):
            for half in range(2):
                cols = slice(half * 256, (half + 1) * 256)
                message[2 * n + half, 0:16, :] = total[n * 16 : (n + 1) * 16, cols].astype(BF)
                message[2 * n + half, 16:24, :] = extra[:, cols]


def spread_row(column):
    return jnp.sum(
        jnp.where(head_sel(512), jnp.broadcast_to(column, (8, 512)), 0.0), axis=0, keepdims=True
    )


ANY = pl.BlockSpec(memory_space=pl.ANY)


def coarse_main(kind, pieces, weights, params, extra):
    taps, both, gain, wst, _ = params
    blocks = len(pieces)
    length = blocks * BLK
    rows = [pl.BlockSpec((BLK, n), lambda i: (i, 0)) for n in (512, 512, 256, 256)]
    last = [sds((16, 1024), BF)]
    if kind == "far_2":
        last = [sds((256, 512)), sds((8, 128)), sds((32, 24, 256), BF)]
    return pl.pallas_call(
        lambda *refs: coarse_main_kernel(kind, blocks, *refs),
        grid=(blocks,),
        in_specs=[VM] * 7 + [ANY] * blocks + [VM] * len(extra),
        out_specs=rows + [VM] * (2 + len(last)),
        out_shape=[
            sds((length, 512)),
            sds((length, 512)),
            sds((length, 256), BF),
            sds((length, 256), BF),
            sds((256, 512)),
            sds((8, 128)),
        ]
        + last,
        scratch_shapes=[pltpu.VMEM((blocks, 256, 1024), BF), pltpu.SemaphoreType.DMA((blocks,))]
        + SCAN_SCRATCH,
        compiler_params=few(16),
    )(gain, *weights, wst, taps, both, *pieces, *extra)


def prefix_kernel(got, out):
    state = jnp.zeros((16, 256), F32)
    for d in range(32):
        out[d] = state.astype(BF)
        state = state * jnp.exp(of_rows(got[d, 16:24, :])) + got[d, 0:16, :].astype(F32)


def prefix(got):
    return pl.pallas_call(
        prefix_kernel,
        in_specs=[VM],
        out_specs=VM,
        out_shape=sds((32, 16, 256), BF),
        compiler_params=few(4),
        name="prefix",
    )(got)


def coarse_close_kernel(near, *refs):
    if near:
        lead, tail, maps, got, far_run, far_log, norm, wo, *refs = refs
    else:
        leads, tails, mapss = refs[0:2], refs[2:4], refs[4:6]
        got, near_run, near_log, run_1, log_1, run_2, log_2, norm, wo, *refs = refs[6:]
    gn, ks, ss, square_sums, states, sums = refs
    y, c = lax.axis_index("y"), lax.axis_index("c")
    h = 2 * y + c
    came = jnp.concatenate(
        [jnp.concatenate([got[2 * n], got[2 * n + 1]], 1) for n in range(16)], 0
    ).astype(F32)

    def after(state, cond, run, log):
        row = jnp.exp(spread_row(log[:, 0:1]))
        return jnp.where(cond, state * row + run[...], state)

    if near:
        states[0] = after(came, y == 1, far_run, far_log).astype(BF)
    else:
        came = after(came, y == 0, near_run, near_log)
        states[0] = after(came, c == 1, run_2, log_2).astype(BF)
        states[1] = after(came, c == 0, run_1, log_1).astype(BF)
    ones = jnp.ones((8, 512), BF)
    for i in range(2):
        if near:
            rows = slice(i * BLK, (i + 1) * BLK)
            gated = lead[rows] + tail[rows] * dot(maps[rows], states[0])
            place = i
        else:
            gated = leads[i][...] + tails[i][...] * dot(mapss[i][...], states[i])
            place = jnp.bitwise_xor(c, i)
        sq = gated * gated
        hi = sq.astype(BF)
        low = (sq - hi.astype(F32)).astype(BF)
        sums[place] = dot(ones, hi, NT) + dot(ones, low, NT)
        scaled = (gated * norm[...]).astype(BF)
        at = pl.ds(pl.multiple_of(place * BLK, BLK), BLK)
        gn[at, :] = scaled
        for k, out in ((2, ks), (3, ss)):
            col = pl.multiple_of((h ^ k) * 256, 256)
            out[at, :] = dot(scaled, wo[:, pl.ds(col, 256)]).astype(BF)
    square_sums[...] = jnp.concatenate([sums[0], sums[1]], 1)
    ss[512:528, :] = sum_rows(sums[0, 0:1], sums[1, 0:1])


def coarse_close(near, *args):
    return pl.pallas_call(
        lambda *refs: coarse_close_kernel(near, *refs),
        in_specs=[VM] * len(args),
        out_specs=[VM] * 4,
        out_shape=[
            sds((512, 512), BF), sds((512, 256), BF), sds((528, 256), BF), sds((8, 512)),
        ],
        scratch_shapes=[pltpu.VMEM((2, 256, 512), BF), pltpu.VMEM((2, 8, 256), F32)],
        compiler_params=few(12),
        name="coarse_close_near" if near else "coarse_close_far",
    )(*args)


def close_rest_kernel(near, far, wo, kk, sk):
    h = lax.axis_index(HEAD)
    for k, out in enumerate((kk, sk)):
        col = pl.multiple_of((h ^ k) * 256, 256)
        for j, ref in enumerate((near, far)):
            out[j * 512 : (j + 1) * 512, :] = dot(ref[...], wo[:, pl.ds(col, 256)]).astype(BF)


def close_rest(near, far, wo):
    return pl.pallas_call(
        close_rest_kernel,
        in_specs=[VM] * 3,
        out_specs=[VM] * 2,
        out_shape=[sds((1024, 256), BF)] * 2,
        compiler_params=few(8),
        name="close_rest",
    )(near, far, wo)


def sum_rows(a, b):
    return jnp.concatenate(three(a) + three(b) + [jnp.zeros((10, 256), F32)], 0).astype(BF)


def rows_sum(ref):
    rows = ref[512:528, :].astype(F32)
    return jnp.concatenate([of_rows(rows[0:3]), of_rows(rows[3:6])], 1)


def relay_kernel(ks, square_sums, came, out, sums):
    out[0:512, :] = (ks[...].astype(F32) + came[0:512, :].astype(F32)).astype(BF)
    total = square_sums[0:1, :] + rows_sum(came)
    out[512:528, :] = sum_rows(total[:, 0:256], total[:, 256:512])
    sums[...] = jnp.broadcast_to(total, (8, 512))


def relay(ks, square_sums, came):
    return pl.pallas_call(
        relay_kernel,
        in_specs=[VM] * 3,
        out_specs=[VM] * 2,
        out_shape=[sds((528, 256), BF), sds((8, 512))],
        compiler_params=few(4),
    )(ks, square_sums, came)


def final_kernel(share, share_1, share_2, kk, sk, sum_a, far_a, sum_b, far_b, out):
    y, c = lax.axis_index("y"), lax.axis_index("c")
    pick = jnp.where(iota((32, 256), 0) % 8 == 0, 1.0, 0.0).astype(BF)
    for side, (half, sums, far) in enumerate(((y, sum_a, far_a), (1 - y, sum_b, far_b))):
        total = sums[...] + rows_sum(far)
        factor = lax.rsqrt(total / 2048.0 + EPSILON)
        for b in range(2):
            rows = slice(b * BLK, (b + 1) * BLK)
            here = slice(side * 512 + b * BLK, side * 512 + (b + 1) * BLK)
            spread = dot(parts(factor[:, rows]), pick, TN)
            total = kk[here].astype(F32) + sk[here].astype(F32) + far[rows].astype(F32)
            if side == 0:
                own = share[rows].astype(F32)
            else:
                own = jnp.where(c == b, share_1[...].astype(F32), share_2[...].astype(F32))
            at = pl.multiple_of(half * 512 + b * BLK, BLK)
            out[pl.ds(at, BLK), :] = (own + total * spread).astype(BF)


def final(*args):
    return pl.pallas_call(
        final_kernel,
        in_specs=[VM] * 9,
        out_specs=VM,
        out_shape=sds((1024, 256), BF),
        compiler_params=few(8),
        name="final",
    )(*args)


def passed(x, axes, pairs):
    return lax.ppermute(x, axes, pairs)


def swapped(x, mask):
    return passed(x, HEAD, [(j, j ^ mask) for j in range(4)])


def round_of(x, axis):
    got = []
    for k in (1, 2, 3):
        got.append(passed(x, axis, [(j, (j + k) % 4) for j in range(4)]))
    return got


def shards(
    tokens, fine_gain, fine_gate, fine_value, fine_scans, fine_steps, fine_kernel, fine_taps,
    fine_bias, fine_decay, fine_norm, fine_output, merge_weight, coarse_gain, coarse_gate,
    coarse_value, coarse_scans, coarse_steps, coarse_kernel, coarse_taps, coarse_bias,
    coarse_decay, coarse_norm, coarse_output,
):
    pack, ends = packed(
        fine_bias[None], fine_decay[None], fine_gate, fine_value, fine_output, fine_steps.T, fine_kernel,
        fine_norm[None], tokens,
    )
    rim = passed(ends, SEQ, [(i, i + 1) for i in range(31)])
    packs = [pack] + [swapped(pack, m) for m in (1, 2, 3)]
    later, later_total, resident, (l0, t0, own, own_total, message) = fine_states(
        tokens, rim, fine_gain[None], pack, fine_scans, fine_taps
    )
    mine, mine_rim, gain, scans, ks = resident
    got = round_of(message, "x")
    first = fine_main(mine, gain, scans, ks, packs, (rim, mine_rim, t0), False)
    *prior, own, own_total, message = middle_stage("x", 4, own, own_total, (), got)
    got = [passed(message, "u", [(0, 1), (1, 0)])]
    params = coarse_params(
        coarse_bias[None], coarse_decay[None], coarse_kernel, coarse_taps, coarse_gain[None],
        coarse_steps.T, coarse_norm[None],
    )
    *prior, own, own_total, message = middle_stage("u", 2, own, own_total, prior, got)
    got = round_of(message, "z")
    second = fine_main(mine, gain, scans, ks, packs, first[3:], True)
    subs = last_stage(own, own_total, prior, got, l0, t0, later, later_total)
    states = [subs[0]] + [swapped(subs[m], m) for m in (1, 2, 3)]
    merged, end_rows = fine_close(
        (first[0], second[0]), (first[1], second[1]), (first[2], second[2]), mine, states, packs,
        merge_weight,
    )

    def rims(pairs):
        return passed(end_rows, ALL, pairs)

    rim_a = rims([(q, q + 1) for q in range(1, 127, 2)])
    rim_b = swapped(rim_a, 1)
    rim_d = rims([(q, q + 4) for q in range(3, 124, 4)])
    rim_e = rims(
        [(q, q - 1) for q in range(2, 128, 4)]
        + [(q, q + 3) for q in range(0, 128, 4)]
        + [(q, q + 3) for q in range(3, 124, 4)],
    )
    across = swapped(merged, 2)
    beside = swapped(merged, 1)
    both = swapped(across, 1)
    weights = (coarse_gate, coarse_value, coarse_scans)
    lead, tail, maps, share, run, run_log, near_ends = coarse_main(
        "near", (merged, beside), weights, params, (rim_a, rim_b)
    )
    lead_1, tail_1, maps_1, share_1, run_1, run_log_1, ends_1 = coarse_main(
        "far_1", (across,), weights, params, (near_ends, rim_e)
    )
    lead_2, tail_2, maps_2, share_2, run_2, run_log_2, run_f, run_log_f, message = coarse_main(
        "far_2", (both,), weights, params,
        (near_ends, ends_1, rim_d, run, run_log, run_1, run_log_1),
    )
    got = lax.all_to_all(message, SEQ, split_axis=0, concat_axis=0, tiled=True)
    got = lax.all_to_all(prefix(got), SEQ, split_axis=0, concat_axis=0, tiled=True)
    norm = params[4]
    gn, ks, ss, sums = coarse_close(
        True, lead, tail, maps, got, run_f, run_log_f, norm, coarse_output
    )
    gn_f, ks_f, ss_f, sums_f = coarse_close(
        False, lead_1, lead_2, tail_1, tail_2, maps_1, maps_2, got, run, run_log,
        run_1, run_log_1, run_2, run_log_2, norm, coarse_output,
    )
    went, sums = relay(ks, sums, swapped(ss, 1))
    went = swapped(went, 2)
    went_f, sums_f = relay(ks_f, sums_f, swapped(ss_f, 1))
    went_f = swapped(went_f, 2)
    kk, sk = close_rest(gn, gn_f, coarse_output)
    sk = swapped(sk, 1)
    return final(share, share_1, share_2, kk, sk, sums, went_f, sums_f, went)


def solution(mesh):
    finer = Mesh(mesh.devices.reshape(4, 2, 4, 2, 2), ALL)
    cols = P(None, HEAD)
    return jax.shard_map(
        shards,
        mesh=finer,
        in_specs=(
            P(SEQ, None), P(), cols, cols, P(), cols, cols, P(), P(HEAD), P(HEAD), P(HEAD),
            P(HEAD, None), P(), P(), cols, cols, P(), cols, cols, P(), P(HEAD), P(HEAD), P(HEAD),
            P(HEAD, None),
        ),
        out_specs=P(SEQ, HEAD),
        check_vma=False,
    )
```

```python
import jax
import jax.numpy as jnp
from jax import lax
from jax.experimental import pallas as pl
from jax.experimental.pallas import tpu as pltpu
from jax.sharding import Mesh
from jax.sharding import PartitionSpec as P


SEQ = ("z", "u", "x")
HEAD = ("y", "c")
ALL = ("z", "u", "x", "y", "c")
EPSILON = 1e-05
BLK = 256
BF = jnp.bfloat16
F32 = jnp.float32
NN = (((1,), (0,)), ((), ()))
NT = (((1,), (1,)), ((), ()))
TN = (((0,), (0,)), ((), ()))


def dot(a, b, dims=NN):
    return lax.dot_general(a, b, dims, preferred_element_type=F32)


def parts(x):
    hi = x.astype(BF).astype(F32)
    rest = x - hi
    mid = rest.astype(BF).astype(F32)
    low = rest - mid
    return jnp.concatenate([hi, mid, low, jnp.zeros_like(x)], 0).astype(BF)


def decay_rows(row):
    hi = row.astype(BF).astype(F32)
    rest = row - hi
    mid = rest.astype(BF).astype(F32)
    low = rest - mid
    return jnp.concatenate([hi, mid, low, jnp.zeros((13, row.shape[1]), F32)], 0).astype(BF)


def of_rows(rows):
    rows = rows.astype(F32)
    return rows[0:1] + rows[1:2] + rows[2:3]


def iota(shape, dim):
    return lax.broadcasted_iota(jnp.int32, shape, dim)


def head_sel(width):
    return iota((8, width), 0) == iota((8, width), 1) // 64


def expander(width):
    r, lane = iota((32, width), 0), iota((32, width), 1)
    return jnp.where((r < 24) & (r % 8 == lane // 64), 1.0, 0.0).astype(BF)


def upper():
    return jnp.where(iota((BLK, BLK), 0) <= iota((BLK, BLK), 1), 1.0, 0.0).astype(BF)


def silu(v):
    h = v * 0.5
    return h + h * jnp.tanh(h)


def softplus(v):
    return jnp.maximum(v, 0.0) + jnp.log1p(jnp.exp(-jnp.abs(v)))


def rms(x, gain):
    x = x.astype(F32)
    return (x * lax.rsqrt(jnp.mean(x * x, axis=-1, keepdims=True) + EPSILON) * gain).astype(BF)


def cumulate(logs, tri):
    s = dot(parts(logs), tri)
    return s[0:8] + s[8:16] + s[16:24]


def spaced(length):
    return length // 8 + 1


def convolve(cv, act, half_taps, length):
    apart = spaced(length)

    def slab(c):
        taps = half_taps[c]
        rows = [cv[c, pl.ds(13 + i, 8, stride=apart), :] for i in range(3)]
        for i in range(apart):
            rows.append(cv[c, pl.ds(16 + i, 8, stride=apart), :])
            h = rows[i] * taps[0:1]
            for k in range(1, 4):
                h = h + rows[i + k] * taps[k : k + 1]
            act[c, pl.ds(i, 8, stride=apart), :] = h + h * jnp.tanh(h)

    for c in range(cv.shape[0]):
        slab(c)


def project(rows, weights, cv, start, slab):
    product = dot(rows, weights)
    for j in range(product.shape[1] // 128):
        cv[slab + j, start : start + rows.shape[0], :] = product[:, j * 128 : (j + 1) * 128]


def rounded(x):
    return x.astype(BF).astype(F32)


def small_rows(pack):
    rows = pack[384:416, :].astype(F32)
    kv = rows[0:4, 0:128] + rows[4:8, 0:128] + rows[8:12, 0:128]
    right = rows[0:16, 128:256]
    norm, b0, b1, d0, d1 = (of_rows(right[3 * j : 3 * j + 3]) for j in range(5))
    return kv, norm, jnp.concatenate([b0, b1], 0), jnp.concatenate([d0, d1], 0), rows[16:18]


def three(row):
    hi = row.astype(BF).astype(F32)
    rest = row - hi
    mid = rest.astype(BF).astype(F32)
    return [hi, mid, rest - mid]


def run_copies(pairs, sems):
    copies = [pltpu.make_async_copy(a, b, sems.at[j]) for j, (a, b) in enumerate(pairs)]
    for copy in copies:
        copy.start()
    return copies


def pack_kernel(
    bias, decay, gate, value, output, steps, kv, norm, tokens,
    pack, ends, kv_v, norm_v, steps_v, bias_v, decay_v, sems,
):
    copies = run_copies(
        (
            (kv, kv_v),
            (norm, norm_v),
            (steps, steps_v),
            (bias, bias_v),
            (decay, decay_v),
            (tokens.at[4080:4096], ends),
            (gate, pack.at[0:256, 0:128]),
            (value, pack.at[0:256, 128:256]),
            (output, pack.at[256:384]),
        ),
        sems,
    )
    for copy in copies[:5]:
        copy.wait()
    left = jnp.concatenate(three(kv_v[...]) + [jnp.zeros((4, 128), F32)], 0)
    rows = three(norm_v[...])
    for ref in (bias_v, decay_v):
        for j in range(2):
            rows = rows + three(jnp.broadcast_to(ref[:, j : j + 1], (1, 128)))
    right = jnp.concatenate(rows + [jnp.zeros((1, 128), F32)], 0)
    below = jnp.concatenate([steps_v[...].astype(F32), jnp.zeros((14, 256), F32)], 0)
    pack[384:416, :] = jnp.concatenate([jnp.concatenate([left, right], 1), below], 0).astype(BF)
    for copy in copies[5:]:
        copy.wait()


def packed(bias, decay, gate, value, output, steps, kv, norm, tokens):
    return pl.pallas_call(
        pack_kernel,
        in_specs=[HBM] * 9,
        out_specs=[VM] * 2,
        out_shape=[sds((416, 256), BF), sds((16, 256), BF)],
        scratch_shapes=[
            pltpu.VMEM((4, 128), F32),
            pltpu.VMEM((1, 128), F32),
            pltpu.VMEM((2, 256), BF),
            pltpu.VMEM((1, 2), F32),
            pltpu.VMEM((1, 2), F32),
            pltpu.SemaphoreType.DMA((9,)),
        ],
        compiler_params=few(4),
        name="pack",
    )(*in_hbm(bias, decay, gate, value, output, steps, kv, norm, tokens))


def params_kernel(bias, decay, kv, ks, gain, steps, norm, taps, both, *refs):
    outs, kv_v, ks_v, bias_v, decay_v, sems = refs[:3], *refs[3:]
    copies = run_copies(
        (
            (kv, kv_v), (ks, ks_v), (bias, bias_v), (decay, decay_v),
            (gain, outs[0]), (steps, outs[1]), (norm, outs[2]),
        ),
        sems,
    )
    for copy in copies:
        copy.wait()
    for j in range(4):
        cols = slice(j * 128, (j + 1) * 128)
        taps[j] = kv_v[:, cols] * 0.5
        taps[4 + j] = ks_v[:, cols] * 0.5
    rows = [
        jnp.broadcast_to(ref[:, j : j + 1], (1, 128)) for ref in (bias_v, decay_v) for j in range(8)
    ]
    both[...] = jnp.concatenate(rows, 0)


def coarse_params(bias, decay, kv, ks, gain, steps, norm):
    return pl.pallas_call(
        params_kernel,
        in_specs=[HBM] * 7,
        out_specs=[VM] * 5,
        out_shape=[
            sds((8, 4, 128)), sds((16, 128)), sds((1, 1024)), sds((8, 1024), BF), sds((1, 512)),
        ],
        scratch_shapes=[
            pltpu.VMEM((4, 512), F32),
            pltpu.VMEM((4, 512), F32),
            pltpu.VMEM((1, 8), F32),
            pltpu.VMEM((1, 8), F32),
            pltpu.SemaphoreType.DMA((7,)),
        ],
        compiler_params=few(4),
        name="coarse_params",
    )(*in_hbm(bias, decay, kv, ks, gain, steps, norm))


def state_chunk(x, rim, gain, pack, scans, ks, taps, cv, act):
    kv, _, bias, decay, steps = small_rows(pack)
    pad = jnp.zeros((6, 128), F32)
    bias = jnp.concatenate([bias, pad], 0)[:, 0:1]
    decay = jnp.concatenate([decay, pad], 0)[:, 0:1]
    steps = jnp.concatenate([steps, jnp.zeros((6, 256), F32)], 0).astype(BF)
    wv, wb = pack[0:256, 128:256], scans[:, 0:256]
    taps[0] = kv * 0.5
    taps[1] = ks[:, 0:128] * 0.5
    taps[2] = ks[:, 128:256] * 0.5
    normed = rms(x, gain[...])
    before = rms(rim, gain[...])
    project(before, wv, cv, 0, 0)
    project(before, wb, cv, 0, 1)
    project(normed, wv, cv, 16, 0)
    project(normed, wb, cv, 16, 1)
    convolve(cv, act, taps, 1024)
    raw = dot(steps, normed, NT)
    dt = softplus(raw + bias)
    logs = -dt * decay
    tri = upper()
    carry = jnp.zeros((8, 1), F32)
    pieces = []
    for b in range(4):
        piece = cumulate(logs[:, b * BLK : (b + 1) * BLK], tri) + carry
        carry = piece[:, BLK - 1 : BLK]
        pieces.append(piece)
    cum = jnp.concatenate(pieces, 1)
    tail = jnp.exp(carry - cum) * dt
    spread = dot(parts(tail), expander(128), TN)
    scaled = (act[0, 0:1024] * spread).astype(BF)
    local = dot(jnp.concatenate([act[1, 0:1024].astype(BF), act[2, 0:1024].astype(BF)], 1), scaled, TN)
    total = jnp.sum(
        jnp.where(head_sel(128), jnp.broadcast_to(carry, (8, 128)), 0.0), axis=0, keepdims=True
    )
    return local, total


def later_chunks_kernel(
    tokens, gain_h, pack, scans_h, ks_h,
    local, total, x0, mine, mine_rim, gain, scans, ks, xs, taps, cv, act, sems, x_sems,
):
    i = pl.program_id(0)
    start = pl.multiple_of(lax.axis_index(HEAD) * 1024, 1024)
    early = pl.multiple_of(jnp.maximum(start - 16, 0), 16)
    mine_pairs = (
        (tokens.at[0:1024], x0),
        (tokens.at[pl.ds(start, 1024)], mine),
        (tokens.at[pl.ds(early, 16)], mine_rim),
    )

    def chunk(j):
        begin_row = pl.multiple_of((j + 1) * 1024 - 16, 16)
        return pltpu.make_async_copy(tokens.at[pl.ds(begin_row, 1040)], xs.at[j], x_sems.at[j])

    @pl.when(i == 0)
    def _():
        chunk(0).start()
        copies = run_copies(((gain_h, gain), (scans_h, scans), (ks_h, ks)), sems)
        chunk(1).start()
        chunk(2).start()
        for j, (a, b) in enumerate(mine_pairs):
            pltpu.make_async_copy(a, b, sems.at[3 + j]).start()
        for copy in copies:
            copy.wait()

    chunk(i).wait()
    state, logs = state_chunk(xs[i, 16:1040], xs[i, 0:16], gain, pack, scans, ks, taps, cv, act)
    local[i] = state
    total[i] = jnp.broadcast_to(logs, (8, 128))

    @pl.when(i == 2)
    def _():
        for j, (a, b) in enumerate(mine_pairs):
            pltpu.make_async_copy(a, b, sems.at[3 + j]).wait()


def first_chunk_kernel(
    x, rim, gain, pack, scans, ks, later, later_total,
    local, total, whole, whole_total, message, taps, cv, act,
):
    state, logs = state_chunk(x[...], rim[...], gain, pack, scans, ks, taps, cv, act)
    local[...] = state
    total[...] = jnp.broadcast_to(logs, (8, 128))
    for j in range(3):
        piece = later_total[j, 0:1, :]
        state = state * jnp.exp(piece) + later[j]
        logs = logs + piece
    whole[...] = state
    whole_total[...] = jnp.broadcast_to(logs, (8, 128))
    message[0:256, :] = state.astype(BF)
    message[256:272, :] = decay_rows(logs)


def sds(shape, dtype=F32):
    return jax.ShapeDtypeStruct(shape, dtype)


def in_hbm(*arrays):
    return [pltpu.with_memory_space_constraint(a, pltpu.HBM) for a in arrays]


def few(mib):
    return pltpu.CompilerParams(vmem_limit_bytes=mib << 20)


VM = pl.BlockSpec(memory_space=pltpu.VMEM)
HBM = pl.BlockSpec(memory_space=pltpu.HBM)


def fine_states(tokens, ends_from, gain, pack, scans, ks):
    scratch = [
        pltpu.VMEM((3, 4, 128), F32),
        pltpu.VMEM((3, 1048, 128), F32),
        pltpu.VMEM((3, 1032, 128), F32),
    ]
    later, later_total, x0, *resident = pl.pallas_call(
        later_chunks_kernel,
        grid=(3,),
        in_specs=[HBM, HBM, VM, HBM, HBM],
        out_specs=[VM] * 8,
        out_shape=[
            sds((3, 256, 128)),
            sds((3, 8, 128)),
            sds((1024, 256), BF),
            sds((1024, 256), BF),
            sds((16, 256), BF),
            sds((1, 256)),
            sds((256, 512), BF),
            sds((4, 512)),
        ],
        scratch_shapes=[pltpu.VMEM((3, 1040, 256), BF)]
        + scratch
        + [pltpu.SemaphoreType.DMA((6,)), pltpu.SemaphoreType.DMA((3,))],
        compiler_params=few(16),
        name="later_chunks",
    )(*in_hbm(tokens, gain), pack, *in_hbm(scans, ks))
    _, _, gain, scans, ks = resident
    first = pl.pallas_call(
        first_chunk_kernel,
        in_specs=[VM] * 8,
        out_specs=[VM] * 5,
        out_shape=[
            sds((256, 128)),
            sds((8, 128)),
            sds((256, 128)),
            sds((8, 128)),
            sds((272, 128), BF),
        ],
        scratch_shapes=scratch,
        compiler_params=few(16),
        name="first_chunk",
    )(x0, ends_from, gain, pack, scans, ks, later, later_total)
    return later, later_total, resident, first


def combine(i, count, own, own_total, prior, prior_total, received):
    state = jnp.zeros_like(own)
    logs = jnp.zeros_like(own_total)
    zero = jnp.zeros((), F32)
    got = [(r[0:256, :].astype(F32), of_rows(r[256:272, :])) for r in received]
    for k in range(count - 1, 0, -1):
        s, l = got[k - 1]
        valid = i >= k
        state = jnp.where(valid, state * jnp.exp(l) + s, state)
        logs = jnp.where(valid, logs + l, logs)
    new_prior = state * jnp.exp(prior_total) + prior
    new_prior_total = logs + prior_total
    state = state * jnp.exp(own_total) + own
    logs = logs + own_total
    for m in range(1, count):
        s, l = got[count - m - 1]
        valid = i + m < count
        state = jnp.where(valid, state * jnp.exp(l) + s, state)
        logs = jnp.where(valid, logs + l, logs)
    return new_prior, new_prior_total, state, logs


def middle_kernel(axis, count, fresh, own, own_total, *refs):
    if fresh:
        prior, prior_total = jnp.zeros((256, 128), F32), jnp.zeros((1, 128), F32)
    else:
        prior, prior_total, refs = refs[0][...], refs[1][0:1, :], refs[2:]
    received, (np_ref, npt_ref, ns_ref, nst_ref, message) = refs[: count - 1], refs[count - 1 :]
    p, pt, s, st = combine(
        lax.axis_index(axis), count, own[...], own_total[0:1, :], prior, prior_total, received
    )
    np_ref[...] = p
    npt_ref[...] = jnp.broadcast_to(pt, (8, 128))
    ns_ref[...] = s
    nst_ref[...] = jnp.broadcast_to(st, (8, 128))
    message[0:256, :] = s.astype(BF)
    message[256:272, :] = decay_rows(st)


def middle_stage(axis, count, own, own_total, prior, received):
    return pl.pallas_call(
        lambda *refs: middle_kernel(axis, count, not prior, *refs),
        in_specs=[VM] * (2 + len(prior) + len(received)),
        out_specs=[VM] * 5,
        out_shape=[
            sds((256, 128)),
            sds((8, 128)),
            sds((256, 128)),
            sds((8, 128)),
            sds((272, 128), BF),
        ],
        compiler_params=few(4),
    )(own, own_total, *prior, *received)


def last_kernel(own, own_total, prior, prior_total, r1, r2, r3, l0, t0, later, later_total,
                o0, o1, o2, o3, sub):
    p, _, _, _ = combine(
        lax.axis_index("z"), 4, own[...], own_total[0:1, :], prior[...], prior_total[0:1, :],
        (r1, r2, r3),
    )
    sub[0] = p
    p = p * jnp.exp(t0[0:1, :]) + l0[...]
    sub[1] = p
    for j in range(2):
        p = p * jnp.exp(later_total[j, 0:1, :]) + later[j]
        sub[j + 2] = p
    h = lax.axis_index(HEAD)
    for k, out in enumerate((o0, o1, o2, o3)):
        out[...] = sub[h ^ k].astype(BF)


def last_stage(own, own_total, prior, received, l0, t0, later, later_total):
    return pl.pallas_call(
        last_kernel,
        in_specs=[VM] * 11,
        out_specs=[VM] * 4,
        out_shape=[sds((256, 128), BF)] * 4,
        scratch_shapes=[pltpu.VMEM((4, 256, 128), F32)],
        compiler_params=few(6),
        name="chain_last",
    )(own, own_total, *prior, *received, l0, t0, later, later_total)


def begin(before, wv, ws, cv, run, run_log):
    project(before, wv[...], cv, 0, 0)
    project(before, ws[...], cv, 0, 4)
    run[...] = jnp.zeros_like(run)
    run_log[...] = jnp.zeros_like(run_log)


def scan_block(
    normed, wg, wv, ws, wst, taps, bias, decay,
    lead, tail_out, maps_out, cv, act, sc, spread, scaled, run, run_log,
):
    project(normed, wv[...], cv, 16, 0)
    project(normed, ws[...], cv, 16, 4)
    tail_out[...] = silu(dot(normed, wg[...]))
    convolve(cv, act, taps, BLK)
    cv[:, 0:16, :] = cv[:, 256:272, :]
    raw = dot(wst[...], normed, NT)
    dt = softplus(raw + bias[...])
    logs = -dt * decay[...]
    cum = cumulate(logs, upper())
    last = cum[:, BLK - 1 : BLK]
    before_log = run_log[:, 0:1]
    stacked = jnp.concatenate(
        [jnp.exp(cum), jnp.exp(cum + before_log), jnp.exp(last - cum) * dt], 1
    )
    spread[...] = dot(parts(stacked), expander(512), TN)
    run_log[...] = run_log[...] + last
    columns = dot(parts(cum), jnp.where(
        (iota((32, 128), 0) < 24) & (iota((32, 128), 0) % 8 == iota((32, 128), 1)), 1.0, 0.0
    ).astype(BF), TN)
    rows = cum - jnp.log(dt)
    in_map = jnp.concatenate([act[4, 0:BLK].astype(BF), act[5, 0:BLK].astype(BF)], 1)
    out_map = jnp.concatenate([act[6, 0:BLK].astype(BF), act[7, 0:BLK].astype(BF)], 1)
    maps_out[...] = out_map
    sc[...] = dot(out_map, in_map, NT)
    lead[...] = spread[0:256, :] * dot(out_map, run[...].astype(BF))
    low_tri = iota((128, 128), 0) >= iota((128, 128), 1)
    lane_low = iota((BLK, 128), 1) < 64
    for p in range(4):
        cols = slice(p * 128, (p + 1) * 128)
        vals = act[p, 0:BLK]
        v0 = jnp.where(lane_low, vals, 0.0).astype(BF)
        v1 = jnp.where(lane_low, 0.0, vals).astype(BF)
        upper_w, lower_w = [], []
        for h in (2 * p, 2 * p + 1):
            c0, c1 = columns[0:128, h : h + 1], columns[128:256, h : h + 1]
            r0, r1 = rows[h : h + 1, 0:128], rows[h : h + 1, 128:256]
            upper_w.append(
                (sc[0:128, 0:128] * jnp.exp(jnp.where(low_tri, c0 - r0, -jnp.inf))).astype(BF)
            )
            lower_w.append((sc[128:256, 0:128] * jnp.exp(c1 - r0)).astype(BF))
            lower_w.append(
                (sc[128:256, 128:256] * jnp.exp(jnp.where(low_tri, c1 - r1, -jnp.inf))).astype(BF)
            )
        top = dot(
            jnp.concatenate(upper_w, 1), jnp.concatenate([v0[0:128], v1[0:128]], 0)
        )
        bottom = dot(jnp.concatenate(lower_w, 1), jnp.concatenate([v0, v1], 0))
        gate = tail_out[:, cols]
        lead[0:128, cols] = (top + lead[0:128, cols]) * gate[0:128]
        lead[128:256, cols] = (bottom + lead[128:256, cols]) * gate[128:256]
        tail_out[:, cols] = spread[256:512, cols] * gate
        scaled[:, cols] = (vals * spread[512:768, cols]).astype(BF)
    run[...] = run[...] * spread[255:256, :] + dot(in_map, scaled[...], TN)


SCAN_SCRATCH = [
    pltpu.VMEM((8, 280, 128), F32),
    pltpu.VMEM((8, BLK + 8, 128), F32),
    pltpu.VMEM((BLK, BLK), F32),
    pltpu.VMEM((768, 512), F32),
    pltpu.VMEM((256, 512), BF),
]


def fine_main_kernel(later, x, gain, ws, ks, p0, p1, p2, p3, *refs):
    (
        x0, x1, x2, lead, tail_out, maps_out, run, run_log, cv_end,
        wg, wv, wst, taps, bias, decay, cv, act, sc, spread, scaled,
    ) = refs

    @pl.when(pl.program_id(0) == 0)
    def _():
        for j in range(4):
            taps[4 + j] = ks[:, j * 128 : (j + 1) * 128] * 0.5
        for j, p in enumerate((p0, p1, p2, p3)):
            cols = slice(j * 128, (j + 1) * 128)
            two = slice(2 * j, 2 * j + 2)
            wg[:, cols] = p[0:256, 0:128]
            wv[:, cols] = p[0:256, 128:256]
            kv, _, bias[two, :], decay[two, :], wst[two, :] = small_rows(p)
            taps[j] = kv * 0.5
        if later:
            run[...] = x0[...]
            run_log[...] = x1[...]
            cv[:, 0:16, :] = x2[...]
        else:
            rim = jnp.where(lax.axis_index(HEAD) == 0, x0[...].astype(F32), x1[...].astype(F32))
            begin(rms(rim, gain[...]), wv, ws, cv, run, run_log)

    scan_block(
        rms(x[...], gain[...]), wg, wv, ws, wst[...].astype(BF), taps, bias[:, 0:1], decay[:, 0:1],
        lead, tail_out, maps_out, cv, act, sc, spread, scaled, run, run_log,
    )
    cv_end[...] = cv[:, 0:16, :]


def fine_main(x, gain, scans, ks, packs, extra, later):
    at = 2 if later else 0
    rows = [pl.BlockSpec((BLK, n), lambda i: (i, 0)) for n in (512, 512, 256)]
    return pl.pallas_call(
        lambda *refs: fine_main_kernel(later, *refs),
        grid=(2,),
        in_specs=[pl.BlockSpec((BLK, 256), lambda i: (at + i, 0))] + [VM] * 10,
        out_specs=rows + [VM] * 3,
        out_shape=[
            sds((512, 512)), sds((512, 512)), sds((512, 256), BF),
            sds((256, 512)), sds((8, 128)), sds((8, 16, 128)),
        ],
        scratch_shapes=[
            pltpu.VMEM((256, 512), BF),
            pltpu.VMEM((256, 512), BF),
            pltpu.VMEM((8, 256), F32),
            pltpu.VMEM((8, 4, 128), F32),
            pltpu.VMEM((8, 128), F32),
            pltpu.VMEM((8, 128), F32),
        ]
        + SCAN_SCRATCH,
        compiler_params=few(16),
        name="fine_main_b" if later else "fine_main_a",
    )(x, gain, scans, ks, *packs, *extra)


def fine_close_kernel(
    lead_a, lead_b, tail_a, tail_b, maps_a, maps_b, x, s0, s1, s2, s3, p0, p1, p2, p3, merge,
    merged, end_rows, lead, tail, maps, hidden, state, wo, norm,
):
    i = pl.program_id(0)

    @pl.when(i < 2)
    def _():
        lead[...], tail[...], maps[...] = lead_a[...], tail_a[...], maps_a[...]

    @pl.when(i >= 2)
    def _():
        lead[...], tail[...], maps[...] = lead_b[...], tail_b[...], maps_b[...]

    @pl.when(i == 0)
    def _():
        for j, (s, p) in enumerate(zip((s0, s1, s2, s3), (p0, p1, p2, p3))):
            cols = slice(j * 128, (j + 1) * 128)
            state[:, cols] = s[...]
            wo[cols, :] = p[256:384, :]
            norm[:, cols] = small_rows(p)[1]

    gated = lead[...] + tail[...] * dot(maps[...], state[...])
    factor = lax.rsqrt(jnp.sum(gated * gated, axis=1, keepdims=True) / 512.0 + EPSILON)
    out = x[...].astype(F32)
    total = dot((gated * factor * norm[...]).astype(BF), wo[...])
    start = pl.multiple_of(i * BLK, BLK)
    hidden[0, pl.ds(start, BLK), :] = rounded(out[:, 0:128] + total[:, 0:128])
    hidden[1, pl.ds(start, BLK), :] = rounded(out[:, 128:256] + total[:, 128:256])

    @pl.when(i == pl.num_programs(0) - 1)
    def _():
        total = None
        for odd in range(2):
            rows = [
                hidden[half, pl.ds(odd, 512, stride=2), :].reshape(8, 2, 32, 128)
                for half in range(2)
            ]
            for line in range(2):
                tile = [r[:, line].reshape(256, 128).astype(BF) for r in rows]
                at = (2 * line + odd) * 256
                piece = dot(jnp.concatenate(tile, 1), merge[at : at + 256, :])
                total = piece if total is None else total + piece
        result = total.astype(BF)
        merged[...] = result
        end_rows[...] = result[240:256]


def fine_close(leads, tails, maps, x, states, packs, merge):
    def halves(width):
        return [
            pl.BlockSpec((BLK, width), lambda i: (jnp.minimum(i, 1), 0)),
            pl.BlockSpec((BLK, width), lambda i: (jnp.maximum(i - 2, 0), 0)),
        ]

    return pl.pallas_call(
        fine_close_kernel,
        grid=(4,),
        in_specs=halves(512)
        + halves(512)
        + halves(256)
        + [pl.BlockSpec((BLK, 256), lambda i: (i, 0))]
        + [VM] * 9,
        out_specs=[VM] * 2,
        scratch_shapes=[
            pltpu.VMEM((BLK, 512), F32),
            pltpu.VMEM((BLK, 512), F32),
            pltpu.VMEM((BLK, 256), BF),
            pltpu.VMEM((2, 1024, 128), F32),
            pltpu.VMEM((256, 512), BF),
            pltpu.VMEM((512, 256), BF),
            pltpu.VMEM((1, 512), F32),
        ],
        out_shape=[sds((256, 1024), BF), sds((16, 1024), BF)],
        compiler_params=few(16),
        name="fine_close",
    )(*leads, *tails, *maps, x, *states, *packs, merge)


def in_order(first, a, a_log, b, b_log):
    lead_log = jnp.where(first, b_log, a_log)
    row = jnp.exp(spread_row(lead_log))
    return jnp.where(first, a, b) * row + jnp.where(first, b, a), a_log + b_log


def coarse_main_kernel(kind, pieces, gain, wg, wv, ws, wst, taps, both, *refs):
    qs, refs = refs[:pieces], refs[pieces:]
    xs, sems, cv, act, sc, spread, scaled = refs[-7:]
    y, c = lax.axis_index("y"), lax.axis_index("c")
    h = 2 * y + c
    if kind == "near":
        ra, rb, lead, tail_out, maps_out, share, run, run_log = refs[:-7]
    elif kind == "far_1":
        re, lead, tail_out, maps_out, share, run, run_log, ends = refs[:-7]
    else:
        (
            ends_1, rd, near_run, near_log, run_1, run_log_1,
            lead, tail_out, maps_out, share, run, run_log, far_run, far_log, message,
        ) = refs[:-7]
    i = pl.program_id(0)

    @pl.when(i == 0)
    def _():
        if kind == "near":
            copies = run_copies(((qs[0], xs.at[c]), (qs[1], xs.at[1 - c])), sems)
            rim = jnp.where(c == 0, ra[...].astype(F32), rb[...].astype(F32))
        else:
            copies = run_copies(((qs[0], xs.at[0]),), sems)
            rim = re[...].astype(F32) if kind == "far_1" else rd[...].astype(F32)
            if kind == "far_2":
                rim = jnp.where(c == 0, ends_1[...].astype(F32), rim)
        begin(rms(rim, gain[...]), wv, ws, cv, run, run_log)
        for copy in copies:
            copy.wait()
        if kind == "far_1":
            ends[...] = xs[0, 240:256, :]

    share[...] = xs[i, :, pl.ds(pl.multiple_of(h * 256, 256), 256)]
    scan_block(
        rms(xs[i], gain[...]), wg, wv, ws, wst[...], taps, both[0:8, 0:1], both[8:16, 0:1],
        lead, tail_out, maps_out, cv, act, sc, spread, scaled, run, run_log,
    )

    if kind == "far_2":
        log_1, log_2, log_n = run_log_1[:, 0:1], run_log[:, 0:1], near_log[:, 0:1]
        far, log_f = in_order(c == 0, run_1[...], log_1, run[...], log_2)
        far_run[...] = far
        far_log[...] = jnp.broadcast_to(log_f, (8, 128))
        total, log = in_order(y == 0, near_run[...], log_n, far, log_f)
        extra = decay_rows(spread_row(log))[0:8]
        for n in range(16):
            for half in range(2):
                cols = slice(half * 256, (half + 1) * 256)
                message[2 * n + half, 0:16, :] = total[n * 16 : (n + 1) * 16, cols].astype(BF)
                message[2 * n + half, 16:24, :] = extra[:, cols]


def spread_row(column):
    return jnp.sum(
        jnp.where(head_sel(512), jnp.broadcast_to(column, (8, 512)), 0.0), axis=0, keepdims=True
    )


ANY = pl.BlockSpec(memory_space=pl.ANY)


def coarse_main(kind, pieces, weights, params, extra):
    taps, both, gain, wst, _ = params
    blocks = len(pieces)
    length = blocks * BLK
    rows = [pl.BlockSpec((BLK, n), lambda i: (i, 0)) for n in (512, 512, 256, 256)]
    last = []
    if kind == "far_1":
        last = [sds((16, 1024), BF)]
    elif kind == "far_2":
        last = [sds((256, 512)), sds((8, 128)), sds((32, 24, 256), BF)]
    return pl.pallas_call(
        lambda *refs: coarse_main_kernel(kind, blocks, *refs),
        grid=(blocks,),
        in_specs=[VM] * 7 + [ANY] * blocks + [VM] * len(extra),
        out_specs=rows + [VM] * (2 + len(last)),
        out_shape=[
            sds((length, 512)),
            sds((length, 512)),
            sds((length, 256), BF),
            sds((length, 256), BF),
            sds((256, 512)),
            sds((8, 128)),
        ]
        + last,
        scratch_shapes=[pltpu.VMEM((blocks, 256, 1024), BF), pltpu.SemaphoreType.DMA((blocks,))]
        + SCAN_SCRATCH,
        compiler_params=few(16),
    )(gain, *weights, wst, taps, both, *pieces, *extra)


def own_rim_kernel(came, beside, out):
    out[...] = jnp.where(
        lax.axis_index("c") == 0, came[...].astype(F32), beside[240:256, :].astype(F32)
    ).astype(BF)


def own_rim(came, beside):
    return pl.pallas_call(
        own_rim_kernel,
        in_specs=[VM] * 2,
        out_specs=VM,
        out_shape=sds((16, 1024), BF),
        compiler_params=few(4),
        name="own_rim",
    )(came, beside)


def prefix_kernel(got, out):
    state = jnp.zeros((16, 256), F32)
    for d in range(32):
        out[d] = state.astype(BF)
        state = state * jnp.exp(of_rows(got[d, 16:24, :])) + got[d, 0:16, :].astype(F32)


def prefix(got):
    return pl.pallas_call(
        prefix_kernel,
        in_specs=[VM],
        out_specs=VM,
        out_shape=sds((32, 16, 256), BF),
        compiler_params=few(4),
        name="prefix",
    )(got)


def coarse_close_kernel(near, *refs):
    if near:
        lead, tail, maps, got, far_run, far_log, norm, wo, *refs = refs
    else:
        leads, tails, mapss = refs[0:2], refs[2:4], refs[4:6]
        got, near_run, near_log, run_1, log_1, run_2, log_2, norm, wo, *refs = refs[6:]
    gn, ks, ss, square_sums, states, sums = refs
    y, c = lax.axis_index("y"), lax.axis_index("c")
    h = 2 * y + c
    came = jnp.concatenate(
        [jnp.concatenate([got[2 * n], got[2 * n + 1]], 1) for n in range(16)], 0
    ).astype(F32)

    def after(state, cond, run, log):
        row = jnp.exp(spread_row(log[:, 0:1]))
        return jnp.where(cond, state * row + run[...], state)

    if near:
        states[0] = after(came, y == 1, far_run, far_log).astype(BF)
    else:
        came = after(came, y == 0, near_run, near_log)
        states[0] = after(came, c == 1, run_2, log_2).astype(BF)
        states[1] = after(came, c == 0, run_1, log_1).astype(BF)
    ones = jnp.ones((8, 512), BF)
    for i in range(2):
        if near:
            rows = slice(i * BLK, (i + 1) * BLK)
            gated = lead[rows] + tail[rows] * dot(maps[rows], states[0])
            place = i
        else:
            gated = leads[i][...] + tails[i][...] * dot(mapss[i][...], states[i])
            place = jnp.bitwise_xor(c, i)
        sq = gated * gated
        hi = sq.astype(BF)
        low = (sq - hi.astype(F32)).astype(BF)
        sums[place] = dot(ones, hi, NT) + dot(ones, low, NT)
        scaled = (gated * norm[...]).astype(BF)
        at = pl.ds(pl.multiple_of(place * BLK, BLK), BLK)
        gn[at, :] = scaled
        for k, out in ((2, ks), (3, ss)):
            col = pl.multiple_of((h ^ k) * 256, 256)
            out[at, :] = dot(scaled, wo[:, pl.ds(col, 256)]).astype(BF)
    square_sums[...] = jnp.concatenate([sums[0], sums[1]], 1)
    ss[512:528, :] = sum_rows(sums[0, 0:1], sums[1, 0:1])


def coarse_close(near, *args):
    return pl.pallas_call(
        lambda *refs: coarse_close_kernel(near, *refs),
        in_specs=[VM] * len(args),
        out_specs=[VM] * 4,
        out_shape=[
            sds((512, 512), BF), sds((512, 256), BF), sds((528, 256), BF), sds((8, 512)),
        ],
        scratch_shapes=[pltpu.VMEM((2, 256, 512), BF), pltpu.VMEM((2, 8, 256), F32)],
        compiler_params=few(12),
        name="coarse_close_near" if near else "coarse_close_far",
    )(*args)


def close_rest_kernel(near, far, wo, kk, sk):
    h = lax.axis_index(HEAD)
    for k, out in enumerate((kk, sk)):
        col = pl.multiple_of((h ^ k) * 256, 256)
        for j, ref in enumerate((near, far)):
            out[j * 512 : (j + 1) * 512, :] = dot(ref[...], wo[:, pl.ds(col, 256)]).astype(BF)


def close_rest(near, far, wo):
    return pl.pallas_call(
        close_rest_kernel,
        in_specs=[VM] * 3,
        out_specs=[VM] * 2,
        out_shape=[sds((1024, 256), BF)] * 2,
        compiler_params=few(8),
        name="close_rest",
    )(near, far, wo)


def sum_rows(a, b):
    return jnp.concatenate(three(a) + three(b) + [jnp.zeros((10, 256), F32)], 0).astype(BF)


def rows_sum(ref):
    rows = ref[512:528, :].astype(F32)
    return jnp.concatenate([of_rows(rows[0:3]), of_rows(rows[3:6])], 1)


def relay_kernel(ks, square_sums, came, out, sums):
    out[0:512, :] = (ks[...].astype(F32) + came[0:512, :].astype(F32)).astype(BF)
    total = square_sums[0:1, :] + rows_sum(came)
    out[512:528, :] = sum_rows(total[:, 0:256], total[:, 256:512])
    sums[...] = jnp.broadcast_to(total, (8, 512))


def relay(ks, square_sums, came):
    return pl.pallas_call(
        relay_kernel,
        in_specs=[VM] * 3,
        out_specs=[VM] * 2,
        out_shape=[sds((528, 256), BF), sds((8, 512))],
        compiler_params=few(4),
    )(ks, square_sums, came)


def final_kernel(share, share_1, share_2, kk, sk, sum_a, far_a, sum_b, far_b, out):
    y, c = lax.axis_index("y"), lax.axis_index("c")
    pick = jnp.where(iota((32, 256), 0) % 8 == 0, 1.0, 0.0).astype(BF)
    for side, (half, sums, far) in enumerate(((y, sum_a, far_a), (1 - y, sum_b, far_b))):
        total = sums[...] + rows_sum(far)
        factor = lax.rsqrt(total / 2048.0 + EPSILON)
        for b in range(2):
            rows = slice(b * BLK, (b + 1) * BLK)
            here = slice(side * 512 + b * BLK, side * 512 + (b + 1) * BLK)
            spread = dot(parts(factor[:, rows]), pick, TN)
            total = kk[here].astype(F32) + sk[here].astype(F32) + far[rows].astype(F32)
            if side == 0:
                own = share[rows].astype(F32)
            else:
                own = jnp.where(c == b, share_1[...].astype(F32), share_2[...].astype(F32))
            at = pl.multiple_of(half * 512 + b * BLK, BLK)
            out[pl.ds(at, BLK), :] = (own + total * spread).astype(BF)


def final(*args):
    return pl.pallas_call(
        final_kernel,
        in_specs=[VM] * 9,
        out_specs=VM,
        out_shape=sds((1024, 256), BF),
        compiler_params=few(8),
        name="final",
    )(*args)


def passed(x, axes, pairs):
    return lax.ppermute(x, axes, pairs)


def swapped(x, mask):
    return passed(x, HEAD, [(j, j ^ mask) for j in range(4)])


def round_of(x, axis):
    got = []
    for k in (1, 2, 3):
        got.append(passed(x, axis, [(j, (j + k) % 4) for j in range(4)]))
    return got


def shards(
    tokens, fine_gain, fine_gate, fine_value, fine_scans, fine_steps, fine_kernel, fine_taps,
    fine_bias, fine_decay, fine_norm, fine_output, merge_weight, coarse_gain, coarse_gate,
    coarse_value, coarse_scans, coarse_steps, coarse_kernel, coarse_taps, coarse_bias,
    coarse_decay, coarse_norm, coarse_output,
):
    pack, ends = packed(
        fine_bias[None], fine_decay[None], fine_gate, fine_value, fine_output, fine_steps.T, fine_kernel,
        fine_norm[None], tokens,
    )
    rim = passed(ends, SEQ, [(i, i + 1) for i in range(31)])
    packs = [pack] + [swapped(pack, m) for m in (1, 2, 3)]
    later, later_total, resident, (l0, t0, own, own_total, message) = fine_states(
        tokens, rim, fine_gain[None], pack, fine_scans, fine_taps
    )
    mine, mine_rim, gain, scans, ks = resident
    got = round_of(message, "x")
    first = fine_main(mine, gain, scans, ks, packs, (rim, mine_rim, t0), False)
    *prior, own, own_total, message = middle_stage("x", 4, own, own_total, (), got)
    got = [passed(message, "u", [(0, 1), (1, 0)])]
    params = coarse_params(
        coarse_bias[None], coarse_decay[None], coarse_kernel, coarse_taps, coarse_gain[None],
        coarse_steps.T, coarse_norm[None],
    )
    *prior, own, own_total, message = middle_stage("u", 2, own, own_total, prior, got)
    got = round_of(message, "z")
    second = fine_main(mine, gain, scans, ks, packs, first[3:], True)
    subs = last_stage(own, own_total, prior, got, l0, t0, later, later_total)
    states = [subs[0]] + [swapped(subs[m], m) for m in (1, 2, 3)]
    merged, end_rows = fine_close(
        (first[0], second[0]), (first[1], second[1]), (first[2], second[2]), mine, states, packs,
        merge_weight,
    )

    rim_a = passed(end_rows, ALL, [(q, q + 1) for q in range(1, 127, 2)])
    across = swapped(merged, 2)
    beside = swapped(merged, 1)
    rim_b = swapped(rim_a, 1)
    rim_y = swapped(own_rim(rim_a, beside), 2)
    rim_yc = swapped(rim_y, 1)
    both = swapped(across, 1)
    weights = (coarse_gate, coarse_value, coarse_scans)
    lead, tail, maps, share, run, run_log = coarse_main(
        "near", (merged, beside), weights, params, (rim_a, rim_b)
    )
    lead_1, tail_1, maps_1, share_1, run_1, run_log_1, ends_1 = coarse_main(
        "far_1", (across,), weights, params, (rim_y,)
    )
    lead_2, tail_2, maps_2, share_2, run_2, run_log_2, run_f, run_log_f, message = coarse_main(
        "far_2", (both,), weights, params,
        (ends_1, rim_yc, run, run_log, run_1, run_log_1),
    )
    got = lax.all_to_all(message, SEQ, split_axis=0, concat_axis=0, tiled=True)
    got = lax.all_to_all(prefix(got), SEQ, split_axis=0, concat_axis=0, tiled=True)
    norm = params[4]
    gn, ks, ss, sums = coarse_close(
        True, lead, tail, maps, got, run_f, run_log_f, norm, coarse_output
    )
    gn_f, ks_f, ss_f, sums_f = coarse_close(
        False, lead_1, lead_2, tail_1, tail_2, maps_1, maps_2, got, run, run_log,
        run_1, run_log_1, run_2, run_log_2, norm, coarse_output,
    )
    went, sums = relay(ks, sums, swapped(ss, 1))
    went = swapped(went, 2)
    went_f, sums_f = relay(ks_f, sums_f, swapped(ss_f, 1))
    went_f = swapped(went_f, 2)
    kk, sk = close_rest(gn, gn_f, coarse_output)
    sk = swapped(sk, 1)
    return final(share, share_1, share_2, kk, sk, sums, went_f, sums_f, went)


def solution(mesh):
    finer = Mesh(mesh.devices.reshape(4, 2, 4, 2, 2), ALL)
    cols = P(None, HEAD)
    return jax.shard_map(
        shards,
        mesh=finer,
        in_specs=(
            P(SEQ, None), P(), cols, cols, P(), cols, cols, P(), P(HEAD), P(HEAD), P(HEAD),
            P(HEAD, None), P(), P(), cols, cols, P(), cols, cols, P(), P(HEAD), P(HEAD), P(HEAD),
            P(HEAD, None),
        ),
        out_specs=P(SEQ, HEAD),
        check_vma=False,
    )
```

```python
import jax
import jax.numpy as jnp
from jax import lax
from jax.experimental import pallas as pl
from jax.experimental.pallas import tpu as pltpu
from jax.sharding import Mesh
from jax.sharding import PartitionSpec as P


SEQ = ("z", "u", "x")
HEAD = ("y", "c")
ALL = ("z", "u", "x", "y", "c")
EPSILON = 1e-05
BLK = 256
BF = jnp.bfloat16
F32 = jnp.float32
NN = (((1,), (0,)), ((), ()))
NT = (((1,), (1,)), ((), ()))
TN = (((0,), (0,)), ((), ()))


def dot(a, b, dims=NN):
    return lax.dot_general(a, b, dims, preferred_element_type=F32)


def parts(x):
    hi = x.astype(BF).astype(F32)
    rest = x - hi
    mid = rest.astype(BF).astype(F32)
    low = rest - mid
    return jnp.concatenate([hi, mid, low, jnp.zeros_like(x)], 0).astype(BF)


def decay_rows(row):
    hi = row.astype(BF).astype(F32)
    rest = row - hi
    mid = rest.astype(BF).astype(F32)
    low = rest - mid
    return jnp.concatenate([hi, mid, low, jnp.zeros((13, row.shape[1]), F32)], 0).astype(BF)


def of_rows(rows):
    rows = rows.astype(F32)
    return rows[0:1] + rows[1:2] + rows[2:3]


def iota(shape, dim):
    return lax.broadcasted_iota(jnp.int32, shape, dim)


def head_sel(width):
    return iota((8, width), 0) == iota((8, width), 1) // 64


def expander(width):
    r, lane = iota((32, width), 0), iota((32, width), 1)
    return jnp.where((r < 24) & (r % 8 == lane // 64), 1.0, 0.0).astype(BF)


def upper():
    return jnp.where(iota((BLK, BLK), 0) <= iota((BLK, BLK), 1), 1.0, 0.0).astype(BF)


def silu(v):
    h = v * 0.5
    return h + h * jnp.tanh(h)


def softplus(v):
    return jnp.maximum(v, 0.0) + jnp.log1p(jnp.exp(-jnp.abs(v)))


def rms(x, gain):
    x = x.astype(F32)
    return (x * lax.rsqrt(jnp.mean(x * x, axis=-1, keepdims=True) + EPSILON) * gain).astype(BF)


def cumulate(logs, tri):
    s = dot(parts(logs), tri)
    return s[0:8] + s[8:16] + s[16:24]


def spaced(length):
    return length // 8 + 1


def convolve(cv, act, half_taps, length):
    apart = spaced(length)

    def slab(c):
        taps = half_taps[c]
        rows = [cv[c, pl.ds(13 + i, 8, stride=apart), :] for i in range(3)]
        for i in range(apart):
            rows.append(cv[c, pl.ds(16 + i, 8, stride=apart), :])
            h = rows[i] * taps[0:1]
            for k in range(1, 4):
                h = h + rows[i + k] * taps[k : k + 1]
            act[c, pl.ds(i, 8, stride=apart), :] = h + h * jnp.tanh(h)

    for c in range(cv.shape[0]):
        slab(c)


def project(rows, weights, cv, start, slab):
    product = dot(rows, weights)
    for j in range(product.shape[1] // 128):
        cv[slab + j, start : start + rows.shape[0], :] = product[:, j * 128 : (j + 1) * 128]


def rounded(x):
    return x.astype(BF).astype(F32)


def small_rows(pack):
    rows = pack[384:416, :].astype(F32)
    kv = rows[0:4, 0:128] + rows[4:8, 0:128] + rows[8:12, 0:128]
    right = rows[0:16, 128:256]
    norm, b0, b1, d0, d1 = (of_rows(right[3 * j : 3 * j + 3]) for j in range(5))
    return kv, norm, jnp.concatenate([b0, b1], 0), jnp.concatenate([d0, d1], 0), rows[16:18]


def three(row):
    hi = row.astype(BF).astype(F32)
    rest = row - hi
    mid = rest.astype(BF).astype(F32)
    return [hi, mid, rest - mid]


def run_copies(pairs, sems):
    copies = [pltpu.make_async_copy(a, b, sems.at[j]) for j, (a, b) in enumerate(pairs)]
    for copy in copies:
        copy.start()
    return copies


def pack_kernel(
    bias, decay, gate, value, output, steps, kv, norm, tokens, gain, scans, ks,
    pack, ends, chunk, gain_v, scans_v, ks_v, kv_v, norm_v, steps_v, bias_v, decay_v, sems,
):
    copies = run_copies(
        (
            (kv, kv_v),
            (norm, norm_v),
            (steps, steps_v),
            (bias, bias_v),
            (decay, decay_v),
            (tokens.at[4080:4096], ends),
            (gate, pack.at[0:256, 0:128]),
            (value, pack.at[0:256, 128:256]),
            (output, pack.at[256:384]),
            (tokens.at[1008:2048], chunk),
            (gain, gain_v),
            (scans, scans_v),
            (ks, ks_v),
        ),
        sems,
    )
    for copy in copies[:5]:
        copy.wait()
    left = jnp.concatenate(three(kv_v[...]) + [jnp.zeros((4, 128), F32)], 0)
    rows = three(norm_v[...])
    for ref in (bias_v, decay_v):
        for j in range(2):
            rows = rows + three(jnp.broadcast_to(ref[:, j : j + 1], (1, 128)))
    right = jnp.concatenate(rows + [jnp.zeros((1, 128), F32)], 0)
    below = jnp.concatenate([steps_v[...].astype(F32), jnp.zeros((14, 256), F32)], 0)
    pack[384:416, :] = jnp.concatenate([jnp.concatenate([left, right], 1), below], 0).astype(BF)
    for copy in copies[5:]:
        copy.wait()


def packed(*args):
    return pl.pallas_call(
        pack_kernel,
        in_specs=[HBM] * 12,
        out_specs=[VM] * 6,
        out_shape=[
            sds((416, 256), BF),
            sds((16, 256), BF),
            sds((1040, 256), BF),
            sds((1, 256)),
            sds((256, 512), BF),
            sds((4, 512)),
        ],
        scratch_shapes=[
            pltpu.VMEM((4, 128), F32),
            pltpu.VMEM((1, 128), F32),
            pltpu.VMEM((2, 256), BF),
            pltpu.VMEM((1, 2), F32),
            pltpu.VMEM((1, 2), F32),
            pltpu.SemaphoreType.DMA((13,)),
        ],
        compiler_params=few(4),
        name="pack",
    )(*in_hbm(*args))


def params_kernel(bias, decay, kv, ks, gain, steps, norm, taps, both, *refs):
    outs, kv_v, ks_v, bias_v, decay_v, sems = refs[:3], *refs[3:]
    copies = run_copies(
        (
            (kv, kv_v), (ks, ks_v), (bias, bias_v), (decay, decay_v),
            (gain, outs[0]), (steps, outs[1]), (norm, outs[2]),
        ),
        sems,
    )
    for copy in copies:
        copy.wait()
    for j in range(4):
        cols = slice(j * 128, (j + 1) * 128)
        taps[j] = kv_v[:, cols] * 0.5
        taps[4 + j] = ks_v[:, cols] * 0.5
    rows = [
        jnp.broadcast_to(ref[:, j : j + 1], (1, 128)) for ref in (bias_v, decay_v) for j in range(8)
    ]
    both[...] = jnp.concatenate(rows, 0)


def coarse_params(bias, decay, kv, ks, gain, steps, norm):
    return pl.pallas_call(
        params_kernel,
        in_specs=[HBM] * 7,
        out_specs=[VM] * 5,
        out_shape=[
            sds((8, 4, 128)), sds((16, 128)), sds((1, 1024)), sds((8, 1024), BF), sds((1, 512)),
        ],
        scratch_shapes=[
            pltpu.VMEM((4, 512), F32),
            pltpu.VMEM((4, 512), F32),
            pltpu.VMEM((1, 8), F32),
            pltpu.VMEM((1, 8), F32),
            pltpu.SemaphoreType.DMA((7,)),
        ],
        compiler_params=few(4),
        name="coarse_params",
    )(*in_hbm(bias, decay, kv, ks, gain, steps, norm))


def state_chunk(x, gain, pack, scans, ks, taps, cv, act):
    kv, _, bias, decay, steps = small_rows(pack)
    pad = jnp.zeros((6, 128), F32)
    bias = jnp.concatenate([bias, pad], 0)[:, 0:1]
    decay = jnp.concatenate([decay, pad], 0)[:, 0:1]
    steps = jnp.concatenate([steps, jnp.zeros((6, 256), F32)], 0).astype(BF)
    wv, wb = pack[0:256, 128:256], scans[:, 0:256]
    taps[0] = kv * 0.5
    taps[1] = ks[:, 0:128] * 0.5
    taps[2] = ks[:, 128:256] * 0.5
    normed = rms(x, gain[...])
    project(normed, wv, cv, 0, 0)
    project(normed, wb, cv, 0, 1)
    raw = dot(steps, normed[16:1040], NT)
    convolve(cv, act, taps, 1024)
    dt = softplus(raw + bias)
    logs = -dt * decay
    tri = upper()
    carry = jnp.zeros((8, 1), F32)
    pieces = []
    for b in range(4):
        piece = cumulate(logs[:, b * BLK : (b + 1) * BLK], tri) + carry
        carry = piece[:, BLK - 1 : BLK]
        pieces.append(piece)
    cum = jnp.concatenate(pieces, 1)
    tail = jnp.exp(carry - cum) * dt
    spread = dot(parts(tail), expander(128), TN)
    scaled = (act[0, 0:1024] * spread).astype(BF)
    maps = jnp.concatenate([act[1, 0:1024].astype(BF), act[2, 0:1024].astype(BF)], 1)
    local = dot(scaled, maps, TN).T
    total = jnp.sum(
        jnp.where(head_sel(128), jnp.broadcast_to(carry, (8, 128)), 0.0), axis=0, keepdims=True
    )
    return local, total


def later_chunks_kernel(
    tokens, chunk_0, gain, pack, scans, ks,
    local, total, x0, mine, mine_rim, xs, taps, cv, act, sems, x_sems,
):
    i = pl.program_id(0)
    start = pl.multiple_of(lax.axis_index(HEAD) * 1024, 1024)
    early = pl.multiple_of(jnp.maximum(start - 16, 0), 16)
    mine_pairs = (
        (tokens.at[0:1024], x0),
        (tokens.at[pl.ds(start, 1024)], mine),
        (tokens.at[pl.ds(early, 16)], mine_rim),
    )

    def chunk(j):
        begin_row = pl.multiple_of((j + 1) * 1024 - 16, 16)
        return pltpu.make_async_copy(tokens.at[pl.ds(begin_row, 1040)], xs.at[j], x_sems.at[j])

    @pl.when(i == 0)
    def _():
        chunk(1).start()
        chunk(2).start()
        for j, (a, b) in enumerate(mine_pairs):
            pltpu.make_async_copy(a, b, sems.at[j]).start()
        xs[0] = chunk_0[...]

    @pl.when(i > 0)
    def _():
        chunk(i).wait()

    state, logs = state_chunk(xs[i], gain, pack, scans, ks, taps, cv, act)
    local[i] = state
    total[i] = jnp.broadcast_to(logs, (8, 128))

    @pl.when(i == 2)
    def _():
        for j, (a, b) in enumerate(mine_pairs):
            pltpu.make_async_copy(a, b, sems.at[j]).wait()


def first_chunk_kernel(
    x, rim, gain, pack, scans, ks, later, later_total,
    local, total, whole, whole_total, message, taps, cv, act,
):
    rows = jnp.concatenate([rim[...], x[...]], 0)
    state, logs = state_chunk(rows, gain, pack, scans, ks, taps, cv, act)
    local[...] = state
    total[...] = jnp.broadcast_to(logs, (8, 128))
    for j in range(3):
        piece = later_total[j, 0:1, :]
        state = state * jnp.exp(piece) + later[j]
        logs = logs + piece
    whole[...] = state
    whole_total[...] = jnp.broadcast_to(logs, (8, 128))
    message[0:256, :] = state.astype(BF)
    message[256:272, :] = decay_rows(logs)


def sds(shape, dtype=F32):
    return jax.ShapeDtypeStruct(shape, dtype)


def in_hbm(*arrays):
    return [pltpu.with_memory_space_constraint(a, pltpu.HBM) for a in arrays]


def few(mib):
    return pltpu.CompilerParams(vmem_limit_bytes=mib << 20)


VM = pl.BlockSpec(memory_space=pltpu.VMEM)
HBM = pl.BlockSpec(memory_space=pltpu.HBM)


def fine_states(tokens, chunk, ends_from, gain, pack, scans, ks):
    scratch = [
        pltpu.VMEM((3, 4, 128), F32),
        pltpu.VMEM((3, 1048, 128), F32),
        pltpu.VMEM((3, 1032, 128), F32),
    ]
    later, later_total, x0, *mine = pl.pallas_call(
        later_chunks_kernel,
        grid=(3,),
        in_specs=[HBM] + [VM] * 5,
        out_specs=[VM] * 5,
        out_shape=[
            sds((3, 256, 128)),
            sds((3, 8, 128)),
            sds((1024, 256), BF),
            sds((1024, 256), BF),
            sds((16, 256), BF),
        ],
        scratch_shapes=[pltpu.VMEM((3, 1040, 256), BF)]
        + scratch
        + [pltpu.SemaphoreType.DMA((3,)), pltpu.SemaphoreType.DMA((3,))],
        compiler_params=few(16),
        name="later_chunks",
    )(*in_hbm(tokens), chunk, gain, pack, scans, ks)
    first = pl.pallas_call(
        first_chunk_kernel,
        in_specs=[VM] * 8,
        out_specs=[VM] * 5,
        out_shape=[
            sds((256, 128)),
            sds((8, 128)),
            sds((256, 128)),
            sds((8, 128)),
            sds((272, 128), BF),
        ],
        scratch_shapes=scratch,
        compiler_params=few(16),
        name="first_chunk",
    )(x0, ends_from, gain, pack, scans, ks, later, later_total)
    return later, later_total, mine, first


def combine(i, count, own, own_total, prior, prior_total, received):
    state = jnp.zeros_like(own)
    logs = jnp.zeros_like(own_total)
    zero = jnp.zeros((), F32)
    got = [(r[0:256, :].astype(F32), of_rows(r[256:272, :])) for r in received]
    for k in range(count - 1, 0, -1):
        s, l = got[k - 1]
        valid = i >= k
        state = jnp.where(valid, state * jnp.exp(l) + s, state)
        logs = jnp.where(valid, logs + l, logs)
    new_prior = state * jnp.exp(prior_total) + prior
    new_prior_total = logs + prior_total
    state = state * jnp.exp(own_total) + own
    logs = logs + own_total
    for m in range(1, count):
        s, l = got[count - m - 1]
        valid = i + m < count
        state = jnp.where(valid, state * jnp.exp(l) + s, state)
        logs = jnp.where(valid, logs + l, logs)
    return new_prior, new_prior_total, state, logs


def middle_kernel(axis, count, fresh, own, own_total, *refs):
    if fresh:
        prior, prior_total = jnp.zeros((256, 128), F32), jnp.zeros((1, 128), F32)
    else:
        prior, prior_total, refs = refs[0][...], refs[1][0:1, :], refs[2:]
    received, (np_ref, npt_ref, ns_ref, nst_ref, message) = refs[: count - 1], refs[count - 1 :]
    p, pt, s, st = combine(
        lax.axis_index(axis), count, own[...], own_total[0:1, :], prior, prior_total, received
    )
    np_ref[...] = p
    npt_ref[...] = jnp.broadcast_to(pt, (8, 128))
    ns_ref[...] = s
    nst_ref[...] = jnp.broadcast_to(st, (8, 128))
    message[0:256, :] = s.astype(BF)
    message[256:272, :] = decay_rows(st)


def middle_stage(axis, count, own, own_total, prior, received):
    return pl.pallas_call(
        lambda *refs: middle_kernel(axis, count, not prior, *refs),
        in_specs=[VM] * (2 + len(prior) + len(received)),
        out_specs=[VM] * 5,
        out_shape=[
            sds((256, 128)),
            sds((8, 128)),
            sds((256, 128)),
            sds((8, 128)),
            sds((272, 128), BF),
        ],
        compiler_params=few(4),
    )(own, own_total, *prior, *received)


def last_kernel(own, own_total, prior, prior_total, r1, r2, r3, l0, t0, later, later_total,
                o0, o1, o2, o3, sub):
    p, _, _, _ = combine(
        lax.axis_index("z"), 4, own[...], own_total[0:1, :], prior[...], prior_total[0:1, :],
        (r1, r2, r3),
    )
    sub[0] = p
    p = p * jnp.exp(t0[0:1, :]) + l0[...]
    sub[1] = p
    for j in range(2):
        p = p * jnp.exp(later_total[j, 0:1, :]) + later[j]
        sub[j + 2] = p
    h = lax.axis_index(HEAD)
    for k, out in enumerate((o0, o1, o2, o3)):
        out[...] = sub[h ^ k].astype(BF)


def last_stage(own, own_total, prior, received, l0, t0, later, later_total):
    return pl.pallas_call(
        last_kernel,
        in_specs=[VM] * 11,
        out_specs=[VM] * 4,
        out_shape=[sds((256, 128), BF)] * 4,
        scratch_shapes=[pltpu.VMEM((4, 256, 128), F32)],
        compiler_params=few(6),
        name="chain_last",
    )(own, own_total, *prior, *received, l0, t0, later, later_total)


def scan_block(
    fresh, normed, wg, wv, ws, wst, taps, bias, decay,
    lead, tail_out, maps_out, cv, act, sc, spread, scaled, run, run_log,
):
    project(normed, wv[...], cv, 0, 0)
    project(normed, ws[...], cv, 0, 4)
    normed = normed[16:272]
    tail_out[...] = silu(dot(normed, wg[...]))
    convolve(cv, act, taps, BLK)
    raw = dot(wst[...], normed, NT)
    dt = softplus(raw + bias[...])
    logs = -dt * decay[...]
    cum = cumulate(logs, upper())
    last = cum[:, BLK - 1 : BLK]
    stacked = [jnp.exp(cum), jnp.exp(last - cum) * dt]
    if fresh:
        run_log[...] = jnp.broadcast_to(last, (8, 128))
    else:
        stacked = [jnp.exp(cum + run_log[:, 0:1])] + stacked
        run_log[...] = run_log[...] + last
    first = 256 * (len(stacked) - 2)
    spread[0 : first + 512, :] = dot(parts(jnp.concatenate(stacked, 1)), expander(512), TN)
    columns = dot(parts(cum), jnp.where(
        (iota((32, 128), 0) < 24) & (iota((32, 128), 0) % 8 == iota((32, 128), 1)), 1.0, 0.0
    ).astype(BF), TN)
    rows = cum - jnp.log(dt)
    in_map = jnp.concatenate([act[4, 0:BLK].astype(BF), act[5, 0:BLK].astype(BF)], 1)
    out_map = jnp.concatenate([act[6, 0:BLK].astype(BF), act[7, 0:BLK].astype(BF)], 1)
    maps_out[...] = out_map
    sc[...] = dot(out_map, in_map, NT)
    if not fresh:
        lead[...] = spread[256:512, :] * dot(out_map, run[...].astype(BF))
    low_tri = iota((128, 128), 0) >= iota((128, 128), 1)
    lane_low = iota((BLK, 128), 1) < 64
    for p in range(4):
        cols = slice(p * 128, (p + 1) * 128)
        vals = act[p, 0:BLK]
        v0 = jnp.where(lane_low, vals, 0.0).astype(BF)
        v1 = jnp.where(lane_low, 0.0, vals).astype(BF)
        upper_w, lower_w = [], []
        for h in (2 * p, 2 * p + 1):
            c0, c1 = columns[0:128, h : h + 1], columns[128:256, h : h + 1]
            r0, r1 = rows[h : h + 1, 0:128], rows[h : h + 1, 128:256]
            upper_w.append(
                (sc[0:128, 0:128] * jnp.exp(jnp.where(low_tri, c0 - r0, -jnp.inf))).astype(BF)
            )
            lower_w.append((sc[128:256, 0:128] * jnp.exp(c1 - r0)).astype(BF))
            lower_w.append(
                (sc[128:256, 128:256] * jnp.exp(jnp.where(low_tri, c1 - r1, -jnp.inf))).astype(BF)
            )
        top = dot(
            jnp.concatenate(upper_w, 1), jnp.concatenate([v0[0:128], v1[0:128]], 0)
        )
        bottom = dot(jnp.concatenate(lower_w, 1), jnp.concatenate([v0, v1], 0))
        gate = tail_out[:, cols]
        if not fresh:
            top = top + lead[0:128, cols]
            bottom = bottom + lead[128:256, cols]
        lead[0:128, cols] = top * gate[0:128]
        lead[128:256, cols] = bottom * gate[128:256]
        tail_out[:, cols] = spread[0:256, cols] * gate
        scaled[:, cols] = (vals * spread[first + 256 : first + 512, cols]).astype(BF)
    local = dot(in_map, scaled[...], TN)
    run[...] = local if fresh else run[...] * spread[511:512, :] + local


SCAN_SCRATCH = [
    pltpu.VMEM((8, 280, 128), F32),
    pltpu.VMEM((8, BLK + 8, 128), F32),
    pltpu.VMEM((BLK, BLK), F32),
    pltpu.VMEM((768, 512), F32),
    pltpu.VMEM((256, 512), BF),
]


def fine_main_kernel(at, mine, gain, ws, *refs):
    later = at > 0
    if later:
        x0, x1, wg, wv, wst, taps, bias, decay, lead, tail_out, maps_out, run, run_log = refs[:13]
    else:
        ks, p0, p1, p2, p3, x0, x1, lead, tail_out, maps_out, run, run_log = refs[:12]
        wg, wv, wst, taps, bias, decay = refs[12:18]
    cv, act, sc, spread, scaled = refs[-5:]
    i = pl.program_id(0)

    @pl.when(i == 0)
    def _():
        if later:
            run[...] = x0[...]
            run_log[...] = x1[...]
            return
        run[...] = jnp.zeros_like(run)
        run_log[...] = jnp.zeros_like(run_log)
        for j in range(4):
            taps[4 + j] = ks[:, j * 128 : (j + 1) * 128] * 0.5
        for j, p in enumerate((p0, p1, p2, p3)):
            cols = slice(j * 128, (j + 1) * 128)
            two = slice(2 * j, 2 * j + 2)
            wg[:, cols] = p[0:256, 0:128]
            wv[:, cols] = p[0:256, 128:256]
            kv, _, bias[two, :], decay[two, :], wst[two, :] = small_rows(p)
            taps[j] = kv * 0.5

    start = pl.multiple_of((i + at) * BLK, BLK)
    rim = mine[pl.ds(pl.multiple_of(jnp.maximum(start - 16, 0), 16), 16), :].astype(F32)
    if not later:
        edge = jnp.where(lax.axis_index(HEAD) == 0, x0[...].astype(F32), x1[...].astype(F32))
        rim = jnp.where(i == 0, edge, rim)
    x = jnp.concatenate([rim, mine[pl.ds(start, BLK), :].astype(F32)], 0)
    scan_block(
        False, rms(x, gain[...]), wg, wv, ws, wst[...].astype(BF), taps, bias[:, 0:1],
        decay[:, 0:1], lead, tail_out, maps_out, cv, act, sc, spread, scaled, run, run_log,
    )


def fine_main(at, blocks, *args):
    length = blocks * BLK
    rows = [pl.BlockSpec((BLK, n), lambda i: (i, 0)) for n in (512, 512, 256)]
    weights = []
    if at == 0:
        weights = [
            sds((256, 512), BF), sds((256, 512), BF), sds((8, 256)), sds((8, 4, 128)),
            sds((8, 128)), sds((8, 128)),
        ]
    return pl.pallas_call(
        lambda *refs: fine_main_kernel(at, *refs),
        grid=(blocks,),
        in_specs=[VM] * len(args),
        out_specs=rows + [VM] * (2 + len(weights)),
        out_shape=[
            sds((length, 512)), sds((length, 512)), sds((length, 256), BF),
            sds((256, 512)), sds((8, 128)),
        ]
        + weights,
        scratch_shapes=SCAN_SCRATCH,
        compiler_params=few(16),
    )(*args)


def fine_close_kernel(
    lead_a, lead_b, lead_c, tail_a, tail_b, tail_c, maps_a, maps_b, maps_c, x, s0, s1, s2, s3, p0, p1, p2, p3, merge,
    merged, end_rows, lead, tail, maps, hidden, state, wo, norm,
):
    i = pl.program_id(0)

    @pl.when(i < 2)
    def _():
        lead[...], tail[...], maps[...] = lead_a[...], tail_a[...], maps_a[...]

    @pl.when(i == 2)
    def _():
        lead[...], tail[...], maps[...] = lead_b[...], tail_b[...], maps_b[...]

    @pl.when(i == 3)
    def _():
        lead[...], tail[...], maps[...] = lead_c[...], tail_c[...], maps_c[...]

    @pl.when(i == 0)
    def _():
        for j, (s, p) in enumerate(zip((s0, s1, s2, s3), (p0, p1, p2, p3))):
            cols = slice(j * 128, (j + 1) * 128)
            state[:, cols] = s[...]
            wo[cols, :] = p[256:384, :]
            norm[:, cols] = small_rows(p)[1]

    gated = lead[...] + tail[...] * dot(maps[...], state[...])
    factor = lax.rsqrt(jnp.sum(gated * gated, axis=1, keepdims=True) / 512.0 + EPSILON)
    out = x[...].astype(F32)
    total = dot((gated * factor * norm[...]).astype(BF), wo[...])
    start = pl.multiple_of(i * BLK, BLK)
    hidden[0, pl.ds(start, BLK), :] = rounded(out[:, 0:128] + total[:, 0:128])
    hidden[1, pl.ds(start, BLK), :] = rounded(out[:, 128:256] + total[:, 128:256])

    @pl.when(i == pl.num_programs(0) - 1)
    def _():
        total = None
        for odd in range(2):
            rows = [
                hidden[half, pl.ds(odd, 512, stride=2), :].reshape(8, 2, 32, 128)
                for half in range(2)
            ]
            for line in range(2):
                tile = [r[:, line].reshape(256, 128).astype(BF) for r in rows]
                at = (2 * line + odd) * 256
                piece = dot(jnp.concatenate(tile, 1), merge[at : at + 256, :])
                total = piece if total is None else total + piece
        result = total.astype(BF)
        merged[...] = result
        end_rows[...] = result[240:256]


def fine_close(leads, tails, maps, x, states, packs, merge):
    def halves(width):
        return [
            pl.BlockSpec((BLK, width), lambda i: (jnp.minimum(i, 1), 0)),
            pl.BlockSpec((BLK, width), lambda i: (0, 0)),
            pl.BlockSpec((BLK, width), lambda i: (0, 0)),
        ]

    return pl.pallas_call(
        fine_close_kernel,
        grid=(4,),
        in_specs=halves(512)
        + halves(512)
        + halves(256)
        + [pl.BlockSpec((BLK, 256), lambda i: (i, 0))]
        + [VM] * 9,
        out_specs=[VM] * 2,
        scratch_shapes=[
            pltpu.VMEM((BLK, 512), F32),
            pltpu.VMEM((BLK, 512), F32),
            pltpu.VMEM((BLK, 256), BF),
            pltpu.VMEM((2, 1024, 128), F32),
            pltpu.VMEM((256, 512), BF),
            pltpu.VMEM((512, 256), BF),
            pltpu.VMEM((1, 512), F32),
        ],
        out_shape=[sds((256, 1024), BF), sds((16, 1024), BF)],
        compiler_params=few(16),
        name="fine_close",
    )(*leads, *tails, *maps, x, *states, *packs, merge)


def in_order(first, a, a_log, b, b_log):
    lead_log = jnp.where(first, b_log, a_log)
    row = jnp.exp(spread_row(lead_log))
    return jnp.where(first, a, b) * row + jnp.where(first, b, a), a_log + b_log


def coarse_main_kernel(kind, pieces, gain, wg, wv, ws, wst, taps, both, *refs):
    qs, refs = refs[:pieces], refs[pieces:]
    xs, sems, rims, cv, act, sc, spread, scaled = refs[-8:]
    y, c = lax.axis_index("y"), lax.axis_index("c")
    h = 2 * y + c
    if kind == "near":
        ra, rb, lead, tail_out, maps_out, share, run, run_log = refs[:-8]
    elif kind == "far_1":
        re, lead, tail_out, maps_out, share, run, run_log, ends = refs[:-8]
    else:
        (
            ends_1, rd, near_run, near_log, run_1, run_log_1,
            lead, tail_out, maps_out, share, run, run_log, far_run, far_log, message,
        ) = refs[:-8]
    i = pl.program_id(0)

    @pl.when(i == 0)
    def _():
        if kind == "near":
            copies = run_copies(((qs[0], xs.at[c]), (qs[1], xs.at[1 - c])), sems)
            rim = jnp.where(c == 0, ra[...].astype(F32), rb[...].astype(F32))
        else:
            copies = run_copies(((qs[0], xs.at[0]),), sems)
            rim = re[...].astype(F32) if kind == "far_1" else rd[...].astype(F32)
            if kind == "far_2":
                rim = jnp.where(c == 0, ends_1[...].astype(F32), rim)
        rims[...] = rim
        if kind == "near":
            run[...] = jnp.zeros_like(run)
            run_log[...] = jnp.zeros_like(run_log)
        for copy in copies:
            copy.wait()
        if kind == "far_1":
            ends[...] = xs[0, 240:256, :]

    share[...] = xs[i, :, pl.ds(pl.multiple_of(h * 256, 256), 256)]
    rim = rims[...]
    if kind == "near":
        rim = jnp.where(i == 0, rim, xs[0, 240:256, :].astype(F32))
    x = jnp.concatenate([rim, xs[i].astype(F32)], 0)
    scan_block(
        kind != "near", rms(x, gain[...]), wg, wv, ws, wst[...], taps, both[0:8, 0:1],
        both[8:16, 0:1], lead, tail_out, maps_out, cv, act, sc, spread, scaled, run, run_log,
    )

    if kind == "far_2":
        log_1, log_2, log_n = run_log_1[:, 0:1], run_log[:, 0:1], near_log[:, 0:1]
        far, log_f = in_order(c == 0, run_1[...], log_1, run[...], log_2)
        far_run[...] = far
        far_log[...] = jnp.broadcast_to(log_f, (8, 128))
        total, log = in_order(y == 0, near_run[...], log_n, far, log_f)
        extra = decay_rows(spread_row(log))[0:8]
        for n in range(16):
            for half in range(2):
                cols = slice(half * 256, (half + 1) * 256)
                message[2 * n + half, 0:16, :] = total[n * 16 : (n + 1) * 16, cols].astype(BF)
                message[2 * n + half, 16:24, :] = extra[:, cols]


def spread_row(column):
    return jnp.sum(
        jnp.where(head_sel(512), jnp.broadcast_to(column, (8, 512)), 0.0), axis=0, keepdims=True
    )


ANY = pl.BlockSpec(memory_space=pl.ANY)


def coarse_main(kind, pieces, weights, params, extra):
    taps, both, gain, wst, _ = params
    blocks = len(pieces)
    length = blocks * BLK
    rows = [pl.BlockSpec((BLK, n), lambda i: (i, 0)) for n in (512, 512, 256, 256)]
    last = []
    if kind == "far_1":
        last = [sds((16, 1024), BF)]
    elif kind == "far_2":
        last = [sds((256, 512)), sds((8, 128)), sds((32, 24, 256), BF)]
    return pl.pallas_call(
        lambda *refs: coarse_main_kernel(kind, blocks, *refs),
        grid=(blocks,),
        in_specs=[VM] * 7 + [ANY] * blocks + [VM] * len(extra),
        out_specs=rows + [VM] * (2 + len(last)),
        out_shape=[
            sds((length, 512)),
            sds((length, 512)),
            sds((length, 256), BF),
            sds((length, 256), BF),
            sds((256, 512)),
            sds((8, 128)),
        ]
        + last,
        scratch_shapes=[
            pltpu.VMEM((blocks, 256, 1024), BF),
            pltpu.SemaphoreType.DMA((blocks,)),
            pltpu.VMEM((16, 1024), F32),
        ]
        + SCAN_SCRATCH,
        compiler_params=few(16),
    )(gain, *weights, wst, taps, both, *pieces, *extra)


def own_rim_kernel(came, beside, out):
    out[...] = jnp.where(
        lax.axis_index("c") == 0, came[...].astype(F32), beside[240:256, :].astype(F32)
    ).astype(BF)


def own_rim(came, beside):
    return pl.pallas_call(
        own_rim_kernel,
        in_specs=[VM] * 2,
        out_specs=VM,
        out_shape=sds((16, 1024), BF),
        compiler_params=few(4),
        name="own_rim",
    )(came, beside)


def prefix_kernel(got, out):
    state = jnp.zeros((16, 256), F32)
    for d in range(32):
        out[d] = state.astype(BF)
        state = state * jnp.exp(of_rows(got[d, 16:24, :])) + got[d, 0:16, :].astype(F32)


def prefix(got):
    return pl.pallas_call(
        prefix_kernel,
        in_specs=[VM],
        out_specs=VM,
        out_shape=sds((32, 16, 256), BF),
        compiler_params=few(4),
        name="prefix",
    )(got)


def coarse_close_kernel(near, *refs):
    if near:
        lead, tail, maps, got, far_run, far_log, norm, wo, *refs = refs
    else:
        leads, tails, mapss = refs[0:2], refs[2:4], refs[4:6]
        got, near_run, near_log, run_1, log_1, run_2, log_2, norm, wo, *refs = refs[6:]
    gn, ks, ss, square_sums, states, sums = refs
    y, c = lax.axis_index("y"), lax.axis_index("c")
    h = 2 * y + c
    came = jnp.concatenate(
        [jnp.concatenate([got[2 * n], got[2 * n + 1]], 1) for n in range(16)], 0
    ).astype(F32)

    def after(state, cond, run, log):
        row = jnp.exp(spread_row(log[:, 0:1]))
        return jnp.where(cond, state * row + run[...], state)

    if near:
        states[0] = after(came, y == 1, far_run, far_log).astype(BF)
    else:
        came = after(came, y == 0, near_run, near_log)
        states[0] = after(came, c == 1, run_2, log_2).astype(BF)
        states[1] = after(came, c == 0, run_1, log_1).astype(BF)
    ones = jnp.ones((8, 512), BF)
    for i in range(2):
        if near:
            rows = slice(i * BLK, (i + 1) * BLK)
            gated = lead[rows] + tail[rows] * dot(maps[rows], states[0])
            place = i
        else:
            gated = leads[i][...] + tails[i][...] * dot(mapss[i][...], states[i])
            place = jnp.bitwise_xor(c, i)
        sq = gated * gated
        hi = sq.astype(BF)
        low = (sq - hi.astype(F32)).astype(BF)
        sums[place] = dot(ones, hi, NT) + dot(ones, low, NT)
        scaled = (gated * norm[...]).astype(BF)
        at = pl.ds(pl.multiple_of(place * BLK, BLK), BLK)
        gn[at, :] = scaled
        for k, out in ((2, ks), (3, ss)):
            col = pl.multiple_of((h ^ k) * 256, 256)
            out[at, :] = dot(scaled, wo[:, pl.ds(col, 256)]).astype(BF)
    square_sums[...] = jnp.concatenate([sums[0], sums[1]], 1)
    ss[512:528, :] = sum_rows(sums[0, 0:1], sums[1, 0:1])


def coarse_close(near, *args):
    return pl.pallas_call(
        lambda *refs: coarse_close_kernel(near, *refs),
        in_specs=[VM] * len(args),
        out_specs=[VM] * 4,
        out_shape=[
            sds((512, 512), BF), sds((512, 256), BF), sds((528, 256), BF), sds((8, 512)),
        ],
        scratch_shapes=[pltpu.VMEM((2, 256, 512), BF), pltpu.VMEM((2, 8, 256), F32)],
        compiler_params=few(12),
        name="coarse_close_near" if near else "coarse_close_far",
    )(*args)


def close_rest_kernel(near, far, wo, kk, sk):
    h = lax.axis_index(HEAD)
    for k, out in enumerate((kk, sk)):
        col = pl.multiple_of((h ^ k) * 256, 256)
        for j, ref in enumerate((near, far)):
            out[j * 512 : (j + 1) * 512, :] = dot(ref[...], wo[:, pl.ds(col, 256)]).astype(BF)


def close_rest(near, far, wo):
    return pl.pallas_call(
        close_rest_kernel,
        in_specs=[VM] * 3,
        out_specs=[VM] * 2,
        out_shape=[sds((1024, 256), BF)] * 2,
        compiler_params=few(8),
        name="close_rest",
    )(near, far, wo)


def sum_rows(a, b):
    return jnp.concatenate(three(a) + three(b) + [jnp.zeros((10, 256), F32)], 0).astype(BF)


def rows_sum(ref):
    rows = ref[512:528, :].astype(F32)
    return jnp.concatenate([of_rows(rows[0:3]), of_rows(rows[3:6])], 1)


def relay_kernel(ks, square_sums, came, out, sums):
    out[0:512, :] = (ks[...].astype(F32) + came[0:512, :].astype(F32)).astype(BF)
    total = square_sums[0:1, :] + rows_sum(came)
    out[512:528, :] = sum_rows(total[:, 0:256], total[:, 256:512])
    sums[...] = jnp.broadcast_to(total, (8, 512))


def relay(ks, square_sums, came):
    return pl.pallas_call(
        relay_kernel,
        in_specs=[VM] * 3,
        out_specs=[VM] * 2,
        out_shape=[sds((528, 256), BF), sds((8, 512))],
        compiler_params=few(4),
    )(ks, square_sums, came)


def final_kernel(share, share_1, share_2, kk, sk, sum_a, far_a, sum_b, far_b, out):
    y, c = lax.axis_index("y"), lax.axis_index("c")
    pick = jnp.where(iota((32, 256), 0) % 8 == 0, 1.0, 0.0).astype(BF)
    for side, (half, sums, far) in enumerate(((y, sum_a, far_a), (1 - y, sum_b, far_b))):
        total = sums[...] + rows_sum(far)
        factor = lax.rsqrt(total / 2048.0 + EPSILON)
        for b in range(2):
            rows = slice(b * BLK, (b + 1) * BLK)
            here = slice(side * 512 + b * BLK, side * 512 + (b + 1) * BLK)
            spread = dot(parts(factor[:, rows]), pick, TN)
            total = kk[here].astype(F32) + sk[here].astype(F32) + far[rows].astype(F32)
            if side == 0:
                own = share[rows].astype(F32)
            else:
                own = jnp.where(c == b, share_1[...].astype(F32), share_2[...].astype(F32))
            at = pl.multiple_of(half * 512 + b * BLK, BLK)
            out[pl.ds(at, BLK), :] = (own + total * spread).astype(BF)


def final(*args):
    return pl.pallas_call(
        final_kernel,
        in_specs=[VM] * 9,
        out_specs=VM,
        out_shape=sds((1024, 256), BF),
        compiler_params=few(8),
        name="final",
    )(*args)


def passed(x, axes, pairs):
    return lax.ppermute(x, axes, pairs)


def swapped(x, mask):
    return passed(x, HEAD, [(j, j ^ mask) for j in range(4)])


def round_of(x, axis):
    got = []
    for k in (1, 2, 3):
        got.append(passed(x, axis, [(j, (j + k) % 4) for j in range(4)]))
    return got


def shards(
    tokens, fine_gain, fine_gate, fine_value, fine_scans, fine_steps, fine_kernel, fine_taps,
    fine_bias, fine_decay, fine_norm, fine_output, merge_weight, coarse_gain, coarse_gate,
    coarse_value, coarse_scans, coarse_steps, coarse_kernel, coarse_taps, coarse_bias,
    coarse_decay, coarse_norm, coarse_output,
):
    pack, ends, chunk, gain, scans, ks = packed(
        fine_bias[None], fine_decay[None], fine_gate, fine_value, fine_output, fine_steps.T,
        fine_kernel, fine_norm[None], tokens, fine_gain[None], fine_scans, fine_taps,
    )
    rim = passed(ends, SEQ, [(i, i + 1) for i in range(31)])
    packs = [pack] + [swapped(pack, m) for m in (1, 2, 3)]
    later, later_total, (mine, mine_rim), (l0, t0, own, own_total, message) = fine_states(
        tokens, chunk, rim, gain, pack, scans, ks
    )
    got = round_of(message, "x")
    first = fine_main(0, 2, mine, gain, scans, ks, *packs, rim, mine_rim)
    *prior, own, own_total, message = middle_stage("x", 4, own, own_total, (), got)
    got = [passed(message, "u", [(0, 1), (1, 0)])]
    params = coarse_params(
        coarse_bias[None], coarse_decay[None], coarse_kernel, coarse_taps, coarse_gain[None],
        coarse_steps.T, coarse_norm[None],
    )
    second = fine_main(2, 1, mine, gain, scans, *first[3:])
    *prior, own, own_total, message = middle_stage("u", 2, own, own_total, prior, got)
    got = round_of(message, "z")
    third = fine_main(3, 1, mine, gain, scans, *second[3:], *first[5:])
    subs = last_stage(own, own_total, prior, got, l0, t0, later, later_total)
    states = [subs[0]] + [swapped(subs[m], m) for m in (1, 2, 3)]
    merged, end_rows = fine_close(
        *([call[j] for call in (first, second, third)] for j in range(3)), mine, states, packs,
        merge_weight,
    )

    rim_a = passed(end_rows, ALL, [(q, q + 1) for q in range(1, 127, 2)])
    across = swapped(merged, 2)
    beside = swapped(merged, 1)
    rim_b = swapped(rim_a, 1)
    rim_y = swapped(own_rim(rim_a, beside), 2)
    rim_yc = swapped(rim_y, 1)
    both = swapped(across, 1)
    weights = (coarse_gate, coarse_value, coarse_scans)
    lead, tail, maps, share, run, run_log = coarse_main(
        "near", (merged, beside), weights, params, (rim_a, rim_b)
    )
    lead_1, tail_1, maps_1, share_1, run_1, run_log_1, ends_1 = coarse_main(
        "far_1", (across,), weights, params, (rim_y,)
    )
    lead_2, tail_2, maps_2, share_2, run_2, run_log_2, run_f, run_log_f, message = coarse_main(
        "far_2", (both,), weights, params,
        (ends_1, rim_yc, run, run_log, run_1, run_log_1),
    )
    got = lax.all_to_all(message, SEQ, split_axis=0, concat_axis=0, tiled=True)
    got = lax.all_to_all(prefix(got), SEQ, split_axis=0, concat_axis=0, tiled=True)
    norm = params[4]
    gn, ks, ss, sums = coarse_close(
        True, lead, tail, maps, got, run_f, run_log_f, norm, coarse_output
    )
    gn_f, ks_f, ss_f, sums_f = coarse_close(
        False, lead_1, lead_2, tail_1, tail_2, maps_1, maps_2, got, run, run_log,
        run_1, run_log_1, run_2, run_log_2, norm, coarse_output,
    )
    went, sums = relay(ks, sums, swapped(ss, 1))
    went = swapped(went, 2)
    went_f, sums_f = relay(ks_f, sums_f, swapped(ss_f, 1))
    went_f = swapped(went_f, 2)
    kk, sk = close_rest(gn, gn_f, coarse_output)
    sk = swapped(sk, 1)
    return final(share, share_1, share_2, kk, sk, sums, went_f, sums_f, went)


def solution(mesh):
    finer = Mesh(mesh.devices.reshape(4, 2, 4, 2, 2), ALL)
    cols = P(None, HEAD)
    return jax.shard_map(
        shards,
        mesh=finer,
        in_specs=(
            P(SEQ, None), P(), cols, cols, P(), cols, cols, P(), P(HEAD), P(HEAD), P(HEAD),
            P(HEAD, None), P(), P(), cols, cols, P(), cols, cols, P(), P(HEAD), P(HEAD), P(HEAD),
            P(HEAD, None),
        ),
        out_specs=P(SEQ, HEAD),
        check_vma=False,
    )
```

```python
import jax
import jax.numpy as jnp
from jax import lax
from jax.experimental import pallas as pl
from jax.experimental.pallas import tpu as pltpu
from jax.sharding import Mesh
from jax.sharding import PartitionSpec as P


SEQ = ("z", "u", "x")
HEAD = ("y", "c")
ALL = ("z", "u", "x", "y", "c")
EPSILON = 1e-05
BLK = 256
BF = jnp.bfloat16
F32 = jnp.float32
NN = (((1,), (0,)), ((), ()))
NT = (((1,), (1,)), ((), ()))
TN = (((0,), (0,)), ((), ()))


def dot(a, b, dims=NN):
    return lax.dot_general(a, b, dims, preferred_element_type=F32)


def parts(x):
    hi = x.astype(BF).astype(F32)
    rest = x - hi
    mid = rest.astype(BF).astype(F32)
    low = rest - mid
    return jnp.concatenate([hi, mid, low, jnp.zeros_like(x)], 0).astype(BF)


def decay_rows(row):
    hi = row.astype(BF).astype(F32)
    rest = row - hi
    mid = rest.astype(BF).astype(F32)
    low = rest - mid
    return jnp.concatenate([hi, mid, low, jnp.zeros((13, row.shape[1]), F32)], 0).astype(BF)


def of_rows(rows):
    rows = rows.astype(F32)
    return rows[0:1] + rows[1:2] + rows[2:3]


def iota(shape, dim):
    return lax.broadcasted_iota(jnp.int32, shape, dim)


def head_sel(width):
    return iota((8, width), 0) == iota((8, width), 1) // 64


def expander(width):
    r, lane = iota((32, width), 0), iota((32, width), 1)
    return jnp.where((r < 24) & (r % 8 == lane // 64), 1.0, 0.0).astype(BF)


def upper():
    return jnp.where(iota((BLK, BLK), 0) <= iota((BLK, BLK), 1), 1.0, 0.0).astype(BF)


def silu(v):
    h = v * 0.5
    return h + h * jnp.tanh(h)


def softplus(v):
    return jnp.maximum(v, 0.0) + jnp.log1p(jnp.exp(-jnp.abs(v)))


def rms(x, gain):
    x = x.astype(F32)
    return (x * lax.rsqrt(jnp.mean(x * x, axis=-1, keepdims=True) + EPSILON) * gain).astype(BF)


def cumulate(logs, tri):
    s = dot(parts(logs), tri)
    return s[0:8] + s[8:16] + s[16:24]


def spaced(length):
    return length // 8 + 1


def convolve(cv, act, half_taps, length):
    apart = spaced(length)

    def slab(c):
        taps = half_taps[c]
        rows = [cv[c, pl.ds(13 + i, 8, stride=apart), :] for i in range(3)]
        for i in range(apart):
            rows.append(cv[c, pl.ds(16 + i, 8, stride=apart), :])
            h = rows[i] * taps[0:1]
            for k in range(1, 4):
                h = h + rows[i + k] * taps[k : k + 1]
            act[c, pl.ds(i, 8, stride=apart), :] = h + h * jnp.tanh(h)

    for c in range(cv.shape[0]):
        slab(c)


def project(rows, weights, cv, start, slab):
    product = dot(rows, weights)
    for j in range(product.shape[1] // 128):
        cv[slab + j, start : start + rows.shape[0], :] = product[:, j * 128 : (j + 1) * 128]


def rounded(x):
    return x.astype(BF).astype(F32)


def small_rows(pack):
    rows = pack[384:416, :].astype(F32)
    kv = rows[0:4, 0:128] + rows[4:8, 0:128] + rows[8:12, 0:128]
    right = rows[0:16, 128:256]
    norm, b0, b1, d0, d1 = (of_rows(right[3 * j : 3 * j + 3]) for j in range(5))
    return kv, norm, jnp.concatenate([b0, b1], 0), jnp.concatenate([d0, d1], 0), rows[16:18]


def three(row):
    hi = row.astype(BF).astype(F32)
    rest = row - hi
    mid = rest.astype(BF).astype(F32)
    return [hi, mid, rest - mid]


def run_copies(pairs, sems):
    copies = [pltpu.make_async_copy(a, b, sems.at[j]) for j, (a, b) in enumerate(pairs)]
    for copy in copies:
        copy.start()
    return copies


def pack_kernel(
    bias, decay, gate, value, output, steps, kv, norm, tokens, gain, scans, ks,
    pack, ends, chunk, gain_v, scans_v, ks_v, kv_v, norm_v, steps_v, bias_v, decay_v, sems,
):
    copies = run_copies(
        (
            (kv, kv_v),
            (norm, norm_v),
            (steps, steps_v),
            (bias, bias_v),
            (decay, decay_v),
            (tokens.at[4080:4096], ends),
            (gate, pack.at[0:256, 0:128]),
            (value, pack.at[0:256, 128:256]),
            (output, pack.at[256:384]),
            (tokens.at[1008:2048], chunk),
            (gain, gain_v),
            (scans, scans_v),
            (ks, ks_v),
        ),
        sems,
    )
    for copy in copies[:5]:
        copy.wait()
    left = jnp.concatenate(three(kv_v[...]) + [jnp.zeros((4, 128), F32)], 0)
    rows = three(norm_v[...])
    for ref in (bias_v, decay_v):
        for j in range(2):
            rows = rows + three(jnp.broadcast_to(ref[:, j : j + 1], (1, 128)))
    right = jnp.concatenate(rows + [jnp.zeros((1, 128), F32)], 0)
    below = jnp.concatenate([steps_v[...].astype(F32), jnp.zeros((14, 256), F32)], 0)
    pack[384:416, :] = jnp.concatenate([jnp.concatenate([left, right], 1), below], 0).astype(BF)
    for copy in copies[5:]:
        copy.wait()


def packed(*args):
    return pl.pallas_call(
        pack_kernel,
        in_specs=[HBM] * 12,
        out_specs=[VM] * 6,
        out_shape=[
            sds((416, 256), BF),
            sds((16, 256), BF),
            sds((1040, 256), BF),
            sds((1, 256)),
            sds((256, 512), BF),
            sds((4, 512)),
        ],
        scratch_shapes=[
            pltpu.VMEM((4, 128), F32),
            pltpu.VMEM((1, 128), F32),
            pltpu.VMEM((2, 256), BF),
            pltpu.VMEM((1, 2), F32),
            pltpu.VMEM((1, 2), F32),
            pltpu.SemaphoreType.DMA((13,)),
        ],
        compiler_params=few(4),
        name="pack",
    )(*in_hbm(*args))


def params_kernel(bias, decay, kv, ks, gain, steps, norm, taps, both, *refs):
    outs, kv_v, ks_v, bias_v, decay_v, sems = refs[:3], *refs[3:]
    copies = run_copies(
        (
            (kv, kv_v), (ks, ks_v), (bias, bias_v), (decay, decay_v),
            (gain, outs[0]), (steps, outs[1]), (norm, outs[2]),
        ),
        sems,
    )
    for copy in copies:
        copy.wait()
    for j in range(4):
        cols = slice(j * 128, (j + 1) * 128)
        taps[j] = kv_v[:, cols] * 0.5
        taps[4 + j] = ks_v[:, cols] * 0.5
    rows = [
        jnp.broadcast_to(ref[:, j : j + 1], (1, 128)) for ref in (bias_v, decay_v) for j in range(8)
    ]
    both[...] = jnp.concatenate(rows, 0)


def coarse_params(bias, decay, kv, ks, gain, steps, norm):
    return pl.pallas_call(
        params_kernel,
        in_specs=[HBM] * 7,
        out_specs=[VM] * 5,
        out_shape=[
            sds((8, 4, 128)), sds((16, 128)), sds((1, 1024)), sds((8, 1024), BF), sds((1, 512)),
        ],
        scratch_shapes=[
            pltpu.VMEM((4, 512), F32),
            pltpu.VMEM((4, 512), F32),
            pltpu.VMEM((1, 8), F32),
            pltpu.VMEM((1, 8), F32),
            pltpu.SemaphoreType.DMA((7,)),
        ],
        compiler_params=few(4),
        name="coarse_params",
    )(*in_hbm(bias, decay, kv, ks, gain, steps, norm))


def state_chunk(x, gain, pack, scans, ks, taps, cv, act):
    kv, _, bias, decay, steps = small_rows(pack)
    pad = jnp.zeros((6, 128), F32)
    bias = jnp.concatenate([bias, pad], 0)[:, 0:1]
    decay = jnp.concatenate([decay, pad], 0)[:, 0:1]
    steps = jnp.concatenate([steps, jnp.zeros((6, 256), F32)], 0).astype(BF)
    wv, wb = pack[0:256, 128:256], scans[:, 0:256]
    taps[0] = kv * 0.5
    taps[1] = ks[:, 0:128] * 0.5
    taps[2] = ks[:, 128:256] * 0.5
    normed = rms(x, gain[...])
    project(normed, wv, cv, 0, 0)
    project(normed, wb, cv, 0, 1)
    raw = dot(steps, normed[16:1040], NT)
    convolve(cv, act, taps, 1024)
    dt = softplus(raw + bias)
    logs = -dt * decay
    tri = upper()
    carry = jnp.zeros((8, 1), F32)
    pieces = []
    for b in range(4):
        piece = cumulate(logs[:, b * BLK : (b + 1) * BLK], tri) + carry
        carry = piece[:, BLK - 1 : BLK]
        pieces.append(piece)
    cum = jnp.concatenate(pieces, 1)
    tail = jnp.exp(carry - cum) * dt
    spread = dot(parts(tail), expander(128), TN)
    scaled = (act[0, 0:1024] * spread).astype(BF)
    maps = jnp.concatenate([act[1, 0:1024].astype(BF), act[2, 0:1024].astype(BF)], 1)
    local = dot(scaled, maps, TN).T
    total = jnp.sum(
        jnp.where(head_sel(128), jnp.broadcast_to(carry, (8, 128)), 0.0), axis=0, keepdims=True
    )
    return local, total


def later_chunks_kernel(
    tokens, chunk_0, gain, pack, scans, ks,
    local, total, x0, mine, mine_rim, xs, taps, cv, act, sems, x_sems,
):
    i = pl.program_id(0)
    start = pl.multiple_of(lax.axis_index(HEAD) * 1024, 1024)
    early = pl.multiple_of(jnp.maximum(start - 16, 0), 16)
    mine_pairs = (
        (tokens.at[0:1024], x0),
        (tokens.at[pl.ds(start, 1024)], mine),
        (tokens.at[pl.ds(early, 16)], mine_rim),
    )

    def chunk(j):
        begin_row = pl.multiple_of((j + 1) * 1024 - 16, 16)
        return pltpu.make_async_copy(tokens.at[pl.ds(begin_row, 1040)], xs.at[j], x_sems.at[j])

    @pl.when(i == 0)
    def _():
        chunk(1).start()
        chunk(2).start()
        for j, (a, b) in enumerate(mine_pairs):
            pltpu.make_async_copy(a, b, sems.at[j]).start()
        xs[0] = chunk_0[...]

    @pl.when(i > 0)
    def _():
        chunk(i).wait()

    state, logs = state_chunk(xs[i], gain, pack, scans, ks, taps, cv, act)
    local[i] = state
    total[i] = jnp.broadcast_to(logs, (8, 128))

    @pl.when(i == 2)
    def _():
        for j, (a, b) in enumerate(mine_pairs):
            pltpu.make_async_copy(a, b, sems.at[j]).wait()


def since_start(rows):
    return jnp.where(lax.axis_index(SEQ) == 0, 0.0, rows[...].astype(F32))


def first_chunk_kernel(
    x, rim, gain, pack, scans, ks, later, later_total,
    local, total, whole, whole_total, message, taps, cv, act,
):
    rows = jnp.concatenate([since_start(rim), x[...].astype(F32)], 0)
    state, logs = state_chunk(rows, gain, pack, scans, ks, taps, cv, act)
    local[...] = state
    total[...] = jnp.broadcast_to(logs, (8, 128))
    for j in range(3):
        piece = later_total[j, 0:1, :]
        state = state * jnp.exp(piece) + later[j]
        logs = logs + piece
    whole[...] = state
    whole_total[...] = jnp.broadcast_to(logs, (8, 128))
    message[0:256, :] = state.astype(BF)
    message[256:272, :] = decay_rows(logs)


def sds(shape, dtype=F32):
    return jax.ShapeDtypeStruct(shape, dtype)


def in_hbm(*arrays):
    return [pltpu.with_memory_space_constraint(a, pltpu.HBM) for a in arrays]


def few(mib):
    return pltpu.CompilerParams(vmem_limit_bytes=mib << 20)


VM = pl.BlockSpec(memory_space=pltpu.VMEM)
HBM = pl.BlockSpec(memory_space=pltpu.HBM)


def fine_states(tokens, chunk, ends_from, gain, pack, scans, ks):
    scratch = [
        pltpu.VMEM((3, 4, 128), F32),
        pltpu.VMEM((3, 1048, 128), F32),
        pltpu.VMEM((3, 1032, 128), F32),
    ]
    later, later_total, x0, *mine = pl.pallas_call(
        later_chunks_kernel,
        grid=(3,),
        in_specs=[HBM] + [VM] * 5,
        out_specs=[VM] * 5,
        out_shape=[
            sds((3, 256, 128)),
            sds((3, 8, 128)),
            sds((1024, 256), BF),
            sds((1024, 256), BF),
            sds((16, 256), BF),
        ],
        scratch_shapes=[pltpu.VMEM((3, 1040, 256), BF)]
        + scratch
        + [pltpu.SemaphoreType.DMA((3,)), pltpu.SemaphoreType.DMA((3,))],
        compiler_params=few(16),
        name="later_chunks",
    )(*in_hbm(tokens), chunk, gain, pack, scans, ks)
    first = pl.pallas_call(
        first_chunk_kernel,
        in_specs=[VM] * 8,
        out_specs=[VM] * 5,
        out_shape=[
            sds((256, 128)),
            sds((8, 128)),
            sds((256, 128)),
            sds((8, 128)),
            sds((272, 128), BF),
        ],
        scratch_shapes=scratch,
        compiler_params=few(16),
        name="first_chunk",
    )(x0, ends_from, gain, pack, scans, ks, later, later_total)
    return later, later_total, mine, first


def combine(i, count, own, own_total, prior, prior_total, received):
    state = jnp.zeros_like(own)
    logs = jnp.zeros_like(own_total)
    zero = jnp.zeros((), F32)
    got = [(r[0:256, :].astype(F32), of_rows(r[256:272, :])) for r in received]
    for k in range(count - 1, 0, -1):
        s, l = got[k - 1]
        valid = i >= k
        state = jnp.where(valid, state * jnp.exp(l) + s, state)
        logs = jnp.where(valid, logs + l, logs)
    new_prior = state * jnp.exp(prior_total) + prior
    new_prior_total = logs + prior_total
    state = state * jnp.exp(own_total) + own
    logs = logs + own_total
    for m in range(1, count):
        s, l = got[count - m - 1]
        valid = i + m < count
        state = jnp.where(valid, state * jnp.exp(l) + s, state)
        logs = jnp.where(valid, logs + l, logs)
    return new_prior, new_prior_total, state, logs


def middle_kernel(axis, count, fresh, own, own_total, *refs):
    if fresh:
        prior, prior_total = jnp.zeros((256, 128), F32), jnp.zeros((1, 128), F32)
    else:
        prior, prior_total, refs = refs[0][...], refs[1][0:1, :], refs[2:]
    received, (np_ref, npt_ref, ns_ref, nst_ref, message) = refs[: count - 1], refs[count - 1 :]
    p, pt, s, st = combine(
        lax.axis_index(axis), count, own[...], own_total[0:1, :], prior, prior_total, received
    )
    np_ref[...] = p
    npt_ref[...] = jnp.broadcast_to(pt, (8, 128))
    ns_ref[...] = s
    nst_ref[...] = jnp.broadcast_to(st, (8, 128))
    message[0:256, :] = s.astype(BF)
    message[256:272, :] = decay_rows(st)


def middle_stage(axis, count, own, own_total, prior, received):
    return pl.pallas_call(
        lambda *refs: middle_kernel(axis, count, not prior, *refs),
        in_specs=[VM] * (2 + len(prior) + len(received)),
        out_specs=[VM] * 5,
        out_shape=[
            sds((256, 128)),
            sds((8, 128)),
            sds((256, 128)),
            sds((8, 128)),
            sds((272, 128), BF),
        ],
        compiler_params=few(4),
    )(own, own_total, *prior, *received)


def last_kernel(own, own_total, prior, prior_total, r1, r2, r3, l0, t0, later, later_total,
                o0, o1, o2, o3, sub):
    p, _, _, _ = combine(
        lax.axis_index("z"), 4, own[...], own_total[0:1, :], prior[...], prior_total[0:1, :],
        (r1, r2, r3),
    )
    sub[0] = p
    p = p * jnp.exp(t0[0:1, :]) + l0[...]
    sub[1] = p
    for j in range(2):
        p = p * jnp.exp(later_total[j, 0:1, :]) + later[j]
        sub[j + 2] = p
    h = lax.axis_index(HEAD)
    for k, out in enumerate((o0, o1, o2, o3)):
        out[...] = sub[h ^ k].astype(BF)


def last_stage(own, own_total, prior, received, l0, t0, later, later_total):
    return pl.pallas_call(
        last_kernel,
        in_specs=[VM] * 11,
        out_specs=[VM] * 4,
        out_shape=[sds((256, 128), BF)] * 4,
        scratch_shapes=[pltpu.VMEM((4, 256, 128), F32)],
        compiler_params=few(6),
        name="chain_last",
    )(own, own_total, *prior, *received, l0, t0, later, later_total)


def scan_block(
    fresh, normed, wg, wv, ws, wst, taps, bias, decay,
    lead, tail_out, maps_out, cv, act, sc, spread, scaled, run, run_log,
):
    project(normed, wv[...], cv, 0, 0)
    project(normed, ws[...], cv, 0, 4)
    normed = normed[16:272]
    tail_out[...] = silu(dot(normed, wg[...]))
    convolve(cv, act, taps, BLK)
    raw = dot(wst[...], normed, NT)
    dt = softplus(raw + bias[...])
    logs = -dt * decay[...]
    cum = cumulate(logs, upper())
    last = cum[:, BLK - 1 : BLK]
    stacked = [jnp.exp(cum), jnp.exp(last - cum) * dt]
    if fresh:
        run_log[...] = jnp.broadcast_to(last, (8, 128))
    else:
        stacked = [jnp.exp(cum + run_log[:, 0:1])] + stacked
        run_log[...] = run_log[...] + last
    first = 256 * (len(stacked) - 2)
    spread[0 : first + 512, :] = dot(parts(jnp.concatenate(stacked, 1)), expander(512), TN)
    columns = dot(parts(cum), jnp.where(
        (iota((32, 128), 0) < 24) & (iota((32, 128), 0) % 8 == iota((32, 128), 1)), 1.0, 0.0
    ).astype(BF), TN)
    rows = cum - jnp.log(dt)
    in_map = jnp.concatenate([act[4, 0:BLK].astype(BF), act[5, 0:BLK].astype(BF)], 1)
    out_map = jnp.concatenate([act[6, 0:BLK].astype(BF), act[7, 0:BLK].astype(BF)], 1)
    maps_out[...] = out_map
    sc[...] = dot(out_map, in_map, NT)
    if not fresh:
        lead[...] = spread[256:512, :] * dot(out_map, run[...].astype(BF))
    low_tri = iota((128, 128), 0) >= iota((128, 128), 1)
    lane_low = iota((BLK, 128), 1) < 64
    for p in range(4):
        cols = slice(p * 128, (p + 1) * 128)
        vals = act[p, 0:BLK]
        v0 = jnp.where(lane_low, vals, 0.0).astype(BF)
        v1 = jnp.where(lane_low, 0.0, vals).astype(BF)
        upper_w, lower_w = [], []
        for h in (2 * p, 2 * p + 1):
            c0, c1 = columns[0:128, h : h + 1], columns[128:256, h : h + 1]
            r0, r1 = rows[h : h + 1, 0:128], rows[h : h + 1, 128:256]
            upper_w.append(
                (sc[0:128, 0:128] * jnp.exp(jnp.where(low_tri, c0 - r0, -jnp.inf))).astype(BF)
            )
            lower_w.append((sc[128:256, 0:128] * jnp.exp(c1 - r0)).astype(BF))
            lower_w.append(
                (sc[128:256, 128:256] * jnp.exp(jnp.where(low_tri, c1 - r1, -jnp.inf))).astype(BF)
            )
        top = dot(
            jnp.concatenate(upper_w, 1), jnp.concatenate([v0[0:128], v1[0:128]], 0)
        )
        bottom = dot(jnp.concatenate(lower_w, 1), jnp.concatenate([v0, v1], 0))
        gate = tail_out[:, cols]
        if not fresh:
            top = top + lead[0:128, cols]
            bottom = bottom + lead[128:256, cols]
        lead[0:128, cols] = top * gate[0:128]
        lead[128:256, cols] = bottom * gate[128:256]
        tail_out[:, cols] = spread[0:256, cols] * gate
        scaled[:, cols] = (vals * spread[first + 256 : first + 512, cols]).astype(BF)
    local = dot(in_map, scaled[...], TN)
    run[...] = local if fresh else run[...] * spread[511:512, :] + local


SCAN_SCRATCH = [
    pltpu.VMEM((8, 280, 128), F32),
    pltpu.VMEM((8, BLK + 8, 128), F32),
    pltpu.VMEM((BLK, BLK), F32),
    pltpu.VMEM((768, 512), F32),
    pltpu.VMEM((256, 512), BF),
]


def fine_main_kernel(at, mine, gain, ws, *refs):
    later = at > 0
    if later:
        x0, x1, wg, wv, wst, taps, bias, decay, lead, tail_out, maps_out, run, run_log = refs[:13]
    else:
        ks, p0, p1, p2, p3, x0, x1, lead, tail_out, maps_out, run, run_log = refs[:12]
        wg, wv, wst, taps, bias, decay = refs[12:18]
    cv, act, sc, spread, scaled = refs[-5:]
    i = pl.program_id(0)

    @pl.when(i == 0)
    def _():
        if later:
            run[...] = x0[...]
            run_log[...] = x1[...]
            return
        run[...] = jnp.zeros_like(run)
        run_log[...] = jnp.zeros_like(run_log)
        for j in range(4):
            taps[4 + j] = ks[:, j * 128 : (j + 1) * 128] * 0.5
        for j, p in enumerate((p0, p1, p2, p3)):
            cols = slice(j * 128, (j + 1) * 128)
            two = slice(2 * j, 2 * j + 2)
            wg[:, cols] = p[0:256, 0:128]
            wv[:, cols] = p[0:256, 128:256]
            kv, _, bias[two, :], decay[two, :], wst[two, :] = small_rows(p)
            taps[j] = kv * 0.5

    start = pl.multiple_of((i + at) * BLK, BLK)
    rim = mine[pl.ds(pl.multiple_of(jnp.maximum(start - 16, 0), 16), 16), :].astype(F32)
    if not later:
        edge = jnp.where(lax.axis_index(HEAD) == 0, since_start(x0), x1[...].astype(F32))
        rim = jnp.where(i == 0, edge, rim)
    x = jnp.concatenate([rim, mine[pl.ds(start, BLK), :].astype(F32)], 0)
    scan_block(
        False, rms(x, gain[...]), wg, wv, ws, wst[...].astype(BF), taps, bias[:, 0:1],
        decay[:, 0:1], lead, tail_out, maps_out, cv, act, sc, spread, scaled, run, run_log,
    )


def fine_main(at, blocks, *args):
    length = blocks * BLK
    rows = [pl.BlockSpec((BLK, n), lambda i: (i, 0)) for n in (512, 512, 256)]
    weights = []
    if at == 0:
        weights = [
            sds((256, 512), BF), sds((256, 512), BF), sds((8, 256)), sds((8, 4, 128)),
            sds((8, 128)), sds((8, 128)),
        ]
    return pl.pallas_call(
        lambda *refs: fine_main_kernel(at, *refs),
        grid=(blocks,),
        in_specs=[VM] * len(args),
        out_specs=rows + [VM] * (2 + len(weights)),
        out_shape=[
            sds((length, 512)), sds((length, 512)), sds((length, 256), BF),
            sds((256, 512)), sds((8, 128)),
        ]
        + weights,
        scratch_shapes=SCAN_SCRATCH,
        compiler_params=few(16),
    )(*args)


def fine_close_kernel(*refs):
    leads, tails, mapss, x, states, packs = (
        refs[0:3], refs[3:6], refs[6:9], refs[9], refs[10:14], refs[14:18]
    )
    merge, merged, end_rows, hidden, state, wo, norm = refs[18:]
    for j, (s, p) in enumerate(zip(states, packs)):
        cols = slice(j * 128, (j + 1) * 128)
        state[:, cols] = s[...]
        wo[cols, :] = p[256:384, :]
        norm[:, cols] = small_rows(p)[1]
    for i, (call, at) in enumerate(((0, 0), (0, 1), (1, 0), (2, 0))):
        part = slice(at * BLK, (at + 1) * BLK)
        rows = slice(i * BLK, (i + 1) * BLK)
        gated = leads[call][part] + tails[call][part] * dot(mapss[call][part], state[...])
        factor = lax.rsqrt(jnp.sum(gated * gated, axis=1, keepdims=True) / 512.0 + EPSILON)
        total = dot((gated * factor * norm[...]).astype(BF), wo[...])
        out = x[rows].astype(F32) + total
        hidden[0, rows, :] = rounded(out[:, 0:128])
        hidden[1, rows, :] = rounded(out[:, 128:256])
    total = None
    for odd in range(2):
        rows = [
            hidden[half, pl.ds(odd, 512, stride=2), :].reshape(8, 2, 32, 128) for half in range(2)
        ]
        for line in range(2):
            tile = [r[:, line].reshape(256, 128).astype(BF) for r in rows]
            at = (2 * line + odd) * 256
            piece = dot(jnp.concatenate(tile, 1), merge[at : at + 256, :])
            total = piece if total is None else total + piece
    result = total.astype(BF)
    merged[...] = result
    end_rows[...] = result[240:256]


def fine_close(leads, tails, maps, x, states, packs, merge):
    return pl.pallas_call(
        fine_close_kernel,
        in_specs=[VM] * 19,
        out_specs=[VM] * 2,
        scratch_shapes=[
            pltpu.VMEM((2, 1024, 128), F32),
            pltpu.VMEM((256, 512), BF),
            pltpu.VMEM((512, 256), BF),
            pltpu.VMEM((1, 512), F32),
        ],
        out_shape=[sds((256, 1024), BF), sds((16, 1024), BF)],
        compiler_params=few(16),
        name="fine_close",
    )(*leads, *tails, *maps, x, *states, *packs, merge)


def in_order(first, a, a_log, b, b_log):
    lead_log = jnp.where(first, b_log, a_log)
    row = jnp.exp(spread_row(lead_log))
    return jnp.where(first, a, b) * row + jnp.where(first, b, a), a_log + b_log


def chip_start(rows):
    first = lax.axis_index(("z", "u", "x", "y")) == 0
    return jnp.where(first, 0.0, rows[...].astype(F32))


def coarse_main_kernel(kind, pieces, gain, wg, wv, ws, wst, taps, both, *refs):
    qs, refs = refs[:pieces], refs[pieces:]
    xs, sems, rims, cv, act, sc, spread, scaled = refs[-8:]
    y, c = lax.axis_index("y"), lax.axis_index("c")
    h = 2 * y + c
    if kind == "near":
        ra, rb, lead, tail_out, maps_out, share, run, run_log = refs[:-8]
    elif kind == "far_1":
        re, lead, tail_out, maps_out, share, run, run_log, ends = refs[:-8]
    else:
        (
            ends_1, rd, near_run, near_log, run_1, run_log_1,
            lead, tail_out, maps_out, share, run, run_log, far_run, far_log, message,
        ) = refs[:-8]
    i = pl.program_id(0)

    @pl.when(i == 0)
    def _():
        if kind == "near":
            copies = run_copies(((qs[0], xs.at[c]), (qs[1], xs.at[1 - c])), sems)
            rim = jnp.where(c == 0, chip_start(ra), chip_start(rb))
        else:
            copies = run_copies(((qs[0], xs.at[0]),), sems)
            rim = re[...].astype(F32) if kind == "far_1" else rd[...].astype(F32)
            if kind == "far_2":
                rim = jnp.where(c == 0, ends_1[...].astype(F32), rim)
        rims[...] = rim
        if kind == "near":
            run[...] = jnp.zeros_like(run)
            run_log[...] = jnp.zeros_like(run_log)
        for copy in copies:
            copy.wait()
        if kind == "far_1":
            ends[...] = xs[0, 240:256, :]

    share[...] = xs[i, :, pl.ds(pl.multiple_of(h * 256, 256), 256)]
    rim = rims[...]
    if kind == "near":
        rim = jnp.where(i == 0, rim, xs[0, 240:256, :].astype(F32))
    x = jnp.concatenate([rim, xs[i].astype(F32)], 0)
    scan_block(
        kind != "near", rms(x, gain[...]), wg, wv, ws, wst[...], taps, both[0:8, 0:1],
        both[8:16, 0:1], lead, tail_out, maps_out, cv, act, sc, spread, scaled, run, run_log,
    )

    if kind == "far_2":
        log_1, log_2, log_n = run_log_1[:, 0:1], run_log[:, 0:1], near_log[:, 0:1]
        far, log_f = in_order(c == 0, run_1[...], log_1, run[...], log_2)
        far_run[...] = far
        far_log[...] = jnp.broadcast_to(log_f, (8, 128))
        total, log = in_order(y == 0, near_run[...], log_n, far, log_f)
        extra = decay_rows(spread_row(log))[0:8]
        for n in range(16):
            for half in range(2):
                cols = slice(half * 256, (half + 1) * 256)
                message[2 * n + half, 0:16, :] = total[n * 16 : (n + 1) * 16, cols].astype(BF)
                message[2 * n + half, 16:24, :] = extra[:, cols]


def spread_row(column):
    return jnp.sum(
        jnp.where(head_sel(512), jnp.broadcast_to(column, (8, 512)), 0.0), axis=0, keepdims=True
    )


ANY = pl.BlockSpec(memory_space=pl.ANY)


def coarse_main(kind, pieces, weights, params, extra):
    taps, both, gain, wst, _ = params
    blocks = len(pieces)
    length = blocks * BLK
    rows = [pl.BlockSpec((BLK, n), lambda i: (i, 0)) for n in (512, 512, 256, 256)]
    last = []
    if kind == "far_1":
        last = [sds((16, 1024), BF)]
    elif kind == "far_2":
        last = [sds((256, 512)), sds((8, 128)), sds((32, 24, 256), BF)]
    return pl.pallas_call(
        lambda *refs: coarse_main_kernel(kind, blocks, *refs),
        grid=(blocks,),
        in_specs=[VM] * 7 + [ANY] * blocks + [VM] * len(extra),
        out_specs=rows + [VM] * (2 + len(last)),
        out_shape=[
            sds((length, 512)),
            sds((length, 512)),
            sds((length, 256), BF),
            sds((length, 256), BF),
            sds((256, 512)),
            sds((8, 128)),
        ]
        + last,
        scratch_shapes=[
            pltpu.VMEM((blocks, 256, 1024), BF),
            pltpu.SemaphoreType.DMA((blocks,)),
            pltpu.VMEM((16, 1024), F32),
        ]
        + SCAN_SCRATCH,
        compiler_params=few(16),
    )(gain, *weights, wst, taps, both, *pieces, *extra)


def own_rim_kernel(came, beside, out):
    out[...] = jnp.where(
        lax.axis_index("c") == 0, chip_start(came), beside[240:256, :].astype(F32)
    ).astype(BF)


def own_rim(came, beside):
    return pl.pallas_call(
        own_rim_kernel,
        in_specs=[VM] * 2,
        out_specs=VM,
        out_shape=sds((16, 1024), BF),
        compiler_params=few(4),
        name="own_rim",
    )(came, beside)


def prefix_kernel(got, out):
    state = jnp.zeros((16, 256), F32)
    for d in range(32):
        out[d] = state.astype(BF)
        state = state * jnp.exp(of_rows(got[d, 16:24, :])) + got[d, 0:16, :].astype(F32)


def prefix(got):
    return pl.pallas_call(
        prefix_kernel,
        in_specs=[VM],
        out_specs=VM,
        out_shape=sds((32, 16, 256), BF),
        compiler_params=few(4),
        name="prefix",
    )(got)


def coarse_close_kernel(near, *refs):
    if near:
        lead, tail, maps, got, far_run, far_log, norm, wo, *refs = refs
    else:
        leads, tails, mapss = refs[0:2], refs[2:4], refs[4:6]
        got, near_run, near_log, run_1, log_1, run_2, log_2, norm, wo, *refs = refs[6:]
    gn, ks, ss, square_sums, states, sums = refs
    y, c = lax.axis_index("y"), lax.axis_index("c")
    h = 2 * y + c
    came = jnp.concatenate(
        [jnp.concatenate([got[2 * n], got[2 * n + 1]], 1) for n in range(16)], 0
    ).astype(F32)

    def after(state, cond, run, log):
        row = jnp.exp(spread_row(log[:, 0:1]))
        return jnp.where(cond, state * row + run[...], state)

    if near:
        states[0] = after(came, y == 1, far_run, far_log).astype(BF)
    else:
        came = after(came, y == 0, near_run, near_log)
        states[0] = after(came, c == 1, run_2, log_2).astype(BF)
        states[1] = after(came, c == 0, run_1, log_1).astype(BF)
    ones = jnp.ones((8, 512), BF)
    for i in range(2):
        if near:
            rows = slice(i * BLK, (i + 1) * BLK)
            gated = lead[rows] + tail[rows] * dot(maps[rows], states[0])
            place = i
        else:
            gated = leads[i][...] + tails[i][...] * dot(mapss[i][...], states[i])
            place = jnp.bitwise_xor(c, i)
        sq = gated * gated
        hi = sq.astype(BF)
        low = (sq - hi.astype(F32)).astype(BF)
        sums[place] = dot(ones, hi, NT) + dot(ones, low, NT)
        scaled = (gated * norm[...]).astype(BF)
        at = pl.ds(pl.multiple_of(place * BLK, BLK), BLK)
        gn[at, :] = scaled
        for k, out in ((2, ks), (3, ss)):
            col = pl.multiple_of((h ^ k) * 256, 256)
            out[at, :] = dot(scaled, wo[:, pl.ds(col, 256)]).astype(BF)
    square_sums[...] = jnp.concatenate([sums[0], sums[1]], 1)
    ss[512:528, :] = sum_rows(sums[0, 0:1], sums[1, 0:1])


def coarse_close(near, *args):
    return pl.pallas_call(
        lambda *refs: coarse_close_kernel(near, *refs),
        in_specs=[VM] * len(args),
        out_specs=[VM] * 4,
        out_shape=[
            sds((512, 512), BF), sds((512, 256), BF), sds((528, 256), BF), sds((8, 512)),
        ],
        scratch_shapes=[pltpu.VMEM((2, 256, 512), BF), pltpu.VMEM((2, 8, 256), F32)],
        compiler_params=few(12),
        name="coarse_close_near" if near else "coarse_close_far",
    )(*args)


def close_rest_kernel(near, far, wo, kk, sk):
    h = lax.axis_index(HEAD)
    for k, out in enumerate((kk, sk)):
        col = pl.multiple_of((h ^ k) * 256, 256)
        for j, ref in enumerate((near, far)):
            out[j * 512 : (j + 1) * 512, :] = dot(ref[...], wo[:, pl.ds(col, 256)]).astype(BF)


def close_rest(near, far, wo):
    return pl.pallas_call(
        close_rest_kernel,
        in_specs=[VM] * 3,
        out_specs=[VM] * 2,
        out_shape=[sds((1024, 256), BF)] * 2,
        compiler_params=few(8),
        name="close_rest",
    )(near, far, wo)


def sum_rows(a, b):
    return jnp.concatenate(three(a) + three(b) + [jnp.zeros((10, 256), F32)], 0).astype(BF)


def rows_sum(ref):
    rows = ref[512:528, :].astype(F32)
    return jnp.concatenate([of_rows(rows[0:3]), of_rows(rows[3:6])], 1)


def relay_kernel(ks, square_sums, came, out, sums):
    out[0:512, :] = (ks[...].astype(F32) + came[0:512, :].astype(F32)).astype(BF)
    total = square_sums[0:1, :] + rows_sum(came)
    out[512:528, :] = sum_rows(total[:, 0:256], total[:, 256:512])
    sums[...] = jnp.broadcast_to(total, (8, 512))


def relay(ks, square_sums, came):
    return pl.pallas_call(
        relay_kernel,
        in_specs=[VM] * 3,
        out_specs=[VM] * 2,
        out_shape=[sds((528, 256), BF), sds((8, 512))],
        compiler_params=few(4),
    )(ks, square_sums, came)


def final_kernel(share, share_1, share_2, kk, sk, sum_a, far_a, sum_b, far_b, out):
    y, c = lax.axis_index("y"), lax.axis_index("c")
    pick = jnp.where(iota((32, 256), 0) % 8 == 0, 1.0, 0.0).astype(BF)
    for side, (half, sums, far) in enumerate(((y, sum_a, far_a), (1 - y, sum_b, far_b))):
        total = sums[...] + rows_sum(far)
        factor = lax.rsqrt(total / 2048.0 + EPSILON)
        for b in range(2):
            rows = slice(b * BLK, (b + 1) * BLK)
            here = slice(side * 512 + b * BLK, side * 512 + (b + 1) * BLK)
            spread = dot(parts(factor[:, rows]), pick, TN)
            total = kk[here].astype(F32) + sk[here].astype(F32) + far[rows].astype(F32)
            if side == 0:
                own = share[rows].astype(F32)
            else:
                own = jnp.where(c == b, share_1[...].astype(F32), share_2[...].astype(F32))
            at = pl.multiple_of(half * 512 + b * BLK, BLK)
            out[pl.ds(at, BLK), :] = (own + total * spread).astype(BF)


def final(*args):
    return pl.pallas_call(
        final_kernel,
        in_specs=[VM] * 9,
        out_specs=VM,
        out_shape=sds((1024, 256), BF),
        compiler_params=few(8),
        name="final",
    )(*args)


def passed(x, axes, pairs):
    return lax.ppermute(x, axes, pairs)


def swapped(x, mask):
    return passed(x, HEAD, [(j, j ^ mask) for j in range(4)])


def round_of(x, axis):
    got = []
    for k in (1, 2, 3):
        got.append(passed(x, axis, [(j, (j + k) % 4) for j in range(4)]))
    return got


def shards(
    tokens, fine_gain, fine_gate, fine_value, fine_scans, fine_steps, fine_kernel, fine_taps,
    fine_bias, fine_decay, fine_norm, fine_output, merge_weight, coarse_gain, coarse_gate,
    coarse_value, coarse_scans, coarse_steps, coarse_kernel, coarse_taps, coarse_bias,
    coarse_decay, coarse_norm, coarse_output,
):
    pack, ends, chunk, gain, scans, ks = packed(
        fine_bias[None], fine_decay[None], fine_gate, fine_value, fine_output, fine_steps.T,
        fine_kernel, fine_norm[None], tokens, fine_gain[None], fine_scans, fine_taps,
    )
    rim = passed(ends, SEQ, [(i, (i + 1) % 32) for i in range(32)])
    packs = [pack] + [swapped(pack, m) for m in (1, 2, 3)]
    later, later_total, (mine, mine_rim), (l0, t0, own, own_total, message) = fine_states(
        tokens, chunk, rim, gain, pack, scans, ks
    )
    got = round_of(message, "x")
    first = fine_main(0, 2, mine, gain, scans, ks, *packs, rim, mine_rim)
    *prior, own, own_total, message = middle_stage("x", 4, own, own_total, (), got)
    got = [passed(message, "u", [(0, 1), (1, 0)])]
    params = coarse_params(
        coarse_bias[None], coarse_decay[None], coarse_kernel, coarse_taps, coarse_gain[None],
        coarse_steps.T, coarse_norm[None],
    )
    second = fine_main(2, 1, mine, gain, scans, *first[3:])
    *prior, own, own_total, message = middle_stage("u", 2, own, own_total, prior, got)
    got = round_of(message, "z")
    third = fine_main(3, 1, mine, gain, scans, *second[3:], *first[5:])
    subs = last_stage(own, own_total, prior, got, l0, t0, later, later_total)
    states = [subs[0]] + [swapped(subs[m], m) for m in (1, 2, 3)]
    merged, end_rows = fine_close(
        *([call[j] for call in (first, second, third)] for j in range(3)), mine, states, packs,
        merge_weight,
    )

    rim_a = passed(end_rows, ALL, [(q, (q - 1 + 2 * (q % 2)) % 128) for q in range(128)])
    across = swapped(merged, 2)
    beside = swapped(merged, 1)
    rim_b = swapped(rim_a, 1)
    rim_y = swapped(own_rim(rim_a, beside), 2)
    rim_yc = swapped(rim_y, 1)
    both = swapped(across, 1)
    weights = (coarse_gate, coarse_value, coarse_scans)
    lead, tail, maps, share, run, run_log = coarse_main(
        "near", (merged, beside), weights, params, (rim_a, rim_b)
    )
    lead_1, tail_1, maps_1, share_1, run_1, run_log_1, ends_1 = coarse_main(
        "far_1", (across,), weights, params, (rim_y,)
    )
    lead_2, tail_2, maps_2, share_2, run_2, run_log_2, run_f, run_log_f, message = coarse_main(
        "far_2", (both,), weights, params,
        (ends_1, rim_yc, run, run_log, run_1, run_log_1),
    )
    got = lax.all_to_all(message, SEQ, split_axis=0, concat_axis=0, tiled=True)
    got = lax.all_to_all(prefix(got), SEQ, split_axis=0, concat_axis=0, tiled=True)
    norm = params[4]
    gn, ks, ss, sums = coarse_close(
        True, lead, tail, maps, got, run_f, run_log_f, norm, coarse_output
    )
    gn_f, ks_f, ss_f, sums_f = coarse_close(
        False, lead_1, lead_2, tail_1, tail_2, maps_1, maps_2, got, run, run_log,
        run_1, run_log_1, run_2, run_log_2, norm, coarse_output,
    )
    went, sums = relay(ks, sums, swapped(ss, 1))
    went = swapped(went, 2)
    went_f, sums_f = relay(ks_f, sums_f, swapped(ss_f, 1))
    went_f = swapped(went_f, 2)
    kk, sk = close_rest(gn, gn_f, coarse_output)
    sk = swapped(sk, 1)
    return final(share, share_1, share_2, kk, sk, sums, went_f, sums_f, went)


def solution(mesh):
    finer = Mesh(mesh.devices.reshape(4, 2, 4, 2, 2), ALL)
    cols = P(None, HEAD)
    return jax.shard_map(
        shards,
        mesh=finer,
        in_specs=(
            P(SEQ, None), P(), cols, cols, P(), cols, cols, P(), P(HEAD), P(HEAD), P(HEAD),
            P(HEAD, None), P(), P(), cols, cols, P(), cols, cols, P(), P(HEAD), P(HEAD), P(HEAD),
            P(HEAD, None),
        ),
        out_specs=P(SEQ, HEAD),
        check_vma=False,
    )
```

```python
import jax
import jax.numpy as jnp
from jax import lax
from jax.experimental import pallas as pl
from jax.experimental.pallas import tpu as pltpu
from jax.sharding import Mesh
from jax.sharding import PartitionSpec as P


SEQ = ("z", "u", "x")
HEAD = ("y", "c")
ALL = ("z", "u", "x", "y", "c")
EPSILON = 1e-05
BLK = 256
BF = jnp.bfloat16
F32 = jnp.float32
NN = (((1,), (0,)), ((), ()))
NT = (((1,), (1,)), ((), ()))
TN = (((0,), (0,)), ((), ()))


def dot(a, b, dims=NN):
    return lax.dot_general(a, b, dims, preferred_element_type=F32)


def parts(x):
    hi = x.astype(BF).astype(F32)
    rest = x - hi
    mid = rest.astype(BF).astype(F32)
    low = rest - mid
    return jnp.concatenate([hi, mid, low, jnp.zeros_like(x)], 0).astype(BF)


def decay_rows(row):
    hi = row.astype(BF).astype(F32)
    rest = row - hi
    mid = rest.astype(BF).astype(F32)
    low = rest - mid
    return jnp.concatenate([hi, mid, low, jnp.zeros((13, row.shape[1]), F32)], 0).astype(BF)


def of_rows(rows):
    rows = rows.astype(F32)
    return rows[0:1] + rows[1:2] + rows[2:3]


def iota(shape, dim):
    return lax.broadcasted_iota(jnp.int32, shape, dim)


def head_sel(width):
    return iota((8, width), 0) == iota((8, width), 1) // 64


def expander(width):
    r, lane = iota((32, width), 0), iota((32, width), 1)
    return jnp.where((r < 24) & (r % 8 == lane // 64), 1.0, 0.0).astype(BF)


def upper():
    return jnp.where(iota((BLK, BLK), 0) <= iota((BLK, BLK), 1), 1.0, 0.0).astype(BF)


def silu(v):
    h = v * 0.5
    return h + h * jnp.tanh(h)


def softplus(v):
    return jnp.maximum(v, 0.0) + jnp.log1p(jnp.exp(-jnp.abs(v)))


def rms(x, gain):
    x = x.astype(F32)
    return (x * lax.rsqrt(jnp.mean(x * x, axis=-1, keepdims=True) + EPSILON) * gain).astype(BF)


def cumulate(logs, tri):
    s = dot(parts(logs), tri)
    return s[0:8] + s[8:16] + s[16:24]


def spaced(length):
    return length // 8 + 1


def convolve(cv, act, half_taps, length):
    apart = spaced(length)

    def slab(c):
        taps = half_taps[c]
        rows = [cv[c, pl.ds(13 + i, 8, stride=apart), :] for i in range(3)]
        for i in range(apart):
            rows.append(cv[c, pl.ds(16 + i, 8, stride=apart), :])
            h = rows[i] * taps[0:1]
            for k in range(1, 4):
                h = h + rows[i + k] * taps[k : k + 1]
            act[c, pl.ds(i, 8, stride=apart), :] = h + h * jnp.tanh(h)

    for c in range(cv.shape[0]):
        slab(c)


def project(rows, weights, cv, start, slab):
    product = dot(rows, weights)
    for j in range(product.shape[1] // 128):
        cv[slab + j, start : start + rows.shape[0], :] = product[:, j * 128 : (j + 1) * 128]


def rounded(x):
    return x.astype(BF).astype(F32)


def small_rows(pack):
    rows = pack[384:416, :].astype(F32)
    kv = rows[0:4, 0:128] + rows[4:8, 0:128] + rows[8:12, 0:128]
    right = rows[0:16, 128:256]
    norm, b0, b1, d0, d1 = (of_rows(right[3 * j : 3 * j + 3]) for j in range(5))
    return kv, norm, jnp.concatenate([b0, b1], 0), jnp.concatenate([d0, d1], 0), rows[16:18]


def three(row):
    hi = row.astype(BF).astype(F32)
    rest = row - hi
    mid = rest.astype(BF).astype(F32)
    return [hi, mid, rest - mid]


def run_copies(pairs, sems):
    copies = [pltpu.make_async_copy(a, b, sems.at[j]) for j, (a, b) in enumerate(pairs)]
    for copy in copies:
        copy.start()
    return copies


def pack_kernel(
    bias, decay, gate, value, output, steps, kv, norm, tokens, gain, scans, ks,
    pack, ends, chunk, gain_v, scans_v, ks_v, kv_v, norm_v, steps_v, bias_v, decay_v, sems,
):
    copies = run_copies(
        (
            (kv, kv_v),
            (norm, norm_v),
            (steps, steps_v),
            (bias, bias_v),
            (decay, decay_v),
            (tokens.at[4080:4096], ends),
            (gate, pack.at[0:256, 0:128]),
            (value, pack.at[0:256, 128:256]),
            (output, pack.at[256:384]),
            (tokens.at[1008:2048], chunk),
            (gain, gain_v),
            (scans, scans_v),
            (ks, ks_v),
        ),
        sems,
    )
    for copy in copies[:5]:
        copy.wait()
    left = jnp.concatenate(three(kv_v[...]) + [jnp.zeros((4, 128), F32)], 0)
    rows = three(norm_v[...])
    for ref in (bias_v, decay_v):
        for j in range(2):
            rows = rows + three(jnp.broadcast_to(ref[:, j : j + 1], (1, 128)))
    right = jnp.concatenate(rows + [jnp.zeros((1, 128), F32)], 0)
    below = jnp.concatenate([steps_v[...].astype(F32), jnp.zeros((14, 256), F32)], 0)
    pack[384:416, :] = jnp.concatenate([jnp.concatenate([left, right], 1), below], 0).astype(BF)
    for copy in copies[5:]:
        copy.wait()


def packed(*args):
    return pl.pallas_call(
        pack_kernel,
        in_specs=[HBM] * 12,
        out_specs=[VM] * 6,
        out_shape=[
            sds((416, 256), BF),
            sds((16, 256), BF),
            sds((1040, 256), BF),
            sds((1, 256)),
            sds((256, 512), BF),
            sds((4, 512)),
        ],
        scratch_shapes=[
            pltpu.VMEM((4, 128), F32),
            pltpu.VMEM((1, 128), F32),
            pltpu.VMEM((2, 256), BF),
            pltpu.VMEM((1, 2), F32),
            pltpu.VMEM((1, 2), F32),
            pltpu.SemaphoreType.DMA((13,)),
        ],
        compiler_params=few(4),
        name="pack",
    )(*in_hbm(*args))


def params_kernel(bias, decay, kv, ks, gain, steps, norm, taps, both, *refs):
    outs, kv_v, ks_v, bias_v, decay_v, sems = refs[:3], *refs[3:]
    copies = run_copies(
        (
            (kv, kv_v), (ks, ks_v), (bias, bias_v), (decay, decay_v),
            (gain, outs[0]), (steps, outs[1]), (norm, outs[2]),
        ),
        sems,
    )
    for copy in copies:
        copy.wait()
    for j in range(4):
        cols = slice(j * 128, (j + 1) * 128)
        taps[j] = kv_v[:, cols] * 0.5
        taps[4 + j] = ks_v[:, cols] * 0.5
    rows = [
        jnp.broadcast_to(ref[:, j : j + 1], (1, 128)) for ref in (bias_v, decay_v) for j in range(8)
    ]
    both[...] = jnp.concatenate(rows, 0)


def coarse_params(bias, decay, kv, ks, gain, steps, norm):
    return pl.pallas_call(
        params_kernel,
        in_specs=[HBM] * 7,
        out_specs=[VM] * 5,
        out_shape=[
            sds((8, 4, 128)), sds((16, 128)), sds((1, 1024)), sds((8, 1024), BF), sds((1, 512)),
        ],
        scratch_shapes=[
            pltpu.VMEM((4, 512), F32),
            pltpu.VMEM((4, 512), F32),
            pltpu.VMEM((1, 8), F32),
            pltpu.VMEM((1, 8), F32),
            pltpu.SemaphoreType.DMA((7,)),
        ],
        compiler_params=few(4),
        name="coarse_params",
    )(*in_hbm(bias, decay, kv, ks, gain, steps, norm))


def state_chunk(x, gain, pack, scans, ks, taps, cv, act):
    kv, _, bias, decay, steps = small_rows(pack)
    pad = jnp.zeros((6, 128), F32)
    bias = jnp.concatenate([bias, pad], 0)[:, 0:1]
    decay = jnp.concatenate([decay, pad], 0)[:, 0:1]
    steps = jnp.concatenate([steps, jnp.zeros((6, 256), F32)], 0).astype(BF)
    wv, wb = pack[0:256, 128:256], scans[:, 0:256]
    taps[0] = kv * 0.5
    taps[1] = ks[:, 0:128] * 0.5
    taps[2] = ks[:, 128:256] * 0.5
    normed = rms(x, gain[...])
    project(normed, wv, cv, 0, 0)
    project(normed, wb, cv, 0, 1)
    raw = dot(steps, normed[16:1040], NT)
    convolve(cv, act, taps, 1024)
    dt = softplus(raw + bias)
    logs = -dt * decay
    tri = upper()
    carry = jnp.zeros((8, 1), F32)
    pieces = []
    for b in range(4):
        piece = cumulate(logs[:, b * BLK : (b + 1) * BLK], tri) + carry
        carry = piece[:, BLK - 1 : BLK]
        pieces.append(piece)
    cum = jnp.concatenate(pieces, 1)
    tail = jnp.exp(carry - cum) * dt
    spread = dot(parts(tail), expander(128), TN)
    scaled = (act[0, 0:1024] * spread).astype(BF)
    maps = jnp.concatenate([act[1, 0:1024].astype(BF), act[2, 0:1024].astype(BF)], 1)
    local = dot(scaled, maps, TN).T
    total = jnp.sum(
        jnp.where(head_sel(128), jnp.broadcast_to(carry, (8, 128)), 0.0), axis=0, keepdims=True
    )
    return local, total


def later_chunks_kernel(
    tokens, chunk_0, gain, pack, scans, ks,
    local, total, x0, mine, mine_rim, xs, taps, cv, act, sems, x_sems,
):
    i = pl.program_id(0)
    start = pl.multiple_of(lax.axis_index(HEAD) * 1024, 1024)
    early = pl.multiple_of(jnp.maximum(start - 16, 0), 16)
    mine_pairs = (
        (tokens.at[0:1024], x0),
        (tokens.at[pl.ds(start, 1024)], mine),
        (tokens.at[pl.ds(early, 16)], mine_rim),
    )

    def chunk(j):
        begin_row = pl.multiple_of((j + 1) * 1024 - 16, 16)
        return pltpu.make_async_copy(tokens.at[pl.ds(begin_row, 1040)], xs.at[j], x_sems.at[j])

    @pl.when(i == 0)
    def _():
        chunk(1).start()
        chunk(2).start()
        for j, (a, b) in enumerate(mine_pairs):
            pltpu.make_async_copy(a, b, sems.at[j]).start()
        xs[0] = chunk_0[...]

    @pl.when(i > 0)
    def _():
        chunk(i).wait()

    state, logs = state_chunk(xs[i], gain, pack, scans, ks, taps, cv, act)
    local[i] = state
    total[i] = jnp.broadcast_to(logs, (8, 128))

    @pl.when(i == 2)
    def _():
        for j, (a, b) in enumerate(mine_pairs):
            pltpu.make_async_copy(a, b, sems.at[j]).wait()


def since_start(rows):
    return jnp.where(lax.axis_index(SEQ) == 0, 0.0, rows[...].astype(F32))


def first_chunk_kernel(
    x, rim, gain, pack, scans, ks, later, later_total,
    local, total, whole, whole_total, message, taps, cv, act,
):
    rows = jnp.concatenate([since_start(rim), x[...].astype(F32)], 0)
    state, logs = state_chunk(rows, gain, pack, scans, ks, taps, cv, act)
    local[...] = state
    total[...] = jnp.broadcast_to(logs, (8, 128))
    for j in range(3):
        piece = later_total[j, 0:1, :]
        state = state * jnp.exp(piece) + later[j]
        logs = logs + piece
    whole[...] = state
    whole_total[...] = jnp.broadcast_to(logs, (8, 128))
    message[0:256, :] = state.astype(BF)
    message[256:272, :] = decay_rows(logs)


def sds(shape, dtype=F32):
    return jax.ShapeDtypeStruct(shape, dtype)


def in_hbm(*arrays):
    return [pltpu.with_memory_space_constraint(a, pltpu.HBM) for a in arrays]


def few(mib):
    return pltpu.CompilerParams(vmem_limit_bytes=mib << 20)


VM = pl.BlockSpec(memory_space=pltpu.VMEM)
HBM = pl.BlockSpec(memory_space=pltpu.HBM)


def fine_states(tokens, chunk, ends_from, gain, pack, scans, ks):
    scratch = [
        pltpu.VMEM((3, 4, 128), F32),
        pltpu.VMEM((3, 1048, 128), F32),
        pltpu.VMEM((3, 1032, 128), F32),
    ]
    later, later_total, x0, *mine = pl.pallas_call(
        later_chunks_kernel,
        grid=(3,),
        in_specs=[HBM] + [VM] * 5,
        out_specs=[VM] * 5,
        out_shape=[
            sds((3, 256, 128)),
            sds((3, 8, 128)),
            sds((1024, 256), BF),
            sds((1024, 256), BF),
            sds((16, 256), BF),
        ],
        scratch_shapes=[pltpu.VMEM((3, 1040, 256), BF)]
        + scratch
        + [pltpu.SemaphoreType.DMA((3,)), pltpu.SemaphoreType.DMA((3,))],
        compiler_params=few(16),
        name="later_chunks",
    )(*in_hbm(tokens), chunk, gain, pack, scans, ks)
    first = pl.pallas_call(
        first_chunk_kernel,
        in_specs=[VM] * 8,
        out_specs=[VM] * 5,
        out_shape=[
            sds((256, 128)),
            sds((8, 128)),
            sds((256, 128)),
            sds((8, 128)),
            sds((272, 128), BF),
        ],
        scratch_shapes=scratch,
        compiler_params=few(16),
        name="first_chunk",
    )(x0, ends_from, gain, pack, scans, ks, later, later_total)
    return later, later_total, mine, first


def combine(i, count, own, own_total, prior, prior_total, received):
    state = jnp.zeros_like(own)
    logs = jnp.zeros_like(own_total)
    zero = jnp.zeros((), F32)
    got = [(r[0:256, :].astype(F32), of_rows(r[256:272, :])) for r in received]
    for k in range(count - 1, 0, -1):
        s, l = got[k - 1]
        valid = i >= k
        state = jnp.where(valid, state * jnp.exp(l) + s, state)
        logs = jnp.where(valid, logs + l, logs)
    new_prior = state * jnp.exp(prior_total) + prior
    new_prior_total = logs + prior_total
    state = state * jnp.exp(own_total) + own
    logs = logs + own_total
    for m in range(1, count):
        s, l = got[count - m - 1]
        valid = i + m < count
        state = jnp.where(valid, state * jnp.exp(l) + s, state)
        logs = jnp.where(valid, logs + l, logs)
    return new_prior, new_prior_total, state, logs


def middle_kernel(axis, count, fresh, own, own_total, *refs):
    if fresh:
        prior, prior_total = jnp.zeros((256, 128), F32), jnp.zeros((1, 128), F32)
    else:
        prior, prior_total, refs = refs[0][...], refs[1][0:1, :], refs[2:]
    received, (np_ref, npt_ref, ns_ref, nst_ref, message) = refs[: count - 1], refs[count - 1 :]
    p, pt, s, st = combine(
        lax.axis_index(axis), count, own[...], own_total[0:1, :], prior, prior_total, received
    )
    np_ref[...] = p
    npt_ref[...] = jnp.broadcast_to(pt, (8, 128))
    ns_ref[...] = s
    nst_ref[...] = jnp.broadcast_to(st, (8, 128))
    message[0:256, :] = s.astype(BF)
    message[256:272, :] = decay_rows(st)


def middle_stage(axis, count, own, own_total, prior, received):
    return pl.pallas_call(
        lambda *refs: middle_kernel(axis, count, not prior, *refs),
        in_specs=[VM] * (2 + len(prior) + len(received)),
        out_specs=[VM] * 5,
        out_shape=[
            sds((256, 128)),
            sds((8, 128)),
            sds((256, 128)),
            sds((8, 128)),
            sds((272, 128), BF),
        ],
        compiler_params=few(4),
    )(own, own_total, *prior, *received)


def last_kernel(own, own_total, prior, prior_total, r1, r2, r3, l0, t0, later, later_total,
                o0, o1, o2, o3, sub):
    p, _, _, _ = combine(
        lax.axis_index("z"), 4, own[...], own_total[0:1, :], prior[...], prior_total[0:1, :],
        (r1, r2, r3),
    )
    sub[0] = p
    p = p * jnp.exp(t0[0:1, :]) + l0[...]
    sub[1] = p
    for j in range(2):
        p = p * jnp.exp(later_total[j, 0:1, :]) + later[j]
        sub[j + 2] = p
    h = lax.axis_index(HEAD)
    for k, out in enumerate((o0, o1, o2, o3)):
        out[...] = sub[h ^ k].astype(BF)


def last_stage(own, own_total, prior, received, l0, t0, later, later_total):
    return pl.pallas_call(
        last_kernel,
        in_specs=[VM] * 11,
        out_specs=[VM] * 4,
        out_shape=[sds((256, 128), BF)] * 4,
        scratch_shapes=[pltpu.VMEM((4, 256, 128), F32)],
        compiler_params=few(6),
        name="chain_last",
    )(own, own_total, *prior, *received, l0, t0, later, later_total)


def scan_block(
    fresh, normed, wg, wv, ws, wst, taps, bias, decay,
    lead, tail_out, maps_out, cv, act, sc, spread, scaled, run, run_log,
):
    project(normed, wv[...], cv, 0, 0)
    project(normed, ws[...], cv, 0, 4)
    normed = normed[16:272]
    tail_out[...] = silu(dot(normed, wg[...]))
    convolve(cv, act, taps, BLK)
    raw = dot(wst[...], normed, NT)
    dt = softplus(raw + bias[...])
    logs = -dt * decay[...]
    cum = cumulate(logs, upper())
    last = cum[:, BLK - 1 : BLK]
    stacked = [jnp.exp(cum), jnp.exp(last - cum) * dt]
    if fresh:
        run_log[...] = jnp.broadcast_to(last, (8, 128))
    else:
        stacked = [jnp.exp(cum + run_log[:, 0:1])] + stacked
        run_log[...] = run_log[...] + last
    first = 256 * (len(stacked) - 2)
    spread[0 : first + 512, :] = dot(parts(jnp.concatenate(stacked, 1)), expander(512), TN)
    columns = dot(parts(cum), jnp.where(
        (iota((32, 128), 0) < 24) & (iota((32, 128), 0) % 8 == iota((32, 128), 1)), 1.0, 0.0
    ).astype(BF), TN)
    rows = cum - jnp.log(dt)
    in_map = jnp.concatenate([act[4, 0:BLK].astype(BF), act[5, 0:BLK].astype(BF)], 1)
    out_map = jnp.concatenate([act[6, 0:BLK].astype(BF), act[7, 0:BLK].astype(BF)], 1)
    maps_out[...] = out_map
    sc[...] = dot(out_map, in_map, NT)
    if not fresh:
        lead[...] = spread[256:512, :] * dot(out_map, run[...].astype(BF))
    low_tri = iota((128, 128), 0) >= iota((128, 128), 1)
    lane_low = iota((BLK, 128), 1) < 64
    for p in range(4):
        cols = slice(p * 128, (p + 1) * 128)
        vals = act[p, 0:BLK]
        v0 = jnp.where(lane_low, vals, 0.0).astype(BF)
        v1 = jnp.where(lane_low, 0.0, vals).astype(BF)
        upper_w, lower_w = [], []
        for h in (2 * p, 2 * p + 1):
            c0, c1 = columns[0:128, h : h + 1], columns[128:256, h : h + 1]
            r0, r1 = rows[h : h + 1, 0:128], rows[h : h + 1, 128:256]
            upper_w.append(
                (sc[0:128, 0:128] * jnp.exp(jnp.where(low_tri, c0 - r0, -jnp.inf))).astype(BF)
            )
            lower_w.append((sc[128:256, 0:128] * jnp.exp(c1 - r0)).astype(BF))
            lower_w.append(
                (sc[128:256, 128:256] * jnp.exp(jnp.where(low_tri, c1 - r1, -jnp.inf))).astype(BF)
            )
        top = dot(
            jnp.concatenate(upper_w, 1), jnp.concatenate([v0[0:128], v1[0:128]], 0)
        )
        bottom = dot(jnp.concatenate(lower_w, 1), jnp.concatenate([v0, v1], 0))
        gate = tail_out[:, cols]
        if not fresh:
            top = top + lead[0:128, cols]
            bottom = bottom + lead[128:256, cols]
        lead[0:128, cols] = top * gate[0:128]
        lead[128:256, cols] = bottom * gate[128:256]
        tail_out[:, cols] = spread[0:256, cols] * gate
        scaled[:, cols] = (vals * spread[first + 256 : first + 512, cols]).astype(BF)
    local = dot(in_map, scaled[...], TN)
    run[...] = local if fresh else run[...] * spread[511:512, :] + local


SCAN_SCRATCH = [
    pltpu.VMEM((8, 280, 128), F32),
    pltpu.VMEM((8, BLK + 8, 128), F32),
    pltpu.VMEM((BLK, BLK), F32),
    pltpu.VMEM((768, 512), F32),
    pltpu.VMEM((256, 512), BF),
]


def fine_main_kernel(at, mine, gain, ws, *refs):
    later = at > 0
    if later:
        x0, x1, wg, wv, wst, taps, bias, decay, lead, tail_out, maps_out, run, run_log = refs[:13]
    else:
        ks, p0, p1, p2, p3, x0, x1, lead, tail_out, maps_out, run, run_log = refs[:12]
        wg, wv, wst, taps, bias, decay = refs[12:18]
    cv, act, sc, spread, scaled = refs[-5:]
    i = pl.program_id(0)

    @pl.when(i == 0)
    def _():
        if later:
            run[...] = x0[...]
            run_log[...] = x1[...]
            return
        run[...] = jnp.zeros_like(run)
        run_log[...] = jnp.zeros_like(run_log)
        for j in range(4):
            taps[4 + j] = ks[:, j * 128 : (j + 1) * 128] * 0.5
        for j, p in enumerate((p0, p1, p2, p3)):
            cols = slice(j * 128, (j + 1) * 128)
            two = slice(2 * j, 2 * j + 2)
            wg[:, cols] = p[0:256, 0:128]
            wv[:, cols] = p[0:256, 128:256]
            kv, _, bias[two, :], decay[two, :], wst[two, :] = small_rows(p)
            taps[j] = kv * 0.5

    start = pl.multiple_of((i + at) * BLK, BLK)
    rim = mine[pl.ds(pl.multiple_of(jnp.maximum(start - 16, 0), 16), 16), :].astype(F32)
    if not later:
        edge = jnp.where(lax.axis_index(HEAD) == 0, since_start(x0), x1[...].astype(F32))
        rim = jnp.where(i == 0, edge, rim)
    x = jnp.concatenate([rim, mine[pl.ds(start, BLK), :].astype(F32)], 0)
    scan_block(
        False, rms(x, gain[...]), wg, wv, ws, wst[...].astype(BF), taps, bias[:, 0:1],
        decay[:, 0:1], lead, tail_out, maps_out, cv, act, sc, spread, scaled, run, run_log,
    )


def fine_main(at, blocks, *args):
    length = blocks * BLK
    rows = [pl.BlockSpec((BLK, n), lambda i: (i, 0)) for n in (512, 512, 256)]
    weights, carried = [], [sds((256, 512)), sds((8, 128))]
    last = at + blocks == 4
    if at == 0:
        weights = [
            sds((256, 512), BF), sds((256, 512), BF), sds((8, 256)), sds((8, 4, 128)),
            sds((8, 128)), sds((8, 128)),
        ]
    return pl.pallas_call(
        lambda *refs: fine_main_kernel(at, *refs),
        grid=(blocks,),
        in_specs=[VM] * len(args),
        out_specs=rows + [VM] * (0 if last else 2 + len(weights)),
        out_shape=[sds((length, 512)), sds((length, 512)), sds((length, 256), BF)]
        + ([] if last else carried + weights),
        scratch_shapes=[pltpu.VMEM(c.shape, F32) for c in carried if last] + SCAN_SCRATCH,
        compiler_params=few(16),
    )(*args)


def fine_close_kernel(*refs):
    leads, tails, mapss, x, states, packs = (
        refs[0:3], refs[3:6], refs[6:9], refs[9], refs[10:14], refs[14:18]
    )
    merge, merged, end_rows, hidden, state, wo, norm = refs[18:]
    for j, (s, p) in enumerate(zip(states, packs)):
        cols = slice(j * 128, (j + 1) * 128)
        state[:, cols] = s[...]
        wo[cols, :] = p[256:384, :]
        norm[:, cols] = small_rows(p)[1]
    for i, (call, at) in enumerate(((0, 0), (0, 1), (1, 0), (2, 0))):
        part = slice(at * BLK, (at + 1) * BLK)
        rows = slice(i * BLK, (i + 1) * BLK)
        gated = leads[call][part] + tails[call][part] * dot(mapss[call][part], state[...])
        factor = lax.rsqrt(jnp.sum(gated * gated, axis=1, keepdims=True) / 512.0 + EPSILON)
        total = dot((gated * factor * norm[...]).astype(BF), wo[...])
        out = x[rows].astype(F32) + total
        hidden[0, rows, :] = rounded(out[:, 0:128])
        hidden[1, rows, :] = rounded(out[:, 128:256])
    total = None
    for odd in range(2):
        rows = [
            hidden[half, pl.ds(odd, 512, stride=2), :].reshape(8, 2, 32, 128) for half in range(2)
        ]
        for line in range(2):
            tile = [r[:, line].reshape(256, 128).astype(BF) for r in rows]
            at = (2 * line + odd) * 256
            piece = dot(jnp.concatenate(tile, 1), merge[at : at + 256, :])
            total = piece if total is None else total + piece
    result = total.astype(BF)
    merged[...] = result
    end_rows[...] = result[240:256]


def fine_close(leads, tails, maps, x, states, packs, merge):
    return pl.pallas_call(
        fine_close_kernel,
        in_specs=[VM] * 19,
        out_specs=[VM] * 2,
        scratch_shapes=[
            pltpu.VMEM((2, 1024, 128), F32),
            pltpu.VMEM((256, 512), BF),
            pltpu.VMEM((512, 256), BF),
            pltpu.VMEM((1, 512), F32),
        ],
        out_shape=[sds((256, 1024), BF), sds((16, 1024), BF)],
        compiler_params=few(16),
        name="fine_close",
    )(*leads, *tails, *maps, x, *states, *packs, merge)


def in_order(first, a, a_log, b, b_log):
    lead_log = jnp.where(first, b_log, a_log)
    row = jnp.exp(spread_row(lead_log))
    return jnp.where(first, a, b) * row + jnp.where(first, b, a), a_log + b_log


def chip_start(rows):
    first = lax.axis_index(("z", "u", "x", "y")) == 0
    return jnp.where(first, 0.0, rows[...].astype(F32))


def coarse_main_kernel(kind, pieces, gain, wg, wv, ws, wst, taps, both, *refs):
    qs, refs = refs[:pieces], refs[pieces:]
    xs, sems, rims, cv, act, sc, spread, scaled = refs[-8:]
    y, c = lax.axis_index("y"), lax.axis_index("c")
    h = 2 * y + c
    if kind == "near":
        ra, rb, lead, tail_out, maps_out, share, run, run_log = refs[:-8]
    elif kind == "far_1":
        re, lead, tail_out, maps_out, share, run, run_log, ends = refs[:-8]
    else:
        (
            ends_1, rd, near_run, near_log, run_1, run_log_1,
            lead, tail_out, maps_out, share, run, run_log, far_run, far_log, message,
        ) = refs[:-8]
    i = pl.program_id(0)

    @pl.when(i == 0)
    def _():
        if kind == "near":
            copies = run_copies(((qs[0], xs.at[c]), (qs[1], xs.at[1 - c])), sems)
            rim = jnp.where(c == 0, chip_start(ra), chip_start(rb))
        else:
            copies = run_copies(((qs[0], xs.at[0]),), sems)
            rim = re[...].astype(F32) if kind == "far_1" else rd[...].astype(F32)
            if kind == "far_2":
                rim = jnp.where(c == 0, ends_1[...].astype(F32), rim)
        rims[...] = rim
        if kind == "near":
            run[...] = jnp.zeros_like(run)
            run_log[...] = jnp.zeros_like(run_log)
        for copy in copies:
            copy.wait()
        if kind == "far_1":
            ends[...] = xs[0, 240:256, :]

    share[...] = xs[i, :, pl.ds(pl.multiple_of(h * 256, 256), 256)]
    rim = rims[...]
    if kind == "near":
        rim = jnp.where(i == 0, rim, xs[0, 240:256, :].astype(F32))
    x = jnp.concatenate([rim, xs[i].astype(F32)], 0)
    scan_block(
        kind != "near", rms(x, gain[...]), wg, wv, ws, wst[...], taps, both[0:8, 0:1],
        both[8:16, 0:1], lead, tail_out, maps_out, cv, act, sc, spread, scaled, run, run_log,
    )

    if kind == "far_2":
        log_1, log_2, log_n = run_log_1[:, 0:1], run_log[:, 0:1], near_log[:, 0:1]
        far, log_f = in_order(c == 0, run_1[...], log_1, run[...], log_2)
        far_run[...] = far
        far_log[...] = jnp.broadcast_to(log_f, (8, 128))
        total, log = in_order(y == 0, near_run[...], log_n, far, log_f)
        extra = decay_rows(spread_row(log))[0:8]
        for n in range(16):
            for half in range(2):
                cols = slice(half * 256, (half + 1) * 256)
                message[2 * n + half, 0:16, :] = total[n * 16 : (n + 1) * 16, cols].astype(BF)
                message[2 * n + half, 16:24, :] = extra[:, cols]


def spread_row(column):
    return jnp.sum(
        jnp.where(head_sel(512), jnp.broadcast_to(column, (8, 512)), 0.0), axis=0, keepdims=True
    )


ANY = pl.BlockSpec(memory_space=pl.ANY)


def coarse_main(kind, pieces, weights, params, extra):
    taps, both, gain, wst, _ = params
    blocks = len(pieces)
    length = blocks * BLK
    rows = [pl.BlockSpec((BLK, n), lambda i: (i, 0)) for n in (512, 512, 256, 256)]
    last = []
    if kind == "far_1":
        last = [sds((16, 1024), BF)]
    elif kind == "far_2":
        last = [sds((256, 512)), sds((8, 128)), sds((32, 24, 256), BF)]
    return pl.pallas_call(
        lambda *refs: coarse_main_kernel(kind, blocks, *refs),
        grid=(blocks,),
        in_specs=[VM] * 7 + [ANY] * blocks + [VM] * len(extra),
        out_specs=rows + [VM] * (2 + len(last)),
        out_shape=[
            sds((length, 512)),
            sds((length, 512)),
            sds((length, 256), BF),
            sds((length, 256), BF),
            sds((256, 512)),
            sds((8, 128)),
        ]
        + last,
        scratch_shapes=[
            pltpu.VMEM((blocks, 256, 1024), BF),
            pltpu.SemaphoreType.DMA((blocks,)),
            pltpu.VMEM((16, 1024), F32),
        ]
        + SCAN_SCRATCH,
        compiler_params=few(16),
    )(gain, *weights, wst, taps, both, *pieces, *extra)


def own_rim_kernel(came, beside, out):
    out[...] = jnp.where(
        lax.axis_index("c") == 0, chip_start(came), beside[240:256, :].astype(F32)
    ).astype(BF)


def own_rim(came, beside):
    return pl.pallas_call(
        own_rim_kernel,
        in_specs=[VM] * 2,
        out_specs=VM,
        out_shape=sds((16, 1024), BF),
        compiler_params=few(4),
        name="own_rim",
    )(came, beside)


def prefix_kernel(got, out):
    state = jnp.zeros((16, 256), F32)
    for d in range(32):
        out[d] = state.astype(BF)
        state = state * jnp.exp(of_rows(got[d, 16:24, :])) + got[d, 0:16, :].astype(F32)


def prefix(got):
    return pl.pallas_call(
        prefix_kernel,
        in_specs=[VM],
        out_specs=VM,
        out_shape=sds((32, 16, 256), BF),
        compiler_params=few(4),
        name="prefix",
    )(got)


def coarse_close_kernel(near, *refs):
    if near:
        lead, tail, maps, got, far_run, far_log, norm, wo, *refs = refs
    else:
        leads, tails, mapss = refs[0:2], refs[2:4], refs[4:6]
        got, near_run, near_log, run_1, log_1, run_2, log_2, norm, wo, *refs = refs[6:]
    gn, ks, ss, square_sums, states, sums = refs
    y, c = lax.axis_index("y"), lax.axis_index("c")
    h = 2 * y + c
    came = jnp.concatenate(
        [jnp.concatenate([got[2 * n], got[2 * n + 1]], 1) for n in range(16)], 0
    ).astype(F32)

    def after(state, cond, run, log):
        row = jnp.exp(spread_row(log[:, 0:1]))
        return jnp.where(cond, state * row + run[...], state)

    if near:
        states[0] = after(came, y == 1, far_run, far_log).astype(BF)
    else:
        came = after(came, y == 0, near_run, near_log)
        states[0] = after(came, c == 1, run_2, log_2).astype(BF)
        states[1] = after(came, c == 0, run_1, log_1).astype(BF)
    ones = jnp.ones((8, 512), BF)
    for i in range(2):
        if near:
            rows = slice(i * BLK, (i + 1) * BLK)
            gated = lead[rows] + tail[rows] * dot(maps[rows], states[0])
            place = i
        else:
            gated = leads[i][...] + tails[i][...] * dot(mapss[i][...], states[i])
            place = jnp.bitwise_xor(c, i)
        sq = gated * gated
        hi = sq.astype(BF)
        low = (sq - hi.astype(F32)).astype(BF)
        sums[place] = dot(ones, hi, NT) + dot(ones, low, NT)
        scaled = (gated * norm[...]).astype(BF)
        at = pl.ds(pl.multiple_of(place * BLK, BLK), BLK)
        gn[at, :] = scaled
        for k, out in ((2, ks), (3, ss)):
            col = pl.multiple_of((h ^ k) * 256, 256)
            out[at, :] = dot(scaled, wo[:, pl.ds(col, 256)]).astype(BF)
    square_sums[...] = jnp.concatenate([sums[0], sums[1]], 1)
    ss[512:528, :] = sum_rows(sums[0, 0:1], sums[1, 0:1])


def coarse_close(near, *args):
    return pl.pallas_call(
        lambda *refs: coarse_close_kernel(near, *refs),
        in_specs=[VM] * len(args),
        out_specs=[VM] * 4,
        out_shape=[
            sds((512, 512), BF), sds((512, 256), BF), sds((528, 256), BF), sds((8, 512)),
        ],
        scratch_shapes=[pltpu.VMEM((2, 256, 512), BF), pltpu.VMEM((2, 8, 256), F32)],
        compiler_params=few(12),
        name="coarse_close_near" if near else "coarse_close_far",
    )(*args)


def close_rest_kernel(near, far, wo, kk, sk):
    h = lax.axis_index(HEAD)
    for k, out in enumerate((kk, sk)):
        col = pl.multiple_of((h ^ k) * 256, 256)
        for j, ref in enumerate((near, far)):
            out[j * 512 : (j + 1) * 512, :] = dot(ref[...], wo[:, pl.ds(col, 256)]).astype(BF)


def close_rest(near, far, wo):
    return pl.pallas_call(
        close_rest_kernel,
        in_specs=[VM] * 3,
        out_specs=[VM] * 2,
        out_shape=[sds((1024, 256), BF)] * 2,
        compiler_params=few(8),
        name="close_rest",
    )(near, far, wo)


def sum_rows(a, b):
    return jnp.concatenate(three(a) + three(b) + [jnp.zeros((10, 256), F32)], 0).astype(BF)


def rows_sum(ref):
    rows = ref[512:528, :].astype(F32)
    return jnp.concatenate([of_rows(rows[0:3]), of_rows(rows[3:6])], 1)


def relay_kernel(ks, square_sums, came, out, sums):
    out[0:512, :] = (ks[...].astype(F32) + came[0:512, :].astype(F32)).astype(BF)
    total = square_sums[0:1, :] + rows_sum(came)
    out[512:528, :] = sum_rows(total[:, 0:256], total[:, 256:512])
    sums[...] = jnp.broadcast_to(total, (8, 512))


def relay(ks, square_sums, came):
    return pl.pallas_call(
        relay_kernel,
        in_specs=[VM] * 3,
        out_specs=[VM] * 2,
        out_shape=[sds((528, 256), BF), sds((8, 512))],
        compiler_params=few(4),
    )(ks, square_sums, came)


def final_kernel(side, *refs):
    shares, (kk, sk, sums, far), refs = refs[: side + 1], refs[side + 1 : side + 5], refs[side + 5 :]
    out, rows_v, sem = refs[-3:]
    y, c = lax.axis_index("y"), lax.axis_index("c")
    pick = jnp.where(iota((32, 256), 0) % 8 == 0, 1.0, 0.0).astype(BF)
    factor = lax.rsqrt((sums[...] + rows_sum(far)) / 2048.0 + EPSILON)
    for b in range(2):
        rows = slice(b * BLK, (b + 1) * BLK)
        here = slice(side * 512 + b * BLK, side * 512 + (b + 1) * BLK)
        spread = dot(parts(factor[:, rows]), pick, TN)
        total = kk[here].astype(F32) + sk[here].astype(F32) + far[rows].astype(F32)
        if side == 0:
            own = shares[0][rows].astype(F32)
        else:
            own = jnp.where(c == b, shares[0][...].astype(F32), shares[1][...].astype(F32))
        rows_v[rows, :] = (own + total * spread).astype(BF)
    half = y if side == 0 else 1 - y
    at = pl.multiple_of(half * 512, 512)
    copy = pltpu.make_async_copy(rows_v, out.at[pl.ds(at, 512)], sem)
    copy.start()
    copy.wait()


def final(side, *args):
    into = len(args) - (side + 5)
    return pl.pallas_call(
        lambda *refs: final_kernel(side, *refs),
        in_specs=[VM] * (side + 5) + [HBM] * into,
        out_specs=HBM,
        out_shape=pltpu.HBM((1024, 256), BF),
        input_output_aliases={side + 5: 0} if into else {},
        scratch_shapes=[pltpu.VMEM((512, 256), BF), pltpu.SemaphoreType.DMA],
        compiler_params=few(6),
    )(*args)


def passed(x, axes, pairs):
    return lax.ppermute(x, axes, pairs)


def swapped(x, mask):
    return passed(x, HEAD, [(j, j ^ mask) for j in range(4)])


def round_of(x, axis):
    got = []
    for k in (1, 2, 3):
        got.append(passed(x, axis, [(j, (j + k) % 4) for j in range(4)]))
    return got


def shards(
    tokens, fine_gain, fine_gate, fine_value, fine_scans, fine_steps, fine_kernel, fine_taps,
    fine_bias, fine_decay, fine_norm, fine_output, merge_weight, coarse_gain, coarse_gate,
    coarse_value, coarse_scans, coarse_steps, coarse_kernel, coarse_taps, coarse_bias,
    coarse_decay, coarse_norm, coarse_output,
):
    pack, ends, chunk, gain, scans, ks = packed(
        fine_bias[None], fine_decay[None], fine_gate, fine_value, fine_output, fine_steps.T,
        fine_kernel, fine_norm[None], tokens, fine_gain[None], fine_scans, fine_taps,
    )
    rim = passed(ends, SEQ, [(i, (i + 1) % 32) for i in range(32)])
    packs = [pack] + [swapped(pack, m) for m in (1, 2, 3)]
    later, later_total, (mine, mine_rim), (l0, t0, own, own_total, message) = fine_states(
        tokens, chunk, rim, gain, pack, scans, ks
    )
    got = round_of(message, "x")
    first = fine_main(0, 2, mine, gain, scans, ks, *packs, rim, mine_rim)
    *prior, own, own_total, message = middle_stage("x", 4, own, own_total, (), got)
    got = [passed(message, "u", [(0, 1), (1, 0)])]
    params = coarse_params(
        coarse_bias[None], coarse_decay[None], coarse_kernel, coarse_taps, coarse_gain[None],
        coarse_steps.T, coarse_norm[None],
    )
    second = fine_main(2, 1, mine, gain, scans, *first[3:])
    *prior, own, own_total, message = middle_stage("u", 2, own, own_total, prior, got)
    got = round_of(message, "z")
    third = fine_main(3, 1, mine, gain, scans, *second[3:], *first[5:])
    subs = last_stage(own, own_total, prior, got, l0, t0, later, later_total)
    states = [subs[0]] + [swapped(subs[m], m) for m in (1, 2, 3)]
    merged, end_rows = fine_close(
        *([call[j] for call in (first, second, third)] for j in range(3)), mine, states, packs,
        merge_weight,
    )

    rim_a = passed(end_rows, ALL, [(q, (q - 1 + 2 * (q % 2)) % 128) for q in range(128)])
    across = swapped(merged, 2)
    beside = swapped(merged, 1)
    rim_b = swapped(rim_a, 1)
    rim_y = swapped(own_rim(rim_a, beside), 2)
    rim_yc = swapped(rim_y, 1)
    both = swapped(across, 1)
    weights = (coarse_gate, coarse_value, coarse_scans)
    lead, tail, maps, share, run, run_log = coarse_main(
        "near", (merged, beside), weights, params, (rim_a, rim_b)
    )
    lead_1, tail_1, maps_1, share_1, run_1, run_log_1, ends_1 = coarse_main(
        "far_1", (across,), weights, params, (rim_y,)
    )
    lead_2, tail_2, maps_2, share_2, run_2, run_log_2, run_f, run_log_f, message = coarse_main(
        "far_2", (both,), weights, params,
        (ends_1, rim_yc, run, run_log, run_1, run_log_1),
    )
    got = lax.all_to_all(message, SEQ, split_axis=0, concat_axis=0, tiled=True)
    got = lax.all_to_all(prefix(got), SEQ, split_axis=0, concat_axis=0, tiled=True)
    norm = params[4]
    gn, ks, ss, sums = coarse_close(
        True, lead, tail, maps, got, run_f, run_log_f, norm, coarse_output
    )
    gn_f, ks_f, ss_f, sums_f = coarse_close(
        False, lead_1, lead_2, tail_1, tail_2, maps_1, maps_2, got, run, run_log,
        run_1, run_log_1, run_2, run_log_2, norm, coarse_output,
    )
    went, sums = relay(ks, sums, swapped(ss, 1))
    went = swapped(went, 2)
    went_f, sums_f = relay(ks_f, sums_f, swapped(ss_f, 1))
    went_f = swapped(went_f, 2)
    kk, sk = close_rest(gn, gn_f, coarse_output)
    sk = swapped(sk, 1)
    out = final(1, share_1, share_2, kk, sk, sums_f, went)
    return final(0, share, kk, sk, sums, went_f, out)


def solution(mesh):
    finer = Mesh(mesh.devices.reshape(4, 2, 4, 2, 2), ALL)
    cols = P(None, HEAD)
    return jax.shard_map(
        shards,
        mesh=finer,
        in_specs=(
            P(SEQ, None), P(), cols, cols, P(), cols, cols, P(), P(HEAD), P(HEAD), P(HEAD),
            P(HEAD, None), P(), P(), cols, cols, P(), cols, cols, P(), P(HEAD), P(HEAD), P(HEAD),
            P(HEAD, None),
        ),
        out_specs=P(SEQ, HEAD),
        check_vma=False,
    )
```
